256 devices in a mesh: lead: 16 (over z, core), grp: 16 (over x, y).
Axes of the slice: x: 4, y: 4, z: 8, core: 2. Of those that a mesh axis runs over, the one named last changes fastest.
Arguments:
- matrix_tiles: bfloat16 [512, 384, 384], P(('lead', 'grp')), may hold values from -0.0546875 to 0.0546875
- tile_slot: int32 [16, 32], P('lead'), may hold values from 0 to 31, each once within a row
- tile_cols: int32 [64, 8], P('lead'), may hold values from 0 to 7, as said below
- send_rows: int32 [16, 2, 2], replicated, may hold values from 0 to 3, as said below
- residual: float32 [24576, 128], P(('lead', 'grp')), may hold values from -6 to 6
- diag_inv: float32 [24576], P(('lead', 'grp')), may hold values from 0.25 to 1
Outputs:
- correction: float32 [24576, 128], P(('lead', 'grp'))
The draws below stay inside these ranges and needn't reach their ends.
Inputs may be any that keep to these rules, and one draw needn't show every extreme that they name: `tile_cols`: entry 0 of every row is that row's own block row within its leader, r for row l * 4 + r; indices below 4 are the leader's own block rows, the next 2 are the rows received from leader l - 1, the last 2 those received from leader l + 1 (cyclic). `send_rows`: the 2 entries of each list are distinct block rows of the sending leader.
All inputs are finite; a program needn't handle non-finite values.
Results may differ from the reference program's by a relative error of at most 0.0013.
Values may be sent and summed in bfloat16 or wider, within the bound.
No kernel may reach another device: no remote copies, remote signals or barrier semaphores. Data moves between devices by JAX's collectives and lax.ppermute only.
A program may use at most 64 MiB of HBM per device.

```python
import math
import jax
import jax.numpy as jnp
from jax import lax

TILE = 384
TILES_ROW = 8
DEGREE = 2
NRHS = 128
GROUP_TILES = 32
BR_LEAD = 4
HALO = 2
EXT = 8
NDOF = 24576
NTILES = 512
N_LEAD = 16


def draw_tile_cols(key, part):
    row_total = N_LEAD * BR_LEAD
    picked = jax.random.randint(key, (row_total, TILES_ROW), 0, EXT, dtype=jnp.int32)
    local_row = jnp.arange(row_total, dtype=jnp.int32) % BR_LEAD
    slot_index = jnp.arange(TILES_ROW, dtype=jnp.int32)[None, :]
    picked = jnp.where(slot_index == 0, local_row[:, None], picked)
    corner_slot = (local_row[:, None] == 0) & (slot_index == TILES_ROW - 1)
    return jnp.where(corner_slot, EXT - 1, picked).astype(jnp.int32)


def draw_send_rows(key, part):
    key_list = jax.random.split(key, N_LEAD * 2)

    def one_order(one_key):
        return jax.random.permutation(one_key, BR_LEAD)
    orders = jax.vmap(one_order)(key_list)
    chosen = orders[:, :HALO].reshape(N_LEAD, 2, HALO).astype(jnp.int32)
    falling = (BR_LEAD - 1 - jnp.arange(HALO, dtype=jnp.int32)).astype(jnp.int32)
    rising = jnp.arange(HALO, dtype=jnp.int32)
    chosen = chosen.at[0, 0].set(falling).at[0, 1].set(rising)
    return chosen.astype(jnp.int32)


def shard_levels(rng, extent, shards, low, high):
    def one(position, blocks):
        heights = jax.random.uniform(jax.random.fold_in(jax.random.fold_in(rng, 6), position), (blocks,), jnp.float32, low / len(shards), high / len(shards))
        return jnp.repeat(jnp.exp(heights), extent[position] // blocks).reshape((-1,) + (1,) * (len(extent) - position - 1))

    loudness = one(*shards[0])
    for cut in shards[1:]:
        loudness = loudness * one(*cut)
    return loudness


def bell_draw(key, dims, spread, most, cuts=(), kind=jnp.bfloat16):
    result = jax.random.normal(key, dims, jnp.float32) * spread
    if len(cuts) > 0:
        result = shard_levels(key, dims, cuts, -0.22, 0.18) * result
    return jnp.clip(result, min=-most, max=most).astype(kind)


def setup_inputs(seed: int = 0) -> dict:
    arg_keys = jax.random.split(jax.random.key(seed), 7)
    matrix_tiles = bell_draw(arg_keys[0], (NTILES, TILE, TILE), (4 * TILE * TILES_ROW) ** -0.5, 0.0546875, ((0, 256),))
    tile_slot = jax.vmap(lambda own: jax.random.permutation(own, GROUP_TILES))(jax.random.split(arg_keys[1], N_LEAD)).reshape((N_LEAD, GROUP_TILES)).astype(jnp.int32)
    tile_cols = draw_tile_cols(jax.random.fold_in(arg_keys[6], 71), 0)
    send_rows = draw_send_rows(jax.random.fold_in(arg_keys[6], 71), 0)
    residual = bell_draw(arg_keys[4], (NDOF, NRHS), 1.0, 6.0, ((0, 256),), jnp.float32)
    diag_inv = jnp.clip(jnp.exp(math.log(1.0) - 1.3862944 * jax.random.uniform(arg_keys[5], (NDOF,), jnp.float32) ** shard_levels(arg_keys[5], (NDOF,), ((0, 256),), -0.2, 0.2)), 0.25, 1.0)
    return dict(matrix_tiles=matrix_tiles, tile_slot=tile_slot, tile_cols=tile_cols, send_rows=send_rows, residual=residual, diag_inv=diag_inv)


lower_bound = 0.5
upper_bound = 1.5


def coupling(vector, slot_tiles, tile_cols, send_rows):
    blocks = vector.astype(jnp.bfloat16).reshape(N_LEAD, BR_LEAD, TILE, NRHS)
    leaders = jnp.arange(N_LEAD, dtype=jnp.int32)
    lower_peer = (leaders - 1) % N_LEAD
    upper_peer = (leaders + 1) % N_LEAD
    from_lower = blocks[lower_peer[:, None], send_rows[lower_peer, 0]]
    from_upper = blocks[upper_peer[:, None], send_rows[upper_peer, 1]]
    extended = jnp.concatenate([blocks, from_lower, from_upper], axis=1)
    columns = tile_cols.reshape(N_LEAD, BR_LEAD, TILES_ROW)

    def one_leader(items):
        ext_rows, leader_tiles, leader_cols = items
        operand = ext_rows[leader_cols].astype(jnp.float32)
        return jnp.einsum("rkij,rkjn->rin", leader_tiles.astype(jnp.float32), operand,
                          precision=lax.Precision.HIGHEST)

    product = lax.map(one_leader, (extended, slot_tiles, columns))
    return product.reshape(NDOF, NRHS)


def one_sweep(start_residual, inverse, apply_operator):
    center_value = (upper_bound + lower_bound) / 2.0
    half_width = (upper_bound - lower_bound) / 2.0
    ratio_value = center_value / half_width
    update = inverse[:, None] * start_residual / center_value
    approx = update
    rho_now = 1.0 / ratio_value
    for repeat in range(DEGREE - 1):
        rho_next = 1.0 / (2.0 * ratio_value - rho_now)
        remaining = start_residual - apply_operator(approx)
        update = rho_next * rho_now * update + (2.0 * rho_next / half_width) * inverse[:, None] * remaining
        approx = approx + update
        rho_now = rho_next
    return approx


def reference(matrix_tiles, tile_slot, tile_cols, send_rows, residual, diag_inv):
    grouped = matrix_tiles.reshape(N_LEAD, GROUP_TILES, TILE, TILE)

    def place(items):
        leader_tiles, slots = items
        return jnp.zeros_like(leader_tiles).at[slots.astype(jnp.int32)].set(leader_tiles)

    slot_tiles = lax.map(place, (grouped, tile_slot)).reshape(N_LEAD, BR_LEAD, TILES_ROW, TILE, TILE)

    def apply_operator(approx):
        return approx / diag_inv[:, None] + coupling(approx, slot_tiles, tile_cols, send_rows)

    first_pass = one_sweep(residual, diag_inv, apply_operator)
    remaining = residual - apply_operator(first_pass)
    second_pass = one_sweep(remaining, diag_inv, apply_operator)
    return first_pass + second_pass
```

```python
import jax
import jax.numpy as jnp
from jax import lax
from jax.experimental import pallas as pl
from jax.experimental.pallas import tpu as pltpu
from jax.sharding import PartitionSpec as P

TILE = 384
NRHS = 128
SIDE = 4
GROUP = 16
SHARE = 96
SLAB = 24
TILES = 32
PIECE = 96
F32 = jnp.float32
BF16 = jnp.bfloat16
GAIN = 8.0 / 7.0

X_GROUPS = [[SIDE * x + y for x in range(SIDE)] for y in range(SIDE)]
VMEM = pl.BlockSpec(memory_space=pltpu.VMEM)
SMEM = pl.BlockSpec(memory_space=pltpu.SMEM)


def column_of(row, first, count):
    line = lax.broadcasted_iota(jnp.int32, (count, 128), 0) + first
    lane = lax.broadcasted_iota(jnp.int32, (count, 128), 1)
    return jnp.sum(jnp.where(line == lane, jnp.broadcast_to(row, (count, 128)), 0.0), axis=1, keepdims=True)


def pack_kernel(tiles_ref, residual_ref, diag_ref, out_ref):
    diag_row = jnp.concatenate([diag_ref[...], jnp.zeros((1, 128 - SHARE), F32)], axis=1)
    scaled = residual_ref[...] * column_of(diag_row, 0, SHARE)
    high = scaled.astype(BF16)
    low = scaled - high.astype(F32)
    high = high.astype(F32)
    wide = jnp.concatenate([high[32 * k:32 * k + 32] for k in range(3)], axis=1).astype(BF16)
    d_high = diag_row.astype(BF16).astype(F32)
    d_mid = (diag_row - d_high).astype(BF16).astype(F32)
    d_low = diag_row - d_high - d_mid
    d_rows = jnp.broadcast_to(jnp.concatenate([d_high, d_mid, d_low], axis=1), (8, 384))
    tiles = [tiles_ref[j].astype(F32) for j in range(2)]
    for x in range(SIDE):
        mine = low[SLAB * x:SLAB * (x + 1)]
        low_rows = jnp.concatenate([mine[8 * k:8 * k + 8] for k in range(3)], axis=1)
        tail = jnp.concatenate([low_rows, d_rows], axis=0).astype(BF16)
        for q in range(SIDE):
            at = SHARE * q + SLAB * x
            slab = jnp.concatenate([tile[at:at + SLAB] for tile in tiles], axis=0).astype(BF16)
            out_ref[SIDE * x + q, 0:48] = slab
            out_ref[SIDE * x + q, 48:80] = wide
            out_ref[SIDE * x + q, 80:96] = tail


def send_blocks(rows_ref, lead, own_ref, up_ref, down_ref):
    for h in range(2):
        up_ref[h] = own_ref[rows_ref[lead, 0, h]]
        down_ref[h] = own_ref[rows_ref[lead, 1, h]]


def first_pick_kernel(place_ref, rows_ref, got_ref, own_ref, up_ref, down_ref):
    for source in range(GROUP):
        for k in range(3):
            at = SHARE * (source % SIDE) + 32 * k
            own_ref[source // SIDE, at:at + 32] = got_ref[source, 48:80, 128 * k:128 * k + 128]
    send_blocks(rows_ref, place_ref[0], own_ref, up_ref, down_ref)


def pick_kernel(place_ref, rows_ref, got_ref, own_ref, up_ref, down_ref):
    for q in range(SIDE):
        parts = [got_ref[SIDE * x + q].astype(F32) for x in range(SIDE)]
        for r in range(SIDE):
            block = jnp.concatenate([p[SLAB * r:SLAB * (r + 1)] for p in parts], axis=0)
            own_ref[r, SHARE * q:SHARE * (q + 1)] = block.astype(BF16)
    send_blocks(rows_ref, place_ref[0], own_ref, up_ref, down_ref)


def coupled(slot_ref, cols_ref, got_ref, own_ref, low_ref, high_ref, product_ref, total_ref):
    slabs = jnp.concatenate([got_ref[m, 0:48] for m in range(GROUP)], axis=0)
    blocks = [own_ref[k] for k in range(4)] + [low_ref[k] for k in range(2)] + [high_ref[k] for k in range(2)]
    for pair in range(4):
        wide = jnp.concatenate(blocks[2 * pair:2 * pair + 2], axis=1)
        product = jnp.dot(slabs, wide, preferred_element_type=F32)
        product_ref[2 * pair] = product[:, :128]
        product_ref[2 * pair + 1] = product[:, 128:]
    total_ref[...] = jnp.zeros_like(total_ref)
    for t in range(TILES):
        slot = slot_ref[0, t]
        row = lax.shift_right_logical(slot, 3)
        col = cols_ref[row, lax.bitwise_and(slot, 7)]
        total_ref[row] += product_ref[col, SLAB * t:SLAB * (t + 1)]
    return total_ref[...].reshape(SHARE, NRHS)


def spread(value, out_ref):
    value = value.astype(BF16)
    for m in range(GROUP):
        out_ref[m] = value


def first_kernel(place_ref, slot_ref, cols_ref, got_ref, own_ref, low_ref, high_ref,
                 wide_ref, first_ref, start_ref, scale_ref, product_ref, total_ref, line_ref):
    x, q = place_ref[1], place_ref[2]
    for r in range(SIDE):
        source = SIDE * r + q
        tail = got_ref[source, 80:96].astype(F32)
        top = got_ref[source, 48:80].astype(F32)
        line_ref[...] = jnp.concatenate([top[:, 128 * k:128 * k + 128] for k in range(3)], axis=0)
        high = line_ref[pl.ds(pl.multiple_of(x * SLAB, 8), SLAB), :]
        low = jnp.concatenate([tail[0:8, 128 * k:128 * k + 128] for k in range(3)], axis=0)
        row = tail[8:9, 0:128] + (tail[8:9, 128:256] + tail[8:9, 256:384])
        start_ref[SLAB * r:SLAB * (r + 1)] = high + low
        scale_ref[SLAB * r:SLAB * (r + 1)] = jnp.broadcast_to(column_of(row, x * SLAB, SLAB), (SLAB, NRHS))
    total = coupled(slot_ref, cols_ref, got_ref, own_ref, low_ref, high_ref, product_ref, total_ref)
    first = GAIN * (start_ref[...] - scale_ref[...] * total)
    first_ref[...] = first
    spread(first, wide_ref)


def second_kernel(slot_ref, cols_ref, got_ref, own_ref, low_ref, high_ref, first_ref, start_ref, scale_ref,
                  wide_ref, second_ref, product_ref, total_ref):
    total = coupled(slot_ref, cols_ref, got_ref, own_ref, low_ref, high_ref, product_ref, total_ref)
    second = start_ref[...] - first_ref[...] - scale_ref[...] * total
    second_ref[...] = second
    spread(second, wide_ref)


def last_kernel(slot_ref, cols_ref, got_ref, own_ref, low_ref, high_ref, first_ref, second_ref, scale_ref,
                out_ref, product_ref, total_ref):
    total = coupled(slot_ref, cols_ref, got_ref, own_ref, low_ref, high_ref, product_ref, total_ref)
    out_ref[...] = first_ref[...] + GAIN * (second_ref[...] - scale_ref[...] * total)


def arr(shape, dtype):
    return jax.ShapeDtypeStruct(shape, dtype)


def call(kernel, name, specs, outs, scratch=()):
    return pl.pallas_call(kernel, name=name, in_specs=specs, out_specs=[VMEM] * len(outs),
                          out_shape=outs, scratch_shapes=list(scratch))


WORK = (pltpu.VMEM((8, TILES * SLAB, NRHS), F32), pltpu.VMEM((SIDE, SLAB, NRHS), F32))
PICKED = [arr((SIDE, TILE, NRHS), BF16), arr((2, TILE, NRHS), BF16), arr((2, TILE, NRHS), BF16)]
ROWS = arr((SHARE, NRHS), F32)
WIDE = arr((GROUP, SHARE, NRHS), BF16)


def local(matrix_tiles, tile_slot, tile_cols, send_rows, residual, diag_inv):
    leads = lax.axis_size("lead")
    lead, member = lax.axis_index("lead"), lax.axis_index("grp")
    place = jnp.stack([lead, member // SIDE, member % SIDE]).astype(jnp.int32)
    ahead = [(i, (i + 1) % leads) for i in range(leads)]
    behind = [(i, (i - 1) % leads) for i in range(leads)]

    def halo(up, down):
        return lax.ppermute(up, "lead", ahead), lax.ppermute(down, "lead", behind)

    def gather(wide):
        return lax.all_to_all(wide, "grp", 0, 0)

    packed, = call(pack_kernel, "pack", [VMEM] * 3, [arr((GROUP, PIECE, TILE), BF16)])(
        matrix_tiles, residual, diag_inv.reshape(1, SHARE))
    got = gather(packed)
    pick_specs = [SMEM, SMEM, VMEM]
    own, up, down = call(first_pick_kernel, "pick0", pick_specs, PICKED)(place, send_rows, got)
    low, high = halo(up, down)
    wide, first, start, scale = call(
        first_kernel, "apply0", [SMEM] * 3 + [VMEM] * 4, [WIDE, ROWS, ROWS, ROWS],
        WORK + (pltpu.VMEM((SHARE, NRHS), F32),))(place, tile_slot, tile_cols, got, own, low, high)
    own, up, down = call(pick_kernel, "pick1", pick_specs, PICKED)(place, send_rows, gather(wide))
    low, high = halo(up, down)
    wide, second = call(second_kernel, "apply1", [SMEM] * 2 + [VMEM] * 7, [WIDE, ROWS], WORK)(
        tile_slot, tile_cols, got, own, low, high, first, start, scale)
    own, up, down = call(pick_kernel, "pick2", pick_specs, PICKED)(place, send_rows, gather(wide))
    low, high = halo(up, down)
    result, = call(last_kernel, "apply2", [SMEM] * 2 + [VMEM] * 7, [ROWS], WORK)(
        tile_slot, tile_cols, got, own, low, high, first, second, scale)
    home = lax.all_to_all(result.reshape(SIDE, SLAB, NRHS), "grp", 0, 0, axis_index_groups=X_GROUPS)
    return home.reshape(SHARE, NRHS)


def solution(mesh):
    in_specs = (
        P(("lead", "grp"), None, None),
        P("lead", None),
        P("lead", None),
        P(),
        P(("lead", "grp"), None),
        P(("lead", "grp")),
    )
    out_specs = P(("lead", "grp"), None)
    return jax.shard_map(local, mesh=mesh, in_specs=in_specs, out_specs=out_specs, check_vma=False)
```

```python
import jax
import jax.numpy as jnp
from jax import lax
from jax.experimental import pallas as pl
from jax.experimental.pallas import tpu as pltpu
from jax.sharding import PartitionSpec as P

TILE = 384
NRHS = 128
SIDE = 4
GROUP = 16
SHARE = 96
SLAB = 24
TILES = 32
F32 = jnp.float32
BF16 = jnp.bfloat16
GAIN = 8.0 / 7.0

X_GROUPS = [[SIDE * x + y for x in range(SIDE)] for y in range(SIDE)]
VMEM = pl.BlockSpec(memory_space=pltpu.VMEM)
SMEM = pl.BlockSpec(memory_space=pltpu.SMEM)


def column_of(row, first, count):
    line = lax.broadcasted_iota(jnp.int32, (count, 128), 0) + first
    lane = lax.broadcasted_iota(jnp.int32, (count, 128), 1)
    return jnp.sum(jnp.where(line == lane, jnp.broadcast_to(row, (count, 128)), 0.0), axis=1, keepdims=True)


def start_kernel(residual_ref, diag_ref, wide_ref, start_ref, scale_ref):
    diag_row = jnp.concatenate([diag_ref[...], jnp.zeros((1, 128 - SHARE), F32)], axis=1)
    scale = jnp.broadcast_to(column_of(diag_row, 0, SHARE), (SHARE, NRHS))
    scaled = residual_ref[...] * scale
    scale_ref[...] = scale
    start_ref[...] = scaled
    high = scaled.astype(BF16)
    low = scaled - high.astype(F32)
    d_high = diag_row.astype(BF16).astype(F32)
    d_mid = (diag_row - d_high).astype(BF16).astype(F32)
    d_low = diag_row - d_high - d_mid
    d_rows = jnp.concatenate([d_high, d_mid, d_low] + [d_low] * 5, axis=0)
    for x in range(SIDE):
        tail = jnp.concatenate([low[SLAB * x:SLAB * (x + 1)], d_rows], axis=0).astype(BF16)
        for q in range(SIDE):
            wide_ref[SIDE * x + q, 0:SHARE] = high
            wide_ref[SIDE * x + q, SHARE:128] = tail


def pack_kernel(tiles_ref, out_ref):
    tiles = [tiles_ref[j].astype(F32) for j in range(2)]
    for x in range(SIDE):
        for q in range(SIDE):
            at = SHARE * q + SLAB * x
            out_ref[SIDE * x + q] = jnp.concatenate([tile[at:at + SLAB] for tile in tiles], axis=0).astype(BF16)


def pick_home_kernel(place_ref, rows_ref, got_ref, up_ref, down_ref):
    lead = place_ref[0]
    for side, ref in ((0, up_ref), (1, down_ref)):
        for h in range(2):
            row = rows_ref[lead, side, h]
            for q in range(SIDE):
                ref[h, SHARE * q:SHARE * (q + 1)] = got_ref[SIDE * row + q, 0:SHARE]


def pick_slab_kernel(place_ref, rows_ref, got_ref, own_ref, up_ref, down_ref):
    lead = place_ref[0]
    for q in range(SIDE):
        parts = [got_ref[SIDE * x + q, 0:SHARE].astype(F32) for x in range(SIDE)]
        for r in range(SIDE):
            block = jnp.concatenate([p[SLAB * r:SLAB * (r + 1)] for p in parts], axis=0)
            own_ref[r, SHARE * q:SHARE * (q + 1)] = block.astype(BF16)
    for side, ref in ((0, up_ref), (1, down_ref)):
        for h in range(2):
            ref[h] = own_ref[rows_ref[lead, side, h]]


def order_kernel(slot_ref, slabs_ref, out_ref):
    for t in range(TILES):
        slot = slot_ref[0, t]
        piece = slabs_ref[t // 2].astype(F32)[SLAB * (t % 2):SLAB * (t % 2 + 1)]
        out_ref[slot] = piece.astype(BF16)


def first_kernel(place_ref, slot_ref, cols_ref, slabs_ref, got_ref, low_ref, high_ref,
                 wide_ref, product_ref, total_ref, line_ref):
    x, q = place_ref[1], place_ref[2]
    slabs = jnp.concatenate([slabs_ref[m] for m in range(GROUP)], axis=0)
    own = [jnp.concatenate([got_ref[SIDE * r + s, 0:SHARE] for s in range(SIDE)], axis=0) for r in range(SIDE)]
    blocks = own + [low_ref[0], low_ref[1], high_ref[0], high_ref[1]]
    for pair in range(4):
        wide = jnp.concatenate(blocks[2 * pair:2 * pair + 2], axis=1)
        product = jnp.dot(slabs, wide, preferred_element_type=F32)
        product_ref[2 * pair] = product[:, :128]
        product_ref[2 * pair + 1] = product[:, 128:]
    total_ref[...] = jnp.zeros_like(total_ref)
    for t in range(TILES):
        slot = slot_ref[0, t]
        row = lax.shift_right_logical(slot, 3)
        col = cols_ref[row, lax.bitwise_and(slot, 7)]
        total_ref[row] += product_ref[col, SLAB * t:SLAB * (t + 1)]
    firsts = []
    for r in range(SIDE):
        whole = got_ref[SIDE * r + q].astype(F32)
        line_ref[...] = whole
        high = line_ref[pl.ds(pl.multiple_of(x * SLAB, 8), SLAB), :]
        row = whole[120:121] + (whole[121:122] + whole[122:123])
        scale = column_of(row, x * SLAB, SLAB)
        firsts.append(GAIN * (high + whole[SHARE:120] - scale * total_ref[r]))
    first = jnp.concatenate(firsts, axis=0)
    high = first.astype(BF16)
    low = first - high.astype(F32)
    for r in range(SIDE):
        tail = jnp.concatenate([low[SLAB * r:SLAB * (r + 1)], jnp.zeros((8, NRHS), F32)], axis=0).astype(BF16)
        for s in range(SIDE):
            wide_ref[SIDE * r + s, 0:SHARE] = high
            wide_ref[SIDE * r + s, SHARE:128] = tail


def home_product(place_ref, cols_ref, matrix_ref, ext_ref):
    row = place_ref[1]
    total = jnp.zeros((SHARE, NRHS), F32)
    for k in range(8):
        left = jnp.concatenate([matrix_ref[s, k] for s in range(SIDE)], axis=0)
        total += jnp.dot(left, ext_ref[cols_ref[row, k]], preferred_element_type=F32)
    return total


def fill_halo(ext_ref, low_ref, high_ref):
    for h in range(2):
        ext_ref[4 + h] = low_ref[h]
        ext_ref[6 + h] = high_ref[h]


def second_kernel(place_ref, cols_ref, matrix_ref, got_ref, own_ref, low_ref, high_ref, start_ref, scale_ref,
                  wide_ref, sum_ref, ext_ref, line_ref):
    ext_ref[0:4] = own_ref[...]
    fill_halo(ext_ref, low_ref, high_ref)
    total = home_product(place_ref, cols_ref, matrix_ref, ext_ref)
    row, q = place_ref[1], place_ref[2]
    firsts = []
    for x in range(SIDE):
        line_ref[...] = got_ref[SIDE * x + q].astype(F32)
        firsts.append(line_ref[pl.ds(pl.multiple_of(row * SLAB, 8), SLAB), :] + line_ref[SHARE:120])
    first = jnp.concatenate(firsts, axis=0)
    second = start_ref[...] - first - scale_ref[...] * total
    sum_ref[...] = first + GAIN * second
    second = second.astype(BF16)
    for m in range(GROUP):
        wide_ref[m] = second


def last_kernel(place_ref, cols_ref, matrix_ref, got_ref, low_ref, high_ref, sum_ref, scale_ref, out_ref, ext_ref):
    for r in range(SIDE):
        for q in range(SIDE):
            ext_ref[r, SHARE * q:SHARE * (q + 1)] = got_ref[SIDE * r + q]
    fill_halo(ext_ref, low_ref, high_ref)
    total = home_product(place_ref, cols_ref, matrix_ref, ext_ref)
    out_ref[...] = sum_ref[...] - GAIN * (scale_ref[...] * total)


def arr(shape, dtype):
    return pltpu.VMEM(shape, dtype)


def call(kernel, name, specs, outs, scratch=()):
    return pl.pallas_call(kernel, name=name, in_specs=specs, out_specs=[VMEM] * len(outs),
                          out_shape=outs, scratch_shapes=list(scratch))


def near(*arrays):
    out = tuple(pltpu.with_memory_space_constraint(a, pltpu.VMEM) for a in arrays)
    return out if len(out) > 1 else out[0]


HALVES = [arr((2, TILE, NRHS), BF16), arr((2, TILE, NRHS), BF16)]
ROWS = arr((SHARE, NRHS), F32)
WIDE = arr((GROUP, 128, NRHS), BF16)
EXT = pltpu.VMEM((8, TILE, NRHS), BF16)
LINE = pltpu.VMEM((128, NRHS), F32)


def local(matrix_tiles, tile_slot, tile_cols, send_rows, residual, diag_inv):
    leads = lax.axis_size("lead")
    lead, member = lax.axis_index("lead"), lax.axis_index("grp")
    place = jnp.stack([lead, member // SIDE, member % SIDE]).astype(jnp.int32)
    ahead = [(i, (i + 1) % leads) for i in range(leads)]
    behind = [(i, (i - 1) % leads) for i in range(leads)]

    def halo(up, down):
        return near(lax.ppermute(up, "lead", ahead), lax.ppermute(down, "lead", behind))

    def gather(wide):
        return near(lax.all_to_all(wide, "grp", 0, 0))

    wide, start, scale = call(start_kernel, "start", [VMEM] * 2, [WIDE, ROWS, ROWS])(
        residual, diag_inv.reshape(1, SHARE))
    start, scale = near(start, scale)
    packed, = call(pack_kernel, "pack", [VMEM], [arr((GROUP, 2 * SLAB, TILE), BF16)])(matrix_tiles)
    got0 = gather(wide)
    slabs = gather(packed)
    up, down = call(pick_home_kernel, "pick0", [SMEM] * 2 + [VMEM], HALVES)(place, send_rows, got0)
    low, high = halo(up, down)
    wide, = call(
        first_kernel, "apply0", [SMEM] * 3 + [VMEM] * 4, [WIDE],
        (pltpu.VMEM((8, TILES * SLAB, NRHS), F32), pltpu.VMEM((SIDE, SLAB, NRHS), F32), LINE))(
        place, tile_slot, tile_cols, slabs, got0, low, high)
    got1 = gather(wide)
    ordered, = call(order_kernel, "order", [SMEM, VMEM], [arr((TILES, SLAB, TILE), BF16)])(tile_slot, slabs)
    matrix = near(lax.all_to_all(ordered.reshape(SIDE, 8, SLAB, TILE), "grp", 0, 0, axis_index_groups=X_GROUPS))
    own, up, down = call(pick_slab_kernel, "pick1", [SMEM] * 2 + [VMEM],
                         [arr((SIDE, TILE, NRHS), BF16)] + HALVES)(place, send_rows, got1)
    low, high = halo(up, down)
    own = near(own)
    wide, partial = call(second_kernel, "apply1", [SMEM] * 2 + [VMEM] * 7,
                         [arr((GROUP, SHARE, NRHS), BF16), ROWS], (EXT, LINE))(
        place, tile_cols, matrix, got1, own, low, high, start, scale)
    got2 = gather(wide)
    partial = near(partial)
    up, down = call(pick_home_kernel, "pick2", [SMEM] * 2 + [VMEM], HALVES)(place, send_rows, got2)
    low, high = halo(up, down)
    result, = call(last_kernel, "apply2", [SMEM] * 2 + [VMEM] * 6, [jax.ShapeDtypeStruct((SHARE, NRHS), F32)], (EXT,))(
        place, tile_cols, matrix, got2, low, high, partial, scale)
    return result


def solution(mesh):
    in_specs = (
        P(("lead", "grp"), None, None),
        P("lead", None),
        P("lead", None),
        P(),
        P(("lead", "grp"), None),
        P(("lead", "grp")),
    )
    out_specs = P(("lead", "grp"), None)
    return jax.shard_map(local, mesh=mesh, in_specs=in_specs, out_specs=out_specs, check_vma=False)
```

```python
import jax
import jax.numpy as jnp
from jax import lax
from jax.experimental import pallas as pl
from jax.experimental.pallas import tpu as pltpu
from jax.sharding import PartitionSpec as P


TILE = 384
NRHS = 128
SIDE = 4
GROUP = 16
SHARE = 96
SLAB = 24
TILES = 32
PIECE = 64
F32 = jnp.float32
BF16 = jnp.bfloat16
GRANT = 20 << 20
GAIN = 8.0 / 7.0

VMEM = pl.BlockSpec(memory_space=pltpu.VMEM)
SMEM = pl.BlockSpec(memory_space=pltpu.SMEM)


def place():
    member = lax.axis_index("grp")
    return lax.shift_right_logical(member, 2), lax.bitwise_and(member, 3)


def wrap(index):
    return lax.bitwise_and(index, 3)


def column_of(row, first, count):
    line = lax.broadcasted_iota(jnp.int32, (count, 128), 0) + first
    lane = lax.broadcasted_iota(jnp.int32, (count, 128), 1)
    return jnp.sum(jnp.where(line == lane, jnp.broadcast_to(row, (count, 128)), 0.0), axis=1, keepdims=True)


def padded(diag_ref):
    return jnp.concatenate([diag_ref[...], jnp.zeros((1, 128 - SHARE), F32)], axis=1)


def start_kernel(residual_ref, diag_ref, high_ref, start_ref, scale_ref):
    scale = jnp.broadcast_to(column_of(padded(diag_ref), 0, SHARE), (SHARE, NRHS))
    scaled = residual_ref[...] * scale
    scale_ref[...] = scale
    start_ref[...] = scaled
    high_ref[...] = scaled.astype(BF16)


def pack_kernel(tiles_ref, start_ref, diag_ref, out_ref):
    scaled = start_ref[...]
    low = scaled - scaled.astype(BF16).astype(F32)
    row = padded(diag_ref)
    d_high = row.astype(BF16).astype(F32)
    d_mid = (row - d_high).astype(BF16).astype(F32)
    d_rows = jnp.broadcast_to(jnp.concatenate([d_high, d_mid, row - d_high - d_mid], axis=1), (8, TILE))
    tiles = [tiles_ref[j].astype(F32) for j in range(2)]
    for x in range(SIDE):
        mine = low[SLAB * x:SLAB * (x + 1)]
        tail = [jnp.concatenate([mine[8 * k:8 * k + 8] for k in range(3)], axis=1), d_rows]
        for q in range(SIDE):
            at = SHARE * q + SLAB * x
            rows = [tile[at:at + SLAB] for tile in tiles]
            out_ref[SIDE * x + q] = jnp.concatenate(rows + tail, axis=0).astype(BF16)


def stack_kernel(*refs):
    out_ref = refs[-1]
    x, _ = place()
    for k in range(SIDE):
        out_ref[wrap(x - k)] = refs[k][...]


def send_halves(rows_ref, own_ref, up_ref, down_ref):
    lead = lax.axis_index("lead")
    for side, ref in ((0, up_ref), (1, down_ref)):
        for h in range(2):
            ref[h] = own_ref[rows_ref[side, h, lead]]


def pick_stack_kernel(rows_ref, *refs):
    own_ref, up_ref, down_ref = refs[4:]
    _, q = place()
    for k in range(SIDE):
        at = pl.multiple_of(wrap(q - k) * SHARE, SHARE)
        for r in range(SIDE):
            own_ref[r, pl.ds(at, SHARE)] = refs[k][r]
    send_halves(rows_ref, own_ref, up_ref, down_ref)


def pick_slab_kernel(rows_ref, got_ref, own_ref, up_ref, down_ref):
    for q in range(SIDE):
        parts = [got_ref[SIDE * x + q, 0:SHARE].astype(F32) for x in range(SIDE)]
        for r in range(SIDE):
            block = jnp.concatenate([p[SLAB * r:SLAB * (r + 1)] for p in parts], axis=0)
            own_ref[r, SHARE * q:SHARE * (q + 1)] = block.astype(BF16)
    send_halves(rows_ref, own_ref, up_ref, down_ref)


def pick_home_kernel(rows_ref, got_ref, own_ref, up_ref, down_ref):
    for r in range(SIDE):
        for q in range(SIDE):
            own_ref[r, SHARE * q:SHARE * (q + 1)] = got_ref[SIDE * r + q]
    send_halves(rows_ref, own_ref, up_ref, down_ref)


def order_kernel(slot_ref, slabs_ref, *refs):
    outs, held_ref = refs[:4], refs[4]
    x, _ = place()
    for t in range(TILES):
        piece = slabs_ref[t // 2].astype(F32)[SLAB * (t % 2):SLAB * (t % 2 + 1)]
        slot = slot_ref[0, t]
        held_ref[lax.bitwise_and(slot - 8 * x, TILES - 1)] = piece.astype(BF16)
    for k in range(SIDE):
        outs[k][...] = held_ref[8 * k:8 * k + 8]


def slab_products(slabs, blocks, product_ref, first):
    for pair in range(len(blocks) // 2):
        wide = jnp.concatenate(blocks[2 * pair:2 * pair + 2], axis=1)
        product = jnp.dot(slabs, wide, preferred_element_type=F32)
        product_ref[first + 2 * pair] = product[:, :NRHS]
        product_ref[first + 2 * pair + 1] = product[:, NRHS:]


def all_slabs(slabs_ref):
    return jnp.concatenate([slabs_ref[m, 0:2 * SLAB] for m in range(GROUP)], axis=0)


def near_kernel(slabs_ref, own_ref, product_ref):
    slab_products(all_slabs(slabs_ref), [own_ref[r] for r in range(SIDE)], product_ref, 0)


def first_kernel(slot_ref, cols_ref, slabs_ref, own_ref, near_ref, low_ref, high_ref,
                 wide_ref, product_ref, total_ref, line_ref):
    x, q = place()
    slab_products(all_slabs(slabs_ref), [low_ref[0], low_ref[1], high_ref[0], high_ref[1]], product_ref, 4)
    product_ref[0:4] = near_ref[...]
    total_ref[...] = jnp.zeros_like(total_ref)
    for t in range(TILES):
        slot = slot_ref[0, t]
        row = lax.shift_right_logical(slot, 3)
        col = cols_ref[row, lax.bitwise_and(slot, 7)]
        total_ref[row] += product_ref[col, SLAB * t:SLAB * (t + 1)]
    firsts = []
    at = pl.multiple_of(q * SHARE, SHARE)
    for r in range(SIDE):
        line_ref[...] = own_ref[r, pl.ds(at, SHARE)].astype(F32)
        high = line_ref[pl.ds(pl.multiple_of(x * SLAB, 8), SLAB), :]
        tail = slabs_ref[SIDE * r + q, 48:PIECE].astype(F32)
        low = jnp.concatenate([tail[0:8, NRHS * k:NRHS * (k + 1)] for k in range(3)], axis=0)
        row = tail[8:9, 0:128] + (tail[8:9, 128:256] + tail[8:9, 256:384])
        firsts.append(GAIN * (high + low - column_of(row, x * SLAB, SLAB) * total_ref[r]))
    first = jnp.concatenate(firsts, axis=0)
    high = first.astype(BF16)
    low = first - high.astype(F32)
    for r in range(SIDE):
        tail = jnp.concatenate([low[SLAB * r:SLAB * (r + 1)], jnp.zeros((8, NRHS), F32)], axis=0).astype(BF16)
        for s in range(SIDE):
            wide_ref[SIDE * r + s, 0:SHARE] = high
            wide_ref[SIDE * r + s, SHARE:128] = tail


def home_product(cols_ref, parts, ext_ref, line_ref):
    x, _ = place()
    total = jnp.zeros((SHARE, NRHS), F32)
    for k in range(8):
        left = jnp.concatenate([part[k] for part in parts], axis=0)
        total += jnp.dot(left, ext_ref[cols_ref[x, k]], preferred_element_type=F32)
    for k in range(SIDE):
        line_ref[pl.ds(pl.multiple_of(wrap(x - k) * SLAB, 8), SLAB), :] = total[SLAB * k:SLAB * (k + 1)]
    return line_ref[0:SHARE]


def fill(ext_ref, own_ref, low_ref, high_ref):
    ext_ref[0:4] = own_ref[...]
    ext_ref[4:6] = low_ref[...]
    ext_ref[6:8] = high_ref[...]


def second_kernel(cols_ref, *refs):
    parts = refs[:4]
    got_ref, own_ref, low_ref, high_ref, start_ref, scale_ref, wide_ref, sum_ref, ext_ref, line_ref = refs[4:]
    fill(ext_ref, own_ref, low_ref, high_ref)
    total = home_product(cols_ref, parts, ext_ref, line_ref)
    row, q = place()
    firsts = []
    for x in range(SIDE):
        line_ref[...] = got_ref[SIDE * x + q].astype(F32)
        firsts.append(line_ref[pl.ds(pl.multiple_of(row * SLAB, 8), SLAB), :] + line_ref[SHARE:120])
    first = jnp.concatenate(firsts, axis=0)
    second = start_ref[...] - first - scale_ref[...] * total
    sum_ref[...] = first + GAIN * second
    second = second.astype(BF16)
    for m in range(GROUP):
        wide_ref[m] = second


def last_kernel(cols_ref, *refs):
    parts = refs[:4]
    own_ref, low_ref, high_ref, sum_ref, scale_ref, out_ref, ext_ref, line_ref = refs[4:]
    fill(ext_ref, own_ref, low_ref, high_ref)
    total = home_product(cols_ref, parts, ext_ref, line_ref)
    out_ref[...] = sum_ref[...] - GAIN * (scale_ref[...] * total)


def arr(shape, dtype):
    return pltpu.VMEM(shape, dtype)


def call(kernel, args, outs, scalars=0, scratch=()):
    vectors = args[scalars:]
    if vectors:
        vectors = [pltpu.with_memory_space_constraint(a, pltpu.VMEM) if near else a for a, near in vectors]
    specs = [SMEM] * scalars + [VMEM] * len(vectors)
    return pl.pallas_call(kernel, in_specs=specs, out_specs=[VMEM] * len(outs),
                          out_shape=outs, scratch_shapes=list(scratch),
                          compiler_params=pltpu.CompilerParams(vmem_limit_bytes=GRANT))(*args[:scalars], *vectors)


def near(*arrays):
    return [(a, True) for a in arrays]


HALVES = [arr((2, TILE, NRHS), BF16), arr((2, TILE, NRHS), BF16)]
OWN = arr((SIDE, TILE, NRHS), BF16)
ROWS = arr((SHARE, NRHS), F32)
EXT = arr((8, TILE, NRHS), BF16)
LINE = arr((128, NRHS), F32)


def body(matrix_tiles, tile_slot, tile_cols, send_rows, residual, diag_inv):
    leads = lax.axis_size("lead")
    rows = send_rows.transpose(1, 2, 0)
    diag = diag_inv.reshape(1, SHARE)

    def halo(up, down):
        return (lax.ppermute(up, "lead", [(i, (i + 1) % leads) for i in range(leads)]),
                lax.ppermute(down, "lead", [(i, (i - 1) % leads) for i in range(leads)]))

    def gather(wide):
        return lax.all_to_all(wide, "grp", 0, 0)

    def along_x(value, k):
        return lax.ppermute(value, "grp", [(m, (m + SIDE * k) % GROUP) for m in range(GROUP)])

    def along_y(value, k):
        return lax.ppermute(value, "grp", [(m, m - m % SIDE + (m + k) % SIDE) for m in range(GROUP)])

    high, start, scale = call(start_kernel, [(residual, False), (diag, False)],
                              [arr((SHARE, NRHS), BF16), ROWS, ROWS])
    shares = [high] + [along_x(high, k) for k in range(1, SIDE)]
    packed, = call(pack_kernel, [(matrix_tiles, False)] + near(start) + [(diag, False)],
                   [arr((GROUP, PIECE, TILE), BF16)])
    slabs = gather(packed)
    column, = call(stack_kernel, near(*shares), [arr((SIDE, SHARE, NRHS), BF16)])
    columns = [column] + [along_y(column, k) for k in range(1, SIDE)]
    own, up, down = call(pick_stack_kernel, [rows] + near(*columns), [OWN] + HALVES, 1)
    lower, upper = halo(up, down)
    product, = call(near_kernel, near(slabs, own), [arr((4, TILES * SLAB, NRHS), F32)])
    wide, = call(first_kernel, [tile_slot, tile_cols] + near(slabs, own, product, lower, upper),
                 [arr((GROUP, 128, NRHS), BF16)], 2,
                 (arr((8, TILES * SLAB, NRHS), F32), arr((SIDE, SLAB, NRHS), F32), arr((SHARE, NRHS), F32)))
    got = gather(wide)
    ordered = call(order_kernel, [tile_slot] + near(slabs), [arr((8, SLAB, TILE), BF16)] * 4, 1,
                   (arr((TILES, SLAB, TILE), BF16),))
    parts = [ordered[0]]
    for k in range(1, SIDE):
        parts.append(along_x(ordered[k], k))
    own, up, down = call(pick_slab_kernel, [rows] + near(got), [OWN] + HALVES, 1)
    lower, upper = halo(up, down)
    wide, partial = call(second_kernel,
                         [tile_cols] + near(*parts, got, own, lower, upper, start, scale),
                         [arr((GROUP, SHARE, NRHS), BF16), ROWS], 1, (EXT, LINE))
    got = gather(wide)
    own, up, down = call(pick_home_kernel, [rows] + near(got), [OWN] + HALVES, 1)
    lower, upper = halo(up, down)
    result, = call(last_kernel, [tile_cols] + near(*parts, own, lower, upper, partial, scale),
                   [jax.ShapeDtypeStruct((SHARE, NRHS), F32)], 1, (EXT, LINE))
    return result


def solution(mesh):
    in_specs = (
        P(("lead", "grp"), None, None),
        P("lead", None),
        P("lead", None),
        P(),
        P(("lead", "grp"), None),
        P(("lead", "grp")),
    )
    out_specs = P(("lead", "grp"), None)
    return jax.shard_map(body, mesh=mesh, in_specs=in_specs, out_specs=out_specs, check_vma=False)
```

```python
import jax
import jax.numpy as jnp
from jax import lax
from jax.experimental import pallas as pl
from jax.experimental.pallas import tpu as pltpu
from jax.sharding import PartitionSpec as P


TILE = 384
NRHS = 128
SIDE = 4
GROUP = 16
SHARE = 96
SLAB = 24
TILES = 32
PIECE = 96
F32 = jnp.float32
BF16 = jnp.bfloat16
GRANT = 20 << 20
GAIN = 8.0 / 7.0

VMEM = pl.BlockSpec(memory_space=pltpu.VMEM)
SMEM = pl.BlockSpec(memory_space=pltpu.SMEM)


def place():
    member = lax.axis_index("grp")
    return lax.shift_right_logical(member, 2), lax.bitwise_and(member, 3)


def wrap(index):
    return lax.bitwise_and(index, 3)


def column_of(row, first, count):
    line = lax.broadcasted_iota(jnp.int32, (count, 128), 0) + first
    lane = lax.broadcasted_iota(jnp.int32, (count, 128), 1)
    return jnp.sum(jnp.where(line == lane, jnp.broadcast_to(row, (count, 128)), 0.0), axis=1, keepdims=True)


def padded(diag_ref):
    return jnp.concatenate([diag_ref[...], jnp.zeros((1, 128 - SHARE), F32)], axis=1)


def start_kernel(tiles_ref, residual_ref, diag_ref, out_ref, start_ref, scale_ref):
    row = padded(diag_ref)
    scale = jnp.broadcast_to(column_of(row, 0, SHARE), (SHARE, NRHS))
    scaled = residual_ref[...] * scale
    scale_ref[...] = scale
    start_ref[...] = scaled
    high = scaled.astype(BF16).astype(F32)
    low = scaled - high
    high = jnp.concatenate([high[32 * k:32 * (k + 1)] for k in range(3)], axis=1).astype(BF16)
    d_high = row.astype(BF16).astype(F32)
    d_mid = (row - d_high).astype(BF16).astype(F32)
    d_rows = jnp.broadcast_to(jnp.concatenate([d_high, d_mid, row - d_high - d_mid], axis=1), (8, TILE))
    tiles = [tiles_ref[j].astype(F32) for j in range(2)]
    for x in range(SIDE):
        mine = low[SLAB * x:SLAB * (x + 1)]
        tail = jnp.concatenate([jnp.concatenate([mine[8 * k:8 * k + 8] for k in range(3)], axis=1), d_rows], axis=0)
        tail = tail.astype(BF16)
        for q in range(SIDE):
            at = SHARE * q + SLAB * x
            out_ref[SIDE * x + q, 0:48] = jnp.concatenate([tile[at:at + SLAB] for tile in tiles], axis=0).astype(BF16)
            out_ref[SIDE * x + q, 48:80] = high
            out_ref[SIDE * x + q, 80:PIECE] = tail


def send_halves(rows_ref, own_ref, up_ref, down_ref):
    lead = lax.axis_index("lead")
    for side, ref in ((0, up_ref), (1, down_ref)):
        for h in range(2):
            ref[h] = own_ref[rows_ref[side, h, lead]]


def pick_first_kernel(rows_ref, got_ref, own_ref, up_ref, down_ref):
    for m in range(GROUP):
        for k in range(3):
            at = SHARE * (m % SIDE) + 32 * k
            own_ref[m // SIDE, at:at + 32] = got_ref[m, 48:80, NRHS * k:NRHS * (k + 1)]
    send_halves(rows_ref, own_ref, up_ref, down_ref)


def pick_slab_kernel(rows_ref, got_ref, own_ref, up_ref, down_ref):
    for q in range(SIDE):
        parts = [got_ref[SIDE * x + q, 0:SHARE].astype(F32) for x in range(SIDE)]
        for r in range(SIDE):
            block = jnp.concatenate([p[SLAB * r:SLAB * (r + 1)] for p in parts], axis=0)
            own_ref[r, SHARE * q:SHARE * (q + 1)] = block.astype(BF16)
    send_halves(rows_ref, own_ref, up_ref, down_ref)


def pick_home_kernel(rows_ref, got_ref, own_ref, up_ref, down_ref):
    for r in range(SIDE):
        for q in range(SIDE):
            own_ref[r, SHARE * q:SHARE * (q + 1)] = got_ref[SIDE * r + q]
    send_halves(rows_ref, own_ref, up_ref, down_ref)


def order_kernel(slot_ref, slabs_ref, *refs):
    outs, held_ref = refs[:4], refs[4]
    x, _ = place()
    for t in range(TILES):
        piece = slabs_ref[t // 2].astype(F32)[SLAB * (t % 2):SLAB * (t % 2 + 1)]
        slot = slot_ref[0, t]
        held_ref[lax.bitwise_and(slot - 8 * x, TILES - 1)] = piece.astype(BF16)
    for k in range(SIDE):
        outs[k][...] = held_ref[8 * k:8 * k + 8]


def slab_products(slabs, blocks, product_ref, first):
    for pair in range(len(blocks) // 2):
        wide = jnp.concatenate(blocks[2 * pair:2 * pair + 2], axis=1)
        product = jnp.dot(slabs, wide, preferred_element_type=F32)
        product_ref[first + 2 * pair] = product[:, :NRHS]
        product_ref[first + 2 * pair + 1] = product[:, NRHS:]


def all_slabs(slabs_ref):
    return jnp.concatenate([slabs_ref[m, 0:2 * SLAB] for m in range(GROUP)], axis=0)


def near_kernel(slabs_ref, own_ref, product_ref):
    slab_products(all_slabs(slabs_ref), [own_ref[r] for r in range(SIDE)], product_ref, 0)


def first_kernel(slot_ref, cols_ref, slabs_ref, own_ref, near_ref, low_ref, high_ref,
                 wide_ref, product_ref, total_ref, line_ref):
    x, q = place()
    slab_products(all_slabs(slabs_ref), [low_ref[0], low_ref[1], high_ref[0], high_ref[1]], product_ref, 4)
    product_ref[0:4] = near_ref[...]
    total_ref[...] = jnp.zeros_like(total_ref)
    for t in range(TILES):
        slot = slot_ref[0, t]
        row = lax.shift_right_logical(slot, 3)
        col = cols_ref[row, lax.bitwise_and(slot, 7)]
        total_ref[row] += product_ref[col, SLAB * t:SLAB * (t + 1)]
    firsts = []
    at = pl.multiple_of(q * SHARE, SHARE)
    for r in range(SIDE):
        line_ref[...] = own_ref[r, pl.ds(at, SHARE)].astype(F32)
        high = line_ref[pl.ds(pl.multiple_of(x * SLAB, 8), SLAB), :]
        tail = slabs_ref[SIDE * r + q, 80:PIECE].astype(F32)
        low = jnp.concatenate([tail[0:8, NRHS * k:NRHS * (k + 1)] for k in range(3)], axis=0)
        row = tail[8:9, 0:128] + (tail[8:9, 128:256] + tail[8:9, 256:384])
        firsts.append(GAIN * (high + low - column_of(row, x * SLAB, SLAB) * total_ref[r]))
    first = jnp.concatenate(firsts, axis=0)
    high = first.astype(BF16)
    low = first - high.astype(F32)
    for r in range(SIDE):
        tail = jnp.concatenate([low[SLAB * r:SLAB * (r + 1)], jnp.zeros((8, NRHS), F32)], axis=0).astype(BF16)
        for s in range(SIDE):
            wide_ref[SIDE * r + s, 0:SHARE] = high
            wide_ref[SIDE * r + s, SHARE:128] = tail


def home_product(cols_ref, parts, ext_ref, line_ref):
    x, _ = place()
    total = jnp.zeros((SHARE, NRHS), F32)
    for k in range(8):
        left = jnp.concatenate([part[k] for part in parts], axis=0)
        total += jnp.dot(left, ext_ref[cols_ref[x, k]], preferred_element_type=F32)
    for k in range(SIDE):
        line_ref[pl.ds(pl.multiple_of(wrap(x - k) * SLAB, 8), SLAB), :] = total[SLAB * k:SLAB * (k + 1)]
    return line_ref[0:SHARE]


def fill(ext_ref, own_ref, low_ref, high_ref):
    ext_ref[0:4] = own_ref[...]
    ext_ref[4:6] = low_ref[...]
    ext_ref[6:8] = high_ref[...]


def second_kernel(cols_ref, *refs):
    parts = refs[:4]
    got_ref, own_ref, low_ref, high_ref, start_ref, scale_ref, wide_ref, sum_ref, ext_ref, line_ref = refs[4:]
    fill(ext_ref, own_ref, low_ref, high_ref)
    total = home_product(cols_ref, parts, ext_ref, line_ref)
    row, q = place()
    firsts = []
    for x in range(SIDE):
        line_ref[...] = got_ref[SIDE * x + q].astype(F32)
        firsts.append(line_ref[pl.ds(pl.multiple_of(row * SLAB, 8), SLAB), :] + line_ref[SHARE:120])
    first = jnp.concatenate(firsts, axis=0)
    second = start_ref[...] - first - scale_ref[...] * total
    sum_ref[...] = first + GAIN * second
    second = second.astype(BF16)
    for m in range(GROUP):
        wide_ref[m] = second


def last_kernel(cols_ref, *refs):
    parts = refs[:4]
    own_ref, low_ref, high_ref, sum_ref, scale_ref, out_ref, ext_ref, line_ref = refs[4:]
    fill(ext_ref, own_ref, low_ref, high_ref)
    total = home_product(cols_ref, parts, ext_ref, line_ref)
    out_ref[...] = sum_ref[...] - GAIN * (scale_ref[...] * total)


def arr(shape, dtype):
    return pltpu.VMEM(shape, dtype)


def call(kernel, args, outs, scalars=0, scratch=()):
    vectors = args[scalars:]
    if vectors:
        vectors = [pltpu.with_memory_space_constraint(a, pltpu.VMEM) if near else a for a, near in vectors]
    specs = [SMEM] * scalars + [VMEM] * len(vectors)
    return pl.pallas_call(kernel, in_specs=specs, out_specs=[VMEM] * len(outs),
                          out_shape=outs, scratch_shapes=list(scratch),
                          compiler_params=pltpu.CompilerParams(vmem_limit_bytes=GRANT))(*args[:scalars], *vectors)


def near(*arrays):
    return [(a, True) for a in arrays]


HALVES = [arr((2, TILE, NRHS), BF16), arr((2, TILE, NRHS), BF16)]
OWN = arr((SIDE, TILE, NRHS), BF16)
ROWS = arr((SHARE, NRHS), F32)
EXT = arr((8, TILE, NRHS), BF16)
LINE = arr((128, NRHS), F32)


def body(matrix_tiles, tile_slot, tile_cols, send_rows, residual, diag_inv):
    leads = lax.axis_size("lead")
    rows = send_rows.transpose(1, 2, 0)
    diag = diag_inv.reshape(1, SHARE)

    def halo(up, down):
        return (lax.ppermute(up, "lead", [(i, (i + 1) % leads) for i in range(leads)]),
                lax.ppermute(down, "lead", [(i, (i - 1) % leads) for i in range(leads)]))

    def gather(wide):
        return lax.all_to_all(wide, "grp", 0, 0)

    def along_x(value, k):
        return lax.ppermute(value, "grp", [(m, (m + SIDE * k) % GROUP) for m in range(GROUP)])

    packed, start, scale = call(start_kernel, [(matrix_tiles, False), (residual, False), (diag, False)],
                                [arr((GROUP, PIECE, TILE), BF16), ROWS, ROWS])
    slabs = gather(packed)
    own, up, down = call(pick_first_kernel, [rows] + near(slabs), [OWN] + HALVES, 1)
    lower, upper = halo(up, down)
    product, = call(near_kernel, near(slabs, own), [arr((4, TILES * SLAB, NRHS), F32)])
    wide, = call(first_kernel, [tile_slot, tile_cols] + near(slabs, own, product, lower, upper),
                 [arr((GROUP, 128, NRHS), BF16)], 2,
                 (arr((8, TILES * SLAB, NRHS), F32), arr((SIDE, SLAB, NRHS), F32), arr((SHARE, NRHS), F32)))
    got = gather(wide)
    ordered = call(order_kernel, [tile_slot] + near(slabs), [arr((8, SLAB, TILE), BF16)] * 4, 1,
                   (arr((TILES, SLAB, TILE), BF16),))
    parts = [ordered[0]]
    for k in range(1, SIDE):
        parts.append(along_x(ordered[k], k))
    own, up, down = call(pick_slab_kernel, [rows] + near(got), [OWN] + HALVES, 1)
    lower, upper = halo(up, down)
    wide, partial = call(second_kernel,
                         [tile_cols] + near(*parts, got, own, lower, upper, start, scale),
                         [arr((GROUP, SHARE, NRHS), BF16), ROWS], 1, (EXT, LINE))
    got = gather(wide)
    own, up, down = call(pick_home_kernel, [rows] + near(got), [OWN] + HALVES, 1)
    lower, upper = halo(up, down)
    result, = call(last_kernel, [tile_cols] + near(*parts, own, lower, upper, partial, scale),
                   [jax.ShapeDtypeStruct((SHARE, NRHS), F32)], 1, (EXT, LINE))
    return result


def solution(mesh):
    in_specs = (
        P(("lead", "grp"), None, None),
        P("lead", None),
        P("lead", None),
        P(),
        P(("lead", "grp"), None),
        P(("lead", "grp")),
    )
    out_specs = P(("lead", "grp"), None)
    return jax.shard_map(body, mesh=mesh, in_specs=in_specs, out_specs=out_specs, check_vma=False)
```

```python
import jax
import jax.numpy as jnp
from jax import lax
from jax.experimental import pallas as pl
from jax.experimental.pallas import tpu as pltpu
from jax.sharding import PartitionSpec as P


TILE = 384
NRHS = 128
SIDE = 4
GROUP = 16
SHARE = 96
SLAB = 24
TILES = 32
F32 = jnp.float32
BF16 = jnp.bfloat16
GRANT = 20 << 20
GAIN = 8.0 / 7.0

VMEM = pl.BlockSpec(memory_space=pltpu.VMEM)
SMEM = pl.BlockSpec(memory_space=pltpu.SMEM)


def place():
    member = lax.axis_index("grp")
    return lax.shift_right_logical(member, 2), lax.bitwise_and(member, 3)


def wrap(index):
    return lax.bitwise_and(index, 3)


def column_of(row, first, count):
    line = lax.broadcasted_iota(jnp.int32, (count, 128), 0) + first
    lane = lax.broadcasted_iota(jnp.int32, (count, 128), 1)
    return jnp.sum(jnp.where(line == lane, jnp.broadcast_to(row, (count, 128)), 0.0), axis=1, keepdims=True)


def padded(diag_ref):
    return jnp.concatenate([diag_ref[...], jnp.zeros((1, 128 - SHARE), F32)], axis=1)


def start_kernel(residual_hbm, diag_hbm, wide_ref, start_ref, scale_ref, residual_ref, diag_ref, sems):
    copies = [pltpu.make_async_copy(residual_hbm, residual_ref, sems.at[0]),
              pltpu.make_async_copy(diag_hbm, diag_ref, sems.at[1])]
    for copy in copies:
        copy.start()
    for copy in copies:
        copy.wait()
    row = padded(diag_ref)
    scale = jnp.broadcast_to(column_of(row, 0, SHARE), (SHARE, NRHS))
    scaled = residual_ref[...] * scale
    scale_ref[...] = scale
    start_ref[...] = scaled
    high = scaled.astype(BF16)
    low = scaled - high.astype(F32)
    d_high = row.astype(BF16).astype(F32)
    d_mid = (row - d_high).astype(BF16).astype(F32)
    d_rows = jnp.concatenate([d_high, d_mid] + [row - d_high - d_mid] * 6, axis=0)
    for x in range(SIDE):
        tail = jnp.concatenate([low[SLAB * x:SLAB * (x + 1)], d_rows], axis=0).astype(BF16)
        for q in range(SIDE):
            wide_ref[SIDE * x + q, 0:SHARE] = high
            wide_ref[SIDE * x + q, SHARE:128] = tail


def pack_kernel(tiles_ref, out_ref):
    tiles = [tiles_ref[j].astype(F32) for j in range(2)]
    for x in range(SIDE):
        for q in range(SIDE):
            at = SHARE * q + SLAB * x
            out_ref[SIDE * x + q] = jnp.concatenate([tile[at:at + SLAB] for tile in tiles], axis=0).astype(BF16)


def send_halves(rows_ref, own_ref, up_ref, down_ref):
    lead = lax.axis_index("lead")
    for side, ref in ((0, up_ref), (1, down_ref)):
        for h in range(2):
            ref[h] = own_ref[rows_ref[side, h, lead]]


def pick_slab_kernel(rows_ref, got_ref, own_ref, up_ref, down_ref):
    for q in range(SIDE):
        parts = [got_ref[SIDE * x + q, 0:SHARE].astype(F32) for x in range(SIDE)]
        for r in range(SIDE):
            block = jnp.concatenate([p[SLAB * r:SLAB * (r + 1)] for p in parts], axis=0)
            own_ref[r, SHARE * q:SHARE * (q + 1)] = block.astype(BF16)
    send_halves(rows_ref, own_ref, up_ref, down_ref)


def pick_home_kernel(rows_ref, got_ref, own_ref, up_ref, down_ref):
    for r in range(SIDE):
        for q in range(SIDE):
            own_ref[r, SHARE * q:SHARE * (q + 1)] = got_ref[SIDE * r + q, 0:SHARE]
    send_halves(rows_ref, own_ref, up_ref, down_ref)


def order_kernel(slot_ref, slabs_ref, *refs):
    outs, held_ref = refs[:4], refs[4]
    x, _ = place()
    for t in range(TILES):
        piece = slabs_ref[t // 2].astype(F32)[SLAB * (t % 2):SLAB * (t % 2 + 1)]
        slot = slot_ref[0, t]
        held_ref[lax.bitwise_and(slot - 8 * x, TILES - 1)] = piece.astype(BF16)
    for k in range(SIDE):
        outs[k][...] = held_ref[8 * k:8 * k + 8]


def slab_products(slabs, blocks, product_ref, first):
    for pair in range(len(blocks) // 2):
        wide = jnp.concatenate(blocks[2 * pair:2 * pair + 2], axis=1)
        product = jnp.dot(slabs, wide, preferred_element_type=F32)
        product_ref[first + 2 * pair] = product[:, :NRHS]
        product_ref[first + 2 * pair + 1] = product[:, NRHS:]


def all_slabs(slabs_ref):
    return jnp.concatenate([slabs_ref[m] for m in range(GROUP)], axis=0)


def near_kernel(slabs_ref, own_ref, product_ref):
    slab_products(all_slabs(slabs_ref), [own_ref[r] for r in range(SIDE)], product_ref, 0)


def first_kernel(slot_ref, cols_ref, slabs_ref, got_ref, near_ref, low_ref, high_ref,
                 wide_ref, product_ref, total_ref, line_ref):
    x, q = place()
    slab_products(all_slabs(slabs_ref), [low_ref[0], low_ref[1], high_ref[0], high_ref[1]], product_ref, 4)
    product_ref[0:4] = near_ref[...]
    total_ref[...] = jnp.zeros_like(total_ref)
    for t in range(TILES):
        slot = slot_ref[0, t]
        row = lax.shift_right_logical(slot, 3)
        col = cols_ref[row, lax.bitwise_and(slot, 7)]
        total_ref[row] += product_ref[col, SLAB * t:SLAB * (t + 1)]
    firsts = []
    for r in range(SIDE):
        whole = got_ref[SIDE * r + q].astype(F32)
        line_ref[...] = whole
        high = line_ref[pl.ds(pl.multiple_of(x * SLAB, 8), SLAB), :]
        row = whole[120:121] + (whole[121:122] + whole[122:123])
        firsts.append(GAIN * (high + whole[SHARE:120] - column_of(row, x * SLAB, SLAB) * total_ref[r]))
    first = jnp.concatenate(firsts, axis=0)
    high = first.astype(BF16)
    low = first - high.astype(F32)
    for r in range(SIDE):
        tail = low[SLAB * r:SLAB * (r + 1)].astype(BF16)
        for s in range(SIDE):
            wide_ref[SIDE * r + s, 0:SHARE] = high
            wide_ref[SIDE * r + s, SHARE:120] = tail


def home_product(cols_ref, parts, ext_ref, line_ref):
    x, _ = place()
    total = jnp.zeros((SHARE, NRHS), F32)
    for k in range(8):
        left = jnp.concatenate([part[k] for part in parts], axis=0)
        total += jnp.dot(left, ext_ref[cols_ref[x, k]], preferred_element_type=F32)
    for k in range(SIDE):
        line_ref[pl.ds(pl.multiple_of(wrap(x - k) * SLAB, 8), SLAB), :] = total[SLAB * k:SLAB * (k + 1)]
    return line_ref[0:SHARE]


def fill(ext_ref, own_ref, low_ref, high_ref):
    ext_ref[0:4] = own_ref[...]
    ext_ref[4:6] = low_ref[...]
    ext_ref[6:8] = high_ref[...]


def second_kernel(cols_ref, *refs):
    parts = refs[:4]
    got_ref, own_ref, low_ref, high_ref, start_ref, scale_ref, wide_ref, sum_ref, ext_ref, line_ref = refs[4:]
    fill(ext_ref, own_ref, low_ref, high_ref)
    total = home_product(cols_ref, parts, ext_ref, line_ref)
    row, q = place()
    firsts = []
    for x in range(SIDE):
        line_ref[0:120] = got_ref[SIDE * x + q].astype(F32)
        firsts.append(line_ref[pl.ds(pl.multiple_of(row * SLAB, 8), SLAB), :] + line_ref[SHARE:120])
    first = jnp.concatenate(firsts, axis=0)
    second = start_ref[...] - first - scale_ref[...] * total
    sum_ref[...] = first + GAIN * second
    second = second.astype(BF16)
    for m in range(GROUP):
        wide_ref[m] = second


def last_kernel(cols_ref, *refs):
    parts = refs[:4]
    own_ref, low_ref, high_ref, sum_ref, scale_ref, out_ref, ext_ref, line_ref = refs[4:]
    fill(ext_ref, own_ref, low_ref, high_ref)
    total = home_product(cols_ref, parts, ext_ref, line_ref)
    out_ref[...] = sum_ref[...] - GAIN * (scale_ref[...] * total)


def arr(shape, dtype):
    return pltpu.VMEM(shape, dtype)


def call(kernel, args, outs, scalars=0, scratch=(), far=0):
    vectors = args[scalars:]
    space = pltpu.HBM if far else pltpu.VMEM
    vectors = [pltpu.with_memory_space_constraint(a, space) for a in vectors]
    specs = [SMEM] * scalars + [pl.BlockSpec(memory_space=space)] * len(vectors)
    return pl.pallas_call(kernel, in_specs=specs, out_specs=[VMEM] * len(outs),
                          out_shape=outs, scratch_shapes=list(scratch),
                          compiler_params=pltpu.CompilerParams(vmem_limit_bytes=GRANT))(*args[:scalars], *vectors)


def near(*arrays):
    return list(arrays)


HALVES = [arr((2, TILE, NRHS), BF16), arr((2, TILE, NRHS), BF16)]
OWN = arr((SIDE, TILE, NRHS), BF16)
ROWS = arr((SHARE, NRHS), F32)
EXT = arr((8, TILE, NRHS), BF16)
LINE = arr((128, NRHS), F32)


def body(matrix_tiles, tile_slot, tile_cols, send_rows, residual, diag_inv):
    leads = lax.axis_size("lead")
    rows = send_rows.transpose(1, 2, 0)
    diag = diag_inv.reshape(1, SHARE)

    def halo(up, down):
        return (lax.ppermute(up, "lead", [(i, (i + 1) % leads) for i in range(leads)]),
                lax.ppermute(down, "lead", [(i, (i - 1) % leads) for i in range(leads)]))

    def gather(wide):
        return lax.all_to_all(wide, "grp", 0, 0)

    def along_x(value, k):
        return lax.ppermute(value, "grp", [(m, (m + SIDE * k) % GROUP) for m in range(GROUP)])

    wide, start, scale = call(start_kernel, [residual, diag], [arr((GROUP, 128, NRHS), BF16), ROWS, ROWS],
                              scratch=(ROWS, arr((1, SHARE), F32), pltpu.SemaphoreType.DMA((2,))), far=1)
    got = gather(wide)
    packed, = call(pack_kernel, near(matrix_tiles), [arr((GROUP, 2 * SLAB, TILE), BF16)])
    slabs = gather(packed)
    own, up, down = call(pick_home_kernel, [rows] + near(got), [OWN] + HALVES, 1)
    lower, upper = halo(up, down)
    product, = call(near_kernel, near(slabs, own), [arr((4, TILES * SLAB, NRHS), F32)])
    wide, = call(first_kernel, [tile_slot, tile_cols] + near(slabs, got, product, lower, upper),
                 [arr((GROUP, 120, NRHS), BF16)], 2,
                 (arr((8, TILES * SLAB, NRHS), F32), arr((SIDE, SLAB, NRHS), F32), LINE))
    got = gather(wide)
    ordered = call(order_kernel, [tile_slot] + near(slabs), [arr((8, SLAB, TILE), BF16)] * 4, 1,
                   (arr((TILES, SLAB, TILE), BF16),))
    parts = [ordered[0]]
    for k in range(1, SIDE):
        parts.append(along_x(ordered[k], k))
    own, up, down = call(pick_slab_kernel, [rows] + near(got), [OWN] + HALVES, 1)
    lower, upper = halo(up, down)
    wide, partial = call(second_kernel,
                         [tile_cols] + near(*parts, got, own, lower, upper, start, scale),
                         [arr((GROUP, SHARE, NRHS), BF16), ROWS], 1, (EXT, LINE))
    got = gather(wide)
    own, up, down = call(pick_home_kernel, [rows] + near(got), [OWN] + HALVES, 1)
    lower, upper = halo(up, down)
    result, = call(last_kernel, [tile_cols] + near(*parts, own, lower, upper, partial, scale),
                   [jax.ShapeDtypeStruct((SHARE, NRHS), F32)], 1, (EXT, LINE))
    return result


def solution(mesh):
    in_specs = (
        P(("lead", "grp"), None, None),
        P("lead", None),
        P("lead", None),
        P(),
        P(("lead", "grp"), None),
        P(("lead", "grp")),
    )
    out_specs = P(("lead", "grp"), None)
    return jax.shard_map(body, mesh=mesh, in_specs=in_specs, out_specs=out_specs, check_vma=False)
```

```python
import jax
import jax.numpy as jnp
from jax import lax
from jax.experimental import pallas as pl
from jax.experimental.pallas import tpu as pltpu
from jax.sharding import PartitionSpec as P


TILE = 384
NRHS = 128
SIDE = 4
GROUP = 16
SHARE = 96
SLAB = 24
TILES = 32
F32 = jnp.float32
BF16 = jnp.bfloat16
GRANT = 20 << 20
GAIN = 8.0 / 7.0

VMEM = pl.BlockSpec(memory_space=pltpu.VMEM)
SMEM = pl.BlockSpec(memory_space=pltpu.SMEM)


def place():
    member = lax.axis_index("grp")
    return lax.shift_right_logical(member, 2), lax.bitwise_and(member, 3)


def wrap(index):
    return lax.bitwise_and(index, 3)


def column_of(row, first, count):
    line = lax.broadcasted_iota(jnp.int32, (count, 128), 0) + first
    lane = lax.broadcasted_iota(jnp.int32, (count, 128), 1)
    return jnp.sum(jnp.where(line == lane, jnp.broadcast_to(row, (count, 128)), 0.0), axis=1, keepdims=True)


def padded(diag_ref):
    return jnp.concatenate([diag_ref[...], jnp.zeros((1, 128 - SHARE), F32)], axis=1)


def start_kernel(tiles_hbm, residual_hbm, diag_hbm, part0, part1, part2, part3, wide_ref, start_ref, scale_ref,
                 residual_ref, diag_ref, sems):
    _, q = place()
    copies = [pltpu.make_async_copy(residual_hbm, residual_ref, sems.at[0]),
              pltpu.make_async_copy(diag_hbm, diag_ref, sems.at[1])]
    for k, part in enumerate((part0, part1, part2, part3)):
        at = pl.multiple_of(wrap(q + k) * SHARE, SHARE)
        copies.append(pltpu.make_async_copy(tiles_hbm.at[:, pl.ds(at, SHARE)], part, sems.at[2 + k]))
    for copy in copies:
        copy.start()
    for copy in copies[:2]:
        copy.wait()
    row = padded(diag_ref)
    scale = jnp.broadcast_to(column_of(row, 0, SHARE), (SHARE, NRHS))
    scaled = residual_ref[...] * scale
    scale_ref[...] = scale
    start_ref[...] = scaled
    high = scaled.astype(BF16)
    low = scaled - high.astype(F32)
    d_high = row.astype(BF16).astype(F32)
    d_mid = (row - d_high).astype(BF16).astype(F32)
    d_rows = jnp.concatenate([d_high, d_mid] + [row - d_high - d_mid] * 6, axis=0)
    for x in range(SIDE):
        tail = jnp.concatenate([low[SLAB * x:SLAB * (x + 1)], d_rows], axis=0).astype(BF16)
        for y in range(SIDE):
            wide_ref[SIDE * x + y, 0:SHARE] = high
            wide_ref[SIDE * x + y, SHARE:128] = tail
    for copy in copies[2:]:
        copy.wait()


def split_kernel(*refs):
    parts, outs, held_ref = refs[:4], refs[4:8], refs[8]
    x, q = place()
    for k in range(SIDE):
        tiles = [parts[k][j].astype(F32) for j in range(2)]
        for s in range(SIDE):
            pair = jnp.concatenate([tile[SLAB * s:SLAB * (s + 1)] for tile in tiles], axis=0)
            held_ref[wrap(s - x), wrap(q - k)] = pair.astype(BF16)
    for k in range(SIDE):
        outs[k][...] = held_ref[k]


def send_halves(rows_ref, own_ref, up_ref, down_ref):
    lead = lax.axis_index("lead")
    for side, ref in ((0, up_ref), (1, down_ref)):
        for h in range(2):
            ref[h] = own_ref[rows_ref[side, h, lead]]


def pick_slab_kernel(rows_ref, got_ref, own_ref, up_ref, down_ref):
    for q in range(SIDE):
        parts = [got_ref[SIDE * x + q, 0:SHARE].astype(F32) for x in range(SIDE)]
        for r in range(SIDE):
            block = jnp.concatenate([p[SLAB * r:SLAB * (r + 1)] for p in parts], axis=0)
            own_ref[r, SHARE * q:SHARE * (q + 1)] = block.astype(BF16)
    send_halves(rows_ref, own_ref, up_ref, down_ref)


def pick_home_kernel(rows_ref, got_ref, own_ref, up_ref, down_ref):
    for r in range(SIDE):
        for q in range(SIDE):
            own_ref[r, SHARE * q:SHARE * (q + 1)] = got_ref[SIDE * r + q, 0:SHARE]
    send_halves(rows_ref, own_ref, up_ref, down_ref)


def slot_of(slot_ref, x, k, i):
    return slot_ref[0, 8 * wrap(x - k) + i]


def order_kernel(slot_ref, *refs):
    parts, outs, held_ref = refs[:4], refs[4:8], refs[8]
    x, _ = place()
    for k in range(SIDE):
        for y in range(SIDE):
            pair = parts[k][y].astype(F32)
            for j in range(2):
                to = lax.bitwise_and(slot_of(slot_ref, x, k, 2 * y + j) - 8 * x, TILES - 1)
                held_ref[to] = pair[SLAB * j:SLAB * (j + 1)].astype(BF16)
    for k in range(SIDE):
        outs[k][...] = held_ref[8 * k:8 * k + 8]


def slab_products(slabs, blocks, product_ref, first):
    for pair in range(len(blocks) // 2):
        wide = jnp.concatenate(blocks[2 * pair:2 * pair + 2], axis=1)
        product = jnp.dot(slabs, wide, preferred_element_type=F32)
        product_ref[first + 2 * pair] = product[:, :NRHS]
        product_ref[first + 2 * pair + 1] = product[:, NRHS:]


def all_slabs(parts):
    return jnp.concatenate([part[y] for part in parts for y in range(SIDE)], axis=0)


def near_kernel(*refs):
    own_ref, product_ref = refs[4:]
    slab_products(all_slabs(refs[:4]), [own_ref[r] for r in range(SIDE)], product_ref, 0)


def first_kernel(slot_ref, cols_ref, *refs):
    got_ref, near_ref, low_ref, high_ref, wide_ref, product_ref, total_ref, line_ref = refs[4:]
    x, q = place()
    slab_products(all_slabs(refs[:4]), [low_ref[0], low_ref[1], high_ref[0], high_ref[1]], product_ref, 4)
    product_ref[0:4] = near_ref[...]
    total_ref[...] = jnp.zeros_like(total_ref)
    for t in range(TILES):
        slot = slot_of(slot_ref, x, t // 8, t % 8)
        row = lax.shift_right_logical(slot, 3)
        col = cols_ref[row, lax.bitwise_and(slot, 7)]
        total_ref[row] += product_ref[col, SLAB * t:SLAB * (t + 1)]
    firsts = []
    for r in range(SIDE):
        whole = got_ref[SIDE * r + q].astype(F32)
        line_ref[...] = whole
        high = line_ref[pl.ds(pl.multiple_of(x * SLAB, 8), SLAB), :]
        row = whole[120:121] + (whole[121:122] + whole[122:123])
        firsts.append(GAIN * (high + whole[SHARE:120] - column_of(row, x * SLAB, SLAB) * total_ref[r]))
    first = jnp.concatenate(firsts, axis=0)
    high = first.astype(BF16)
    low = first - high.astype(F32)
    for r in range(SIDE):
        tail = low[SLAB * r:SLAB * (r + 1)].astype(BF16)
        for s in range(SIDE):
            wide_ref[SIDE * r + s, 0:SHARE] = high
            wide_ref[SIDE * r + s, SHARE:120] = tail


def home_product(cols_ref, parts, ext_ref, line_ref):
    x, _ = place()
    total = jnp.zeros((SHARE, NRHS), F32)
    for k in range(8):
        left = jnp.concatenate([part[k] for part in parts], axis=0)
        total += jnp.dot(left, ext_ref[cols_ref[x, k]], preferred_element_type=F32)
    for k in range(SIDE):
        line_ref[pl.ds(pl.multiple_of(wrap(x - k) * SLAB, 8), SLAB), :] = total[SLAB * k:SLAB * (k + 1)]
    return line_ref[0:SHARE]


def fill(ext_ref, own_ref, low_ref, high_ref):
    ext_ref[0:4] = own_ref[...]
    ext_ref[4:6] = low_ref[...]
    ext_ref[6:8] = high_ref[...]


def second_kernel(cols_ref, *refs):
    parts = refs[:4]
    got_ref, own_ref, low_ref, high_ref, start_ref, scale_ref, wide_ref, sum_ref, ext_ref, line_ref = refs[4:]
    fill(ext_ref, own_ref, low_ref, high_ref)
    total = home_product(cols_ref, parts, ext_ref, line_ref)
    row, q = place()
    firsts = []
    for x in range(SIDE):
        line_ref[0:120] = got_ref[SIDE * x + q].astype(F32)
        firsts.append(line_ref[pl.ds(pl.multiple_of(row * SLAB, 8), SLAB), :] + line_ref[SHARE:120])
    first = jnp.concatenate(firsts, axis=0)
    second = start_ref[...] - first - scale_ref[...] * total
    sum_ref[...] = first + GAIN * second
    second = second.astype(BF16)
    for m in range(GROUP):
        wide_ref[m] = second


def last_kernel(cols_ref, *refs):
    parts = refs[:4]
    own_ref, low_ref, high_ref, sum_ref, scale_ref, out_ref, ext_ref, line_ref = refs[4:]
    fill(ext_ref, own_ref, low_ref, high_ref)
    total = home_product(cols_ref, parts, ext_ref, line_ref)
    out_ref[...] = sum_ref[...] - GAIN * (scale_ref[...] * total)


def arr(shape, dtype):
    return pltpu.VMEM(shape, dtype)


def call(kernel, args, outs, scalars=0, scratch=(), far=0):
    vectors = args[scalars:]
    space = pltpu.HBM if far else pltpu.VMEM
    vectors = [pltpu.with_memory_space_constraint(a, space) for a in vectors]
    specs = [SMEM] * scalars + [pl.BlockSpec(memory_space=space)] * len(vectors)
    return pl.pallas_call(kernel, in_specs=specs, out_specs=[VMEM] * len(outs),
                          out_shape=outs, scratch_shapes=list(scratch),
                          compiler_params=pltpu.CompilerParams(vmem_limit_bytes=GRANT))(*args[:scalars], *vectors)


def near(*arrays):
    return list(arrays)


HALVES = [arr((2, TILE, NRHS), BF16), arr((2, TILE, NRHS), BF16)]
OWN = arr((SIDE, TILE, NRHS), BF16)
ROWS = arr((SHARE, NRHS), F32)
EXT = arr((8, TILE, NRHS), BF16)
LINE = arr((128, NRHS), F32)


def body(matrix_tiles, tile_slot, tile_cols, send_rows, residual, diag_inv):
    leads = lax.axis_size("lead")
    rows = send_rows.transpose(1, 2, 0)
    diag = diag_inv.reshape(1, SHARE)

    def halo(up, down):
        return (lax.ppermute(up, "lead", [(i, (i + 1) % leads) for i in range(leads)]),
                lax.ppermute(down, "lead", [(i, (i - 1) % leads) for i in range(leads)]))

    def gather(wide):
        return lax.all_to_all(pltpu.with_memory_space_constraint(wide, pltpu.VMEM), "grp", 0, 0)

    def along_x(value, k):
        return lax.ppermute(value, "grp", [(m, (m + SIDE * k) % GROUP) for m in range(GROUP)])

    def along_y(value, k):
        return lax.ppermute(value, "grp", [(m, m - m % SIDE + (m + k) % SIDE) for m in range(GROUP)])

    *quarters, wide, start, scale = call(
        start_kernel, [matrix_tiles, residual, diag],
        [arr((2, SHARE, TILE), BF16)] * 4 + [arr((GROUP, 128, NRHS), BF16), ROWS, ROWS],
        scratch=(ROWS, arr((1, SHARE), F32), pltpu.SemaphoreType.DMA((6,))), far=1)
    for k in range(1, SIDE):
        quarters[k] = along_y(quarters[k], k)
    got = gather(wide)
    slabs = list(call(split_kernel, near(*quarters), [arr((SIDE, 2 * SLAB, TILE), BF16)] * 4, 0,
                 (arr((SIDE, SIDE, 2 * SLAB, TILE), BF16),)))
    for k in range(1, SIDE):
        slabs[k] = along_x(slabs[k], k)
    own, up, down = call(pick_home_kernel, [rows] + near(got), [OWN] + HALVES, 1)
    lower, upper = halo(up, down)
    product, = call(near_kernel, near(*slabs, own), [arr((4, TILES * SLAB, NRHS), F32)])
    wide, = call(first_kernel, [tile_slot, tile_cols] + near(*slabs, got, product, lower, upper),
                 [arr((GROUP, 120, NRHS), BF16)], 2,
                 (arr((8, TILES * SLAB, NRHS), F32), arr((SIDE, SLAB, NRHS), F32), LINE))
    got = gather(wide)
    ordered = call(order_kernel, [tile_slot] + near(*slabs), [arr((8, SLAB, TILE), BF16)] * 4, 1,
                   (arr((TILES, SLAB, TILE), BF16),))
    parts = [ordered[0]]
    for k in range(1, SIDE):
        parts.append(along_x(ordered[k], k))
    own, up, down = call(pick_slab_kernel, [rows] + near(got), [OWN] + HALVES, 1)
    lower, upper = halo(up, down)
    wide, partial = call(second_kernel,
                         [tile_cols] + near(*parts, got, own, lower, upper, start, scale),
                         [arr((GROUP, SHARE, NRHS), BF16), ROWS], 1, (EXT, LINE))
    got = gather(wide)
    own, up, down = call(pick_home_kernel, [rows] + near(got), [OWN] + HALVES, 1)
    lower, upper = halo(up, down)
    result, = call(last_kernel, [tile_cols] + near(*parts, own, lower, upper, partial, scale),
                   [jax.ShapeDtypeStruct((SHARE, NRHS), F32)], 1, (EXT, LINE))
    return result


def solution(mesh):
    in_specs = (
        P(("lead", "grp"), None, None),
        P("lead", None),
        P("lead", None),
        P(),
        P(("lead", "grp"), None),
        P(("lead", "grp")),
    )
    out_specs = P(("lead", "grp"), None)
    return jax.shard_map(body, mesh=mesh, in_specs=in_specs, out_specs=out_specs, check_vma=False)
```

```python
import jax
import jax.numpy as jnp
from jax import lax
from jax.experimental import pallas as pl
from jax.experimental.pallas import tpu as pltpu
from jax.sharding import PartitionSpec as P


TILE = 384
NRHS = 128
SIDE = 4
GROUP = 16
SHARE = 96
SLAB = 24
TILES = 32
PIECE = 216
F32 = jnp.float32
BF16 = jnp.bfloat16
GRANT = 20 << 20
GAIN = 8.0 / 7.0

VMEM = pl.BlockSpec(memory_space=pltpu.VMEM)
SMEM = pl.BlockSpec(memory_space=pltpu.SMEM)


def place():
    member = lax.axis_index("grp")
    return lax.shift_right_logical(member, 2), lax.bitwise_and(member, 3)


def wrap(index):
    return lax.bitwise_and(index, 3)


def column_of(row, first, count):
    line = lax.broadcasted_iota(jnp.int32, (count, 128), 0) + first
    lane = lax.broadcasted_iota(jnp.int32, (count, 128), 1)
    return jnp.sum(jnp.where(line == lane, jnp.broadcast_to(row, (count, 128)), 0.0), axis=1, keepdims=True)


def padded(diag_ref):
    return jnp.concatenate([diag_ref[...], jnp.zeros((1, 128 - SHARE), F32)], axis=1)


def start_kernel(tiles_hbm, residual_hbm, diag_hbm, part0, part1, part2, part3, wide_ref, start_ref, scale_ref,
                 line_ref, residual_ref, diag_ref, sems):
    _, q = place()
    copies = [pltpu.make_async_copy(residual_hbm, residual_ref, sems.at[0]),
              pltpu.make_async_copy(diag_hbm, diag_ref, sems.at[1])]
    for k, part in enumerate((part0, part1, part2, part3)):
        at = pl.multiple_of(wrap(q + k) * SHARE, SHARE)
        copies.append(pltpu.make_async_copy(tiles_hbm.at[:, pl.ds(at, SHARE)], part, sems.at[2 + k]))
    for copy in copies:
        copy.start()
    for copy in copies[:2]:
        copy.wait()
    row = padded(diag_ref)
    d_high = row.astype(BF16).astype(F32)
    d_mid = (row - d_high).astype(BF16).astype(F32)
    line_ref[...] = jnp.broadcast_to(jnp.concatenate([d_high, d_mid, row - d_high - d_mid], axis=1), (8, TILE))
    scale = jnp.broadcast_to(column_of(row, 0, SHARE), (SHARE, NRHS))
    scaled = residual_ref[...] * scale
    scale_ref[...] = scale
    start_ref[...] = scaled
    spread(scaled, wide_ref)
    for copy in copies[2:]:
        copy.wait()


def spread(value, wide_ref):
    value = value.astype(BF16)
    for m in range(GROUP):
        wide_ref[m] = value


def thirds(rows):
    return jnp.concatenate([rows[8 * k:8 * k + 8] for k in range(3)], axis=1)


def unthirds(rows):
    return jnp.concatenate([rows[:, NRHS * k:NRHS * (k + 1)] for k in range(3)], axis=0)


def split_kernel(*refs):
    parts, (start_ref, line_ref), outs, held_ref = refs[:4], refs[4:6], refs[6:10], refs[10]
    x, q = place()
    high = start_ref[...].astype(BF16).astype(F32)
    low = start_ref[...] - high
    for s in range(SIDE):
        at = slice(SLAB * s, SLAB * (s + 1))
        tail = jnp.concatenate([thirds(high[at]), thirds(low[at]), line_ref[...]], axis=0)
        held_ref[wrap(s - x), 192:PIECE] = tail.astype(BF16)
    for k in range(SIDE):
        tiles = [parts[k][j].astype(F32) for j in range(2)]
        to = pl.multiple_of(48 * wrap(q - k), 48)
        for s in range(SIDE):
            pair = jnp.concatenate([tile[SLAB * s:SLAB * (s + 1)] for tile in tiles], axis=0)
            held_ref[wrap(s - x), pl.ds(to, 48)] = pair.astype(BF16)
    for k in range(SIDE):
        outs[k][...] = held_ref[k]


def send_halves(rows_ref, own_ref, up_ref, down_ref):
    lead = lax.axis_index("lead")
    for side, ref in ((0, up_ref), (1, down_ref)):
        for h in range(2):
            ref[h] = own_ref[rows_ref[side, h, lead]]


def pick_slab_kernel(rows_ref, got_ref, own_ref, up_ref, down_ref):
    for q in range(SIDE):
        parts = [got_ref[SIDE * x + q].astype(F32) for x in range(SIDE)]
        for r in range(SIDE):
            block = jnp.concatenate([p[SLAB * r:SLAB * (r + 1)] for p in parts], axis=0)
            own_ref[r, SHARE * q:SHARE * (q + 1)] = block.astype(BF16)
    send_halves(rows_ref, own_ref, up_ref, down_ref)


def pick_home_kernel(rows_ref, got_ref, own_ref, up_ref, down_ref):
    for r in range(SIDE):
        for q in range(SIDE):
            own_ref[r, SHARE * q:SHARE * (q + 1)] = got_ref[SIDE * r + q]
    send_halves(rows_ref, own_ref, up_ref, down_ref)


def slot_of(slot_ref, x, k, i):
    return slot_ref[0, 8 * wrap(x - k) + i]


def order_kernel(slot_ref, *refs):
    parts, outs, held_ref = refs[:4], refs[4:8], refs[8]
    x, _ = place()
    for k in range(SIDE):
        for y in range(SIDE):
            pair = parts[k][48 * y:48 * (y + 1)].astype(F32)
            for j in range(2):
                to = lax.bitwise_and(slot_of(slot_ref, x, k, 2 * y + j) - 8 * x, TILES - 1)
                held_ref[to] = pair[SLAB * j:SLAB * (j + 1)].astype(BF16)
    for k in range(SIDE):
        outs[k][...] = held_ref[8 * k:8 * k + 8]


def slab_products(slabs, blocks, product_ref, first):
    for pair in range(len(blocks) // 2):
        wide = jnp.concatenate(blocks[2 * pair:2 * pair + 2], axis=1)
        product = jnp.dot(slabs, wide, preferred_element_type=F32)
        product_ref[first + 2 * pair] = product[:, :NRHS]
        product_ref[first + 2 * pair + 1] = product[:, NRHS:]


def all_slabs(parts):
    return jnp.concatenate([part[0:192] for part in parts], axis=0)


def near_kernel(*refs):
    own_ref, product_ref = refs[4:]
    slab_products(all_slabs(refs[:4]), [own_ref[r] for r in range(SIDE)], product_ref, 0)


def slab_total(slot_ref, cols_ref, parts, near_ref, low_ref, high_ref, product_ref, total_ref):
    x, _ = place()
    slab_products(all_slabs(parts), [low_ref[0], low_ref[1], high_ref[0], high_ref[1]], product_ref, 4)
    product_ref[0:4] = near_ref[...]
    total_ref[...] = jnp.zeros_like(total_ref)
    for t in range(TILES):
        slot = slot_of(slot_ref, x, t // 8, t % 8)
        row = lax.shift_right_logical(slot, 3)
        col = cols_ref[row, lax.bitwise_and(slot, 7)]
        total_ref[row] += product_ref[col, SLAB * t:SLAB * (t + 1)]


def first_kernel(slot_ref, cols_ref, *refs):
    parts, halo, (wide_ref, first_ref, start_ref, scale_ref), work = refs[:4], refs[4:7], refs[7:11], refs[11:]
    slab_total(slot_ref, cols_ref, parts, *halo, *work)
    total_ref = work[1]
    x, _ = place()
    for k in range(SIDE):
        tail = parts[k][192:PIECE].astype(F32)
        row = tail[16:17, 0:128] + (tail[16:17, 128:256] + tail[16:17, 256:384])
        start = unthirds(tail[0:8]) + unthirds(tail[8:16])
        scale = jnp.broadcast_to(column_of(row, x * SLAB, SLAB), (SLAB, NRHS))
        r = wrap(x - k)
        start_ref[r] = start
        scale_ref[r] = scale
        first_ref[r] = GAIN * (start - scale * total_ref[r])
    spread(jnp.concatenate([first_ref[r] for r in range(SIDE)], axis=0), wide_ref)


def second_kernel(slot_ref, cols_ref, *refs):
    parts, halo, (first_ref, start_ref, scale_ref) = refs[:4], refs[4:7], refs[7:10]
    wide_ref, outs, work = refs[10], refs[11:15], refs[15:]
    slab_total(slot_ref, cols_ref, parts, *halo, *work)
    x, _ = place()
    seconds = []
    total_ref = work[1]
    for r in range(SIDE):
        second = start_ref[r] - first_ref[r] - scale_ref[r] * total_ref[r]
        seconds.append(second)
        total_ref[r] = first_ref[r] + GAIN * second
    spread(jnp.concatenate(seconds, axis=0), wide_ref)
    for k in range(SIDE):
        outs[k][...] = total_ref[wrap(x + k)]


def last_kernel(cols_ref, *refs):
    parts, sums, (own_ref, low_ref, high_ref, scale_ref, out_ref, ext_ref) = refs[:4], refs[4:8], refs[8:]
    x, _ = place()
    ext_ref[0:4] = own_ref[...]
    ext_ref[4:6] = low_ref[...]
    ext_ref[6:8] = high_ref[...]
    total = jnp.zeros((SHARE, NRHS), F32)
    for k in range(8):
        left = jnp.concatenate([part[k] for part in parts], axis=0)
        total += jnp.dot(left, ext_ref[cols_ref[x, k]], preferred_element_type=F32)
    for k in range(SIDE):
        at = pl.ds(pl.multiple_of(wrap(x - k) * SLAB, 8), SLAB)
        out_ref[at, :] = sums[k][...] - GAIN * (scale_ref[at, :] * total[SLAB * k:SLAB * (k + 1)])


def arr(shape, dtype):
    return pltpu.VMEM(shape, dtype)


def call(kernel, args, outs, scalars=0, scratch=(), far=0):
    vectors = args[scalars:]
    space = pltpu.HBM if far else pltpu.VMEM
    vectors = [pltpu.with_memory_space_constraint(a, space) for a in vectors]
    specs = [SMEM] * scalars + [pl.BlockSpec(memory_space=space)] * len(vectors)
    return pl.pallas_call(kernel, in_specs=specs, out_specs=[VMEM] * len(outs),
                          out_shape=outs, scratch_shapes=list(scratch),
                          compiler_params=pltpu.CompilerParams(vmem_limit_bytes=GRANT))(*args[:scalars], *vectors)


def near(*arrays):
    return list(arrays)


HALVES = [arr((2, TILE, NRHS), BF16), arr((2, TILE, NRHS), BF16)]
OWN = arr((SIDE, TILE, NRHS), BF16)
ROWS = arr((SHARE, NRHS), F32)
EXT = arr((8, TILE, NRHS), BF16)
SLABS = arr((SIDE, SLAB, NRHS), F32)
WIDE = arr((GROUP, SHARE, NRHS), BF16)
NEAR = arr((4, TILES * SLAB, NRHS), F32)
WORK = (arr((8, TILES * SLAB, NRHS), F32), SLABS)


def body(matrix_tiles, tile_slot, tile_cols, send_rows, residual, diag_inv):
    leads = lax.axis_size("lead")
    rows = send_rows.transpose(1, 2, 0)
    diag = diag_inv.reshape(1, SHARE)

    def halo(up, down):
        lower = lax.ppermute(up, "lead", [(i, (i + 1) % leads) for i in range(leads)])
        upper = lax.ppermute(down, "lead", [(i, (i - 1) % leads) for i in range(leads)])
        return lower, upper

    def gather(wide):
        return lax.all_to_all(wide, "grp", 0, 0)

    def choose(kernel, got):
        return call(kernel, [rows] + near(got), [OWN] + HALVES, 1)

    def along_x(values):
        pairs = [[(m, (m + SIDE * k) % GROUP) for m in range(GROUP)] for k in range(SIDE)]
        return exchange(values, pairs)

    def along_y(values):
        pairs = [[(m, m - m % SIDE + (m + k) % SIDE) for m in range(GROUP)] for k in range(SIDE)]
        return exchange(values, pairs)

    def exchange(values, pairs):
        out = [values[0]]
        for k in range(1, SIDE):
            out.append(lax.ppermute(values[k], "grp", pairs[k]))
        return out

    *quarters, wide, start, scale, line = call(
        start_kernel, [matrix_tiles, residual, diag],
        [arr((2, SHARE, TILE), BF16)] * 4 + [WIDE, ROWS, ROWS, arr((8, TILE), F32)],
        scratch=(ROWS, arr((1, SHARE), F32), pltpu.SemaphoreType.DMA((6,))), far=1)
    quarters = along_y(quarters)
    got = gather(wide)
    slabs = call(split_kernel, near(*quarters, start, line), [arr((PIECE, TILE), BF16)] * 4, 0,
                 (arr((SIDE, PIECE, TILE), BF16),))
    slabs = along_x(slabs)
    own, up, down = choose(pick_home_kernel, got)
    halos = halo(up, down)
    ordered = call(order_kernel, [tile_slot] + near(*slabs), [arr((8, SLAB, TILE), BF16)] * 4, 1,
                   (arr((TILES, SLAB, TILE), BF16),))
    product, = call(near_kernel, near(*slabs, own), [NEAR])
    wide, *state = call(first_kernel, [tile_slot, tile_cols] + near(*slabs, product, *halos),
                        [WIDE] + [SLABS] * 3, 2, WORK)
    own, up, down = choose(pick_slab_kernel, gather(wide))
    halos = halo(up, down)
    parts = along_x(ordered)
    product, = call(near_kernel, near(*slabs, own), [NEAR])
    wide, *sums = call(second_kernel, [tile_slot, tile_cols] + near(*slabs, product, *halos, *state),
                       [WIDE] + [arr((SLAB, NRHS), F32)] * 4, 2, WORK)
    own, up, down = choose(pick_slab_kernel, gather(wide))
    halos = halo(up, down)
    sums = along_x(sums)
    result, = call(last_kernel, [tile_cols] + near(*parts, *sums, own, *halos, scale),
                   [jax.ShapeDtypeStruct((SHARE, NRHS), F32)], 1, (EXT,))
    return result


def solution(mesh):
    in_specs = (
        P(("lead", "grp"), None, None),
        P("lead", None),
        P("lead", None),
        P(),
        P(("lead", "grp"), None),
        P(("lead", "grp")),
    )
    out_specs = P(("lead", "grp"), None)
    return jax.shard_map(body, mesh=mesh, in_specs=in_specs, out_specs=out_specs, check_vma=False)
```

```python
import jax
import jax.numpy as jnp
from jax import lax
from jax.experimental import pallas as pl
from jax.experimental.pallas import tpu as pltpu
from jax.sharding import PartitionSpec as P


TILE = 384
NRHS = 128
SIDE = 4
GROUP = 16
SHARE = 96
SLAB = 24
TILES = 32
PIECE = 216
F32 = jnp.float32
BF16 = jnp.bfloat16
GRANT = 20 << 20
GAIN = 8.0 / 7.0

VMEM = pl.BlockSpec(memory_space=pltpu.VMEM)
SMEM = pl.BlockSpec(memory_space=pltpu.SMEM)


def place():
    member = lax.axis_index("grp")
    return lax.shift_right_logical(member, 2), lax.bitwise_and(member, 3)


def wrap(index):
    return lax.bitwise_and(index, 3)


def column_of(row, first, count):
    line = lax.broadcasted_iota(jnp.int32, (count, 128), 0) + first
    lane = lax.broadcasted_iota(jnp.int32, (count, 128), 1)
    return jnp.sum(jnp.where(line == lane, jnp.broadcast_to(row, (count, 128)), 0.0), axis=1, keepdims=True)


def padded(diag_ref):
    return jnp.concatenate([diag_ref[...], jnp.zeros((1, 128 - SHARE), F32)], axis=1)


def start_kernel(tiles_hbm, residual_hbm, diag_hbm, part0, part1, part2, part3, wide_ref, start_ref, scale_ref,
                 line_ref, residual_ref, diag_ref, sems):
    _, q = place()
    copies = [pltpu.make_async_copy(residual_hbm, residual_ref, sems.at[0]),
              pltpu.make_async_copy(diag_hbm, diag_ref, sems.at[1])]
    for k, part in enumerate((part0, part1, part2, part3)):
        at = pl.multiple_of(wrap(q + k) * SHARE, SHARE)
        copies.append(pltpu.make_async_copy(tiles_hbm.at[:, pl.ds(at, SHARE)], part, sems.at[2 + k]))
    for copy in copies:
        copy.start()
    for copy in copies[:2]:
        copy.wait()
    row = padded(diag_ref)
    d_high = row.astype(BF16).astype(F32)
    d_mid = (row - d_high).astype(BF16).astype(F32)
    line_ref[...] = jnp.broadcast_to(jnp.concatenate([d_high, d_mid, row - d_high - d_mid], axis=1), (8, TILE))
    scale = jnp.broadcast_to(column_of(row, 0, SHARE), (SHARE, NRHS))
    scaled = residual_ref[...] * scale
    scale_ref[...] = scale
    start_ref[...] = scaled
    spread(scaled, wide_ref)
    for copy in copies[2:]:
        copy.wait()


def spread(value, wide_ref):
    value = value.astype(BF16)
    for m in range(GROUP):
        wide_ref[m] = value


def thirds(rows):
    return jnp.concatenate([rows[8 * k:8 * k + 8] for k in range(3)], axis=1)


def unthirds(rows):
    return jnp.concatenate([rows[:, NRHS * k:NRHS * (k + 1)] for k in range(3)], axis=0)


def split_kernel(*refs):
    parts, (start_ref, line_ref), outs, held_ref = refs[:4], refs[4:6], refs[6:10], refs[10]
    x, q = place()
    high = start_ref[...].astype(BF16).astype(F32)
    low = start_ref[...] - high
    for s in range(SIDE):
        at = slice(SLAB * s, SLAB * (s + 1))
        tail = jnp.concatenate([thirds(high[at]), thirds(low[at]), line_ref[...]], axis=0)
        held_ref[wrap(s - x), 192:PIECE] = tail.astype(BF16)
    for k in range(SIDE):
        tiles = [parts[k][j].astype(F32) for j in range(2)]
        to = pl.multiple_of(48 * wrap(q - k), 48)
        for s in range(SIDE):
            pair = jnp.concatenate([tile[SLAB * s:SLAB * (s + 1)] for tile in tiles], axis=0)
            held_ref[wrap(s - x), pl.ds(to, 48)] = pair.astype(BF16)
    for k in range(SIDE):
        outs[k][...] = held_ref[k]


def table_kernel(slot_ref, cols_ref, rows_ref, slot_out, cols_out, rows_out):
    for t in range(TILES):
        slot_out[0, t] = slot_ref[0, t]
    for r in range(SIDE):
        for k in range(8):
            cols_out[r, k] = cols_ref[r, k]
    lead = lax.axis_index("lead")
    for side in range(2):
        for h in range(2):
            rows_out[side, h] = rows_ref[side, h, lead]


def send_halves(rows_ref, own_ref, up_ref, down_ref):
    for side, ref in ((0, up_ref), (1, down_ref)):
        for h in range(2):
            ref[h] = own_ref[rows_ref[side, h]]


def pick_slab_kernel(rows_ref, got_ref, own_ref, up_ref, down_ref):
    for q in range(SIDE):
        parts = [got_ref[SIDE * x + q].astype(F32) for x in range(SIDE)]
        for r in range(SIDE):
            block = jnp.concatenate([p[SLAB * r:SLAB * (r + 1)] for p in parts], axis=0)
            own_ref[r, SHARE * q:SHARE * (q + 1)] = block.astype(BF16)
    send_halves(rows_ref, own_ref, up_ref, down_ref)


def pick_home_kernel(rows_ref, got_ref, own_ref, up_ref, down_ref):
    for r in range(SIDE):
        for q in range(SIDE):
            own_ref[r, SHARE * q:SHARE * (q + 1)] = got_ref[SIDE * r + q]
    send_halves(rows_ref, own_ref, up_ref, down_ref)


def slot_of(slot_ref, x, k, i):
    return slot_ref[0, 8 * wrap(x - k) + i]


def order_kernel(slot_ref, *refs):
    parts, outs, held_ref = refs[:4], refs[4:8], refs[8]
    x, _ = place()
    for k in range(SIDE):
        for y in range(SIDE):
            pair = parts[k][48 * y:48 * (y + 1)].astype(F32)
            for j in range(2):
                to = lax.bitwise_and(slot_of(slot_ref, x, k, 2 * y + j) - 8 * x, TILES - 1)
                held_ref[to] = pair[SLAB * j:SLAB * (j + 1)].astype(BF16)
    for k in range(SIDE):
        outs[k][...] = held_ref[8 * k:8 * k + 8]


def slab_products(slabs, blocks, product_ref, first):
    for pair in range(len(blocks) // 2):
        wide = jnp.concatenate(blocks[2 * pair:2 * pair + 2], axis=1)
        product = jnp.dot(slabs, wide, preferred_element_type=F32)
        product_ref[first + 2 * pair] = product[:, :NRHS]
        product_ref[first + 2 * pair + 1] = product[:, NRHS:]


def all_slabs(parts):
    return jnp.concatenate([part[0:192] for part in parts], axis=0)


def near_kernel(*refs):
    own_ref, product_ref = refs[4:]
    slab_products(all_slabs(refs[:4]), [own_ref[r] for r in range(SIDE)], product_ref, 0)


def slab_total(slot_ref, cols_ref, parts, near_ref, low_ref, high_ref, product_ref, total_ref):
    x, _ = place()
    slab_products(all_slabs(parts), [low_ref[0], low_ref[1], high_ref[0], high_ref[1]], product_ref, 4)
    product_ref[0:4] = near_ref[...]
    total_ref[...] = jnp.zeros_like(total_ref)
    for t in range(TILES):
        slot = slot_of(slot_ref, x, t // 8, t % 8)
        row = lax.shift_right_logical(slot, 3)
        col = cols_ref[row, lax.bitwise_and(slot, 7)]
        total_ref[row] += product_ref[col, SLAB * t:SLAB * (t + 1)]


def first_kernel(slot_ref, cols_ref, *refs):
    parts, halo, (wide_ref, first_ref, start_ref, scale_ref), work = refs[:4], refs[4:7], refs[7:11], refs[11:]
    slab_total(slot_ref, cols_ref, parts, *halo, *work)
    total_ref = work[1]
    x, _ = place()
    for k in range(SIDE):
        tail = parts[k][192:PIECE].astype(F32)
        row = tail[16:17, 0:128] + (tail[16:17, 128:256] + tail[16:17, 256:384])
        start = unthirds(tail[0:8]) + unthirds(tail[8:16])
        scale = jnp.broadcast_to(column_of(row, x * SLAB, SLAB), (SLAB, NRHS))
        r = wrap(x - k)
        start_ref[r] = start
        scale_ref[r] = scale
        first_ref[r] = GAIN * (start - scale * total_ref[r])
    spread(jnp.concatenate([first_ref[r] for r in range(SIDE)], axis=0), wide_ref)


def second_kernel(slot_ref, cols_ref, *refs):
    parts, halo, (first_ref, start_ref, scale_ref) = refs[:4], refs[4:7], refs[7:10]
    wide_ref, outs, work = refs[10], refs[11:15], refs[15:]
    slab_total(slot_ref, cols_ref, parts, *halo, *work)
    x, _ = place()
    seconds = []
    total_ref = work[1]
    for r in range(SIDE):
        second = start_ref[r] - first_ref[r] - scale_ref[r] * total_ref[r]
        seconds.append(second)
        total_ref[r] = first_ref[r] + GAIN * second
    spread(jnp.concatenate(seconds, axis=0), wide_ref)
    for k in range(SIDE):
        outs[k][...] = total_ref[wrap(x + k)]


def last_kernel(cols_ref, *refs):
    parts, sums, (own_ref, low_ref, high_ref, scale_ref, out_ref, ext_ref) = refs[:4], refs[4:8], refs[8:]
    x, _ = place()
    ext_ref[0:4] = own_ref[...]
    ext_ref[4:6] = low_ref[...]
    ext_ref[6:8] = high_ref[...]
    total = jnp.zeros((SHARE, NRHS), F32)
    for k in range(8):
        left = jnp.concatenate([part[k] for part in parts], axis=0)
        total += jnp.dot(left, ext_ref[cols_ref[x, k]], preferred_element_type=F32)
    for k in range(SIDE):
        at = pl.ds(pl.multiple_of(wrap(x - k) * SLAB, 8), SLAB)
        out_ref[at, :] = sums[k][...] - GAIN * (scale_ref[at, :] * total[SLAB * k:SLAB * (k + 1)])


def arr(shape, dtype):
    return pltpu.VMEM(shape, dtype)


def call(kernel, args, outs, scalars=0, scratch=(), far=0):
    vectors = args[scalars:]
    space = pltpu.HBM if far else pltpu.VMEM
    vectors = [pltpu.with_memory_space_constraint(a, space) for a in vectors]
    specs = [SMEM] * scalars + [pl.BlockSpec(memory_space=space)] * len(vectors)
    tables = [pltpu.with_memory_space_constraint(a, pltpu.SMEM) for a in args[:scalars]]
    return pl.pallas_call(kernel, in_specs=specs, out_specs=[VMEM] * len(outs),
                          out_shape=outs, scratch_shapes=list(scratch),
                          compiler_params=pltpu.CompilerParams(vmem_limit_bytes=GRANT))(*tables, *vectors)


def near(*arrays):
    return list(arrays)


HALVES = [arr((2, TILE, NRHS), BF16), arr((2, TILE, NRHS), BF16)]
OWN = arr((SIDE, TILE, NRHS), BF16)
ROWS = arr((SHARE, NRHS), F32)
EXT = arr((8, TILE, NRHS), BF16)
SLABS = arr((SIDE, SLAB, NRHS), F32)
WIDE = arr((GROUP, SHARE, NRHS), BF16)
NEAR = arr((4, TILES * SLAB, NRHS), F32)
WORK = (arr((8, TILES * SLAB, NRHS), F32), SLABS)


def body(matrix_tiles, tile_slot, tile_cols, send_rows, residual, diag_inv):
    leads = lax.axis_size("lead")
    rows = send_rows.transpose(1, 2, 0)
    diag = diag_inv.reshape(1, SHARE)

    def halo(up, down):
        lower = lax.ppermute(up, "lead", [(i, (i + 1) % leads) for i in range(leads)])
        upper = lax.ppermute(down, "lead", [(i, (i - 1) % leads) for i in range(leads)])
        return lower, upper

    def gather(wide):
        return lax.all_to_all(wide, "grp", 0, 0)

    def choose(kernel, got):
        return call(kernel, [rows] + near(got), [OWN] + HALVES, 1)

    def along_x(values):
        pairs = [[(m, (m + SIDE * k) % GROUP) for m in range(GROUP)] for k in range(SIDE)]
        return exchange(values, pairs)

    def along_y(values):
        pairs = [[(m, m - m % SIDE + (m + k) % SIDE) for m in range(GROUP)] for k in range(SIDE)]
        return exchange(values, pairs)

    def exchange(values, pairs):
        out = [values[0]]
        for k in range(1, SIDE):
            out.append(lax.ppermute(values[k], "grp", pairs[k]))
        return out

    *quarters, wide, start, scale, line = call(
        start_kernel, [matrix_tiles, residual, diag],
        [arr((2, SHARE, TILE), BF16)] * 4 + [WIDE, ROWS, ROWS, arr((8, TILE), F32)],
        scratch=(ROWS, arr((1, SHARE), F32), pltpu.SemaphoreType.DMA((6,))), far=1)
    tables = [pltpu.SMEM((1, TILES), jnp.int32), pltpu.SMEM((SIDE, 8), jnp.int32), pltpu.SMEM((2, 2), jnp.int32)]
    tile_slot, tile_cols, rows = pl.pallas_call(
        table_kernel, name="tables", in_specs=[SMEM] * 3, out_specs=[SMEM] * 3, out_shape=tables)(
        tile_slot, tile_cols, rows)
    quarters = along_y(quarters)
    got = gather(wide)
    slabs = call(split_kernel, near(*quarters, start, line), [arr((PIECE, TILE), BF16)] * 4, 0,
                 (arr((SIDE, PIECE, TILE), BF16),))
    slabs = along_x(slabs)
    own, up, down = choose(pick_home_kernel, got)
    halos = halo(up, down)
    ordered = call(order_kernel, [tile_slot] + near(*slabs), [arr((8, SLAB, TILE), BF16)] * 4, 1,
                   (arr((TILES, SLAB, TILE), BF16),))
    product, = call(near_kernel, near(*slabs, own), [NEAR])
    wide, *state = call(first_kernel, [tile_slot, tile_cols] + near(*slabs, product, *halos),
                        [WIDE] + [SLABS] * 3, 2, WORK)
    own, up, down = choose(pick_slab_kernel, gather(wide))
    halos = halo(up, down)
    parts = along_x(ordered)
    product, = call(near_kernel, near(*slabs, own), [NEAR])
    wide, *sums = call(second_kernel, [tile_slot, tile_cols] + near(*slabs, product, *halos, *state),
                       [WIDE] + [arr((SLAB, NRHS), F32)] * 4, 2, WORK)
    own, up, down = choose(pick_slab_kernel, gather(wide))
    halos = halo(up, down)
    sums = along_x(sums)
    result, = call(last_kernel, [tile_cols] + near(*parts, *sums, own, *halos, scale),
                   [jax.ShapeDtypeStruct((SHARE, NRHS), F32)], 1, (EXT,))
    return result


def solution(mesh):
    in_specs = (
        P(("lead", "grp"), None, None),
        P("lead", None),
        P("lead", None),
        P(),
        P(("lead", "grp"), None),
        P(("lead", "grp")),
    )
    out_specs = P(("lead", "grp"), None)
    return jax.shard_map(body, mesh=mesh, in_specs=in_specs, out_specs=out_specs, check_vma=False)
```

```python
import jax
import jax.numpy as jnp
from jax import lax
from jax.experimental import pallas as pl
from jax.experimental.pallas import tpu as pltpu
from jax.sharding import PartitionSpec as P


TILE = 384
NRHS = 128
SIDE = 4
GROUP = 16
SHARE = 96
SLAB = 24
TILES = 32
PIECE = 216
F32 = jnp.float32
BF16 = jnp.bfloat16
GRANT = 20 << 20
GAIN = 8.0 / 7.0

VMEM = pl.BlockSpec(memory_space=pltpu.VMEM)
SMEM = pl.BlockSpec(memory_space=pltpu.SMEM)


def place():
    member = lax.axis_index("grp")
    return lax.shift_right_logical(member, 2), lax.bitwise_and(member, 3)


def wrap(index):
    return lax.bitwise_and(index, 3)


def column_of(row, first, count):
    line = lax.broadcasted_iota(jnp.int32, (count, 128), 0) + first
    lane = lax.broadcasted_iota(jnp.int32, (count, 128), 1)
    return jnp.sum(jnp.where(line == lane, jnp.broadcast_to(row, (count, 128)), 0.0), axis=1, keepdims=True)


def padded(diag_ref):
    return jnp.concatenate([diag_ref[...], jnp.zeros((1, 128 - SHARE), F32)], axis=1)


def start_kernel(tiles_hbm, residual_hbm, diag_hbm, part0, part1, part2, part3, wide_ref, start_ref, scale_ref,
                 line_ref, residual_ref, diag_ref, sems):
    _, q = place()
    copies = [pltpu.make_async_copy(residual_hbm, residual_ref, sems.at[0]),
              pltpu.make_async_copy(diag_hbm, diag_ref, sems.at[1])]
    for k, part in enumerate((part0, part1, part2, part3)):
        at = pl.multiple_of(wrap(q + k) * SHARE, SHARE)
        copies.append(pltpu.make_async_copy(tiles_hbm.at[:, pl.ds(at, SHARE)], part, sems.at[2 + k]))
    for copy in copies:
        copy.start()
    for copy in copies[:2]:
        copy.wait()
    row = padded(diag_ref)
    d_high = row.astype(BF16).astype(F32)
    d_mid = (row - d_high).astype(BF16).astype(F32)
    line_ref[...] = jnp.broadcast_to(jnp.concatenate([d_high, d_mid, row - d_high - d_mid], axis=1), (8, TILE))
    scale = jnp.broadcast_to(column_of(row, 0, SHARE), (SHARE, NRHS))
    scaled = residual_ref[...] * scale
    scale_ref[...] = scale
    start_ref[...] = scaled
    spread(scaled, wide_ref)
    for copy in copies[2:]:
        copy.wait()


def spread(value, wide_ref):
    value = value.astype(BF16)
    for m in range(GROUP):
        wide_ref[m] = value


def thirds(rows):
    return jnp.concatenate([rows[8 * k:8 * k + 8] for k in range(3)], axis=1)


def unthirds(rows):
    return jnp.concatenate([rows[:, NRHS * k:NRHS * (k + 1)] for k in range(3)], axis=0)


def split_kernel(*refs):
    parts, (start_ref, line_ref), outs, held_ref = refs[:4], refs[4:6], refs[6:10], refs[10]
    x, q = place()
    high = start_ref[...].astype(BF16).astype(F32)
    low = start_ref[...] - high
    for s in range(SIDE):
        at = slice(SLAB * s, SLAB * (s + 1))
        tail = jnp.concatenate([thirds(high[at]), thirds(low[at]), line_ref[...]], axis=0)
        held_ref[wrap(s - x), 192:PIECE] = tail.astype(BF16)
    for k in range(SIDE):
        tiles = [parts[k][j].astype(F32) for j in range(2)]
        to = pl.multiple_of(48 * wrap(q - k), 48)
        for s in range(SIDE):
            pair = jnp.concatenate([tile[SLAB * s:SLAB * (s + 1)] for tile in tiles], axis=0)
            held_ref[wrap(s - x), pl.ds(to, 48)] = pair.astype(BF16)
    for k in range(SIDE):
        outs[k][...] = held_ref[k]


def table_kernel(slot_ref, cols_ref, rows_ref, slot_out, cols_out, rows_out):
    for t in range(TILES):
        slot_out[0, t] = slot_ref[0, t]
    for r in range(SIDE):
        for k in range(8):
            cols_out[r, k] = cols_ref[r, k]
    lead = lax.axis_index("lead")
    for side in range(2):
        for h in range(2):
            rows_out[side, h] = rows_ref[side, h, lead]


def send_halves(rows_ref, own_ref, up_ref, down_ref):
    for side, ref in ((0, up_ref), (1, down_ref)):
        for h in range(2):
            ref[h] = own_ref[rows_ref[side, h]]


def pick_slab_kernel(rows_ref, got_ref, own_ref, up_ref, down_ref):
    for q in range(SIDE):
        parts = [got_ref[SIDE * x + q, 0:SHARE].astype(F32) for x in range(SIDE)]
        for r in range(SIDE):
            block = jnp.concatenate([p[SLAB * r:SLAB * (r + 1)] for p in parts], axis=0)
            own_ref[r, SHARE * q:SHARE * (q + 1)] = block.astype(BF16)
    send_halves(rows_ref, own_ref, up_ref, down_ref)


def pick_home_kernel(rows_ref, got_ref, own_ref, up_ref, down_ref):
    for r in range(SIDE):
        for q in range(SIDE):
            own_ref[r, SHARE * q:SHARE * (q + 1)] = got_ref[SIDE * r + q]
    send_halves(rows_ref, own_ref, up_ref, down_ref)


def slot_of(slot_ref, x, k, i):
    return slot_ref[0, 8 * wrap(x - k) + i]


def order_kernel(slot_ref, *refs):
    parts, outs, held_ref = refs[:4], refs[4:8], refs[8]
    x, _ = place()
    for k in range(SIDE):
        for y in range(SIDE):
            pair = parts[k][48 * y:48 * (y + 1)].astype(F32)
            for j in range(2):
                to = lax.bitwise_and(slot_of(slot_ref, x, k, 2 * y + j) - 8 * x, TILES - 1)
                held_ref[to] = pair[SLAB * j:SLAB * (j + 1)].astype(BF16)
    for k in range(SIDE):
        outs[k][...] = held_ref[8 * k:8 * k + 8]


def slab_products(slabs, blocks, product_ref, first):
    for pair in range(len(blocks) // 2):
        wide = jnp.concatenate(blocks[2 * pair:2 * pair + 2], axis=1)
        product = jnp.dot(slabs, wide, preferred_element_type=F32)
        product_ref[first + 2 * pair] = product[:, :NRHS]
        product_ref[first + 2 * pair + 1] = product[:, NRHS:]


def all_slabs(parts):
    return jnp.concatenate([part[0:192] for part in parts], axis=0)


def near_kernel(*refs):
    own_ref, product_ref = refs[4:]
    slab_products(all_slabs(refs[:4]), [own_ref[r] for r in range(SIDE)], product_ref, 0)


def slab_total(slot_ref, cols_ref, parts, near_ref, low_ref, high_ref, product_ref, total_ref):
    x, _ = place()
    slab_products(all_slabs(parts), [low_ref[0], low_ref[1], high_ref[0], high_ref[1]], product_ref, 4)
    product_ref[0:4] = near_ref[...]
    total_ref[...] = jnp.zeros_like(total_ref)
    for t in range(TILES):
        slot = slot_of(slot_ref, x, t // 8, t % 8)
        row = lax.shift_right_logical(slot, 3)
        col = cols_ref[row, lax.bitwise_and(slot, 7)]
        total_ref[row] += product_ref[col, SLAB * t:SLAB * (t + 1)]


def first_kernel(slot_ref, cols_ref, *refs):
    parts, halo, (wide_ref, first_ref, start_ref, scale_ref), work = refs[:4], refs[4:7], refs[7:11], refs[11:]
    slab_total(slot_ref, cols_ref, parts, *halo, *work)
    total_ref = work[1]
    x, _ = place()
    for k in range(SIDE):
        tail = parts[k][192:PIECE].astype(F32)
        row = tail[16:17, 0:128] + (tail[16:17, 128:256] + tail[16:17, 256:384])
        start = unthirds(tail[0:8]) + unthirds(tail[8:16])
        scale = jnp.broadcast_to(column_of(row, x * SLAB, SLAB), (SLAB, NRHS))
        r = wrap(x - k)
        start_ref[r] = start
        scale_ref[r] = scale
        first_ref[r] = GAIN * (start - scale * total_ref[r])
    spread(jnp.concatenate([first_ref[r] for r in range(SIDE)], axis=0), wide_ref)


def second_kernel(slot_ref, cols_ref, *refs):
    parts, halo, (first_ref, start_ref, scale_ref) = refs[:4], refs[4:7], refs[7:10]
    wide_ref, work = refs[10], refs[11:]
    slab_total(slot_ref, cols_ref, parts, *halo, *work)
    total_ref = work[1]
    seconds, rests = [], []
    for r in range(SIDE):
        first = first_ref[r]
        second = start_ref[r] - first - scale_ref[r] * total_ref[r]
        seconds.append(second)
        rest = first - first.astype(BF16).astype(F32) + GAIN * (second - second.astype(BF16).astype(F32))
        rests.append(rest.astype(BF16))
    high = jnp.concatenate(seconds, axis=0).astype(BF16)
    for r in range(SIDE):
        for s in range(SIDE):
            wide_ref[SIDE * r + s, 0:SHARE] = high
            wide_ref[SIDE * r + s, SHARE:120] = rests[r]


def last_kernel(cols_ref, *refs):
    parts, halo, (got_ref, first_ref, scale_ref, out_ref, ext_ref, line_ref) = refs[:4], refs[4:7], refs[7:]
    own_ref, low_ref, high_ref = halo
    x, q = place()
    ext_ref[0:4] = own_ref[...]
    ext_ref[4:6] = low_ref[...]
    ext_ref[6:8] = high_ref[...]
    total = jnp.zeros((SHARE, NRHS), F32)
    for k in range(8):
        left = jnp.concatenate([part[k] for part in parts], axis=0)
        total += jnp.dot(left, ext_ref[cols_ref[x, k]], preferred_element_type=F32)
    for k in range(SIDE):
        line_ref[pl.ds(pl.multiple_of(wrap(x - k) * SLAB, 8), SLAB), :] = total[SLAB * k:SLAB * (k + 1)]
    mine = pl.ds(pl.multiple_of(q * SHARE, SHARE), SHARE)
    rest = jnp.concatenate([got_ref[SIDE * s + q, SHARE:120].astype(F32) for s in range(SIDE)], axis=0)
    second = own_ref[x, mine].astype(F32) - scale_ref[...] * line_ref[...]
    out_ref[...] = first_ref[x, mine].astype(F32) + rest + GAIN * second


def arr(shape, dtype):
    return pltpu.VMEM(shape, dtype)


def call(kernel, args, outs, scalars=0, scratch=(), far=0):
    vectors = args[scalars:]
    space = pltpu.HBM if far else pltpu.VMEM
    vectors = [pltpu.with_memory_space_constraint(a, space) for a in vectors]
    specs = [SMEM] * scalars + [pl.BlockSpec(memory_space=space)] * len(vectors)
    tables = [pltpu.with_memory_space_constraint(a, pltpu.SMEM) for a in args[:scalars]]
    return pl.pallas_call(kernel, in_specs=specs, out_specs=[VMEM] * len(outs),
                          out_shape=outs, scratch_shapes=list(scratch),
                          compiler_params=pltpu.CompilerParams(vmem_limit_bytes=GRANT))(*tables, *vectors)


def near(*arrays):
    return list(arrays)


HALVES = [arr((2, TILE, NRHS), BF16), arr((2, TILE, NRHS), BF16)]
OWN = arr((SIDE, TILE, NRHS), BF16)
ROWS = arr((SHARE, NRHS), F32)
EXT = arr((8, TILE, NRHS), BF16)
SLABS = arr((SIDE, SLAB, NRHS), F32)
WIDE = arr((GROUP, SHARE, NRHS), BF16)
NEAR = arr((4, TILES * SLAB, NRHS), F32)
WORK = (arr((8, TILES * SLAB, NRHS), F32), SLABS)


def body(matrix_tiles, tile_slot, tile_cols, send_rows, residual, diag_inv):
    leads = lax.axis_size("lead")
    rows = send_rows.transpose(1, 2, 0)
    diag = diag_inv.reshape(1, SHARE)

    def halo(up, down):
        lower = lax.ppermute(up, "lead", [(i, (i + 1) % leads) for i in range(leads)])
        upper = lax.ppermute(down, "lead", [(i, (i - 1) % leads) for i in range(leads)])
        return lower, upper

    def gather(wide):
        return lax.all_to_all(wide, "grp", 0, 0)

    def choose(kernel, got):
        return call(kernel, [rows] + near(got), [OWN] + HALVES, 1)

    def along_x(values):
        pairs = [[(m, (m + SIDE * k) % GROUP) for m in range(GROUP)] for k in range(SIDE)]
        return exchange(values, pairs)

    def along_y(values):
        pairs = [[(m, m - m % SIDE + (m + k) % SIDE) for m in range(GROUP)] for k in range(SIDE)]
        return exchange(values, pairs)

    def exchange(values, pairs):
        out = [values[0]]
        for k in range(1, SIDE):
            out.append(lax.ppermute(values[k], "grp", pairs[k]))
        return out

    *quarters, wide, start, scale, line = call(
        start_kernel, [matrix_tiles, residual, diag],
        [arr((2, SHARE, TILE), BF16)] * 4 + [WIDE, ROWS, ROWS, arr((8, TILE), F32)],
        scratch=(ROWS, arr((1, SHARE), F32), pltpu.SemaphoreType.DMA((6,))), far=1)
    tables = [pltpu.SMEM((1, TILES), jnp.int32), pltpu.SMEM((SIDE, 8), jnp.int32), pltpu.SMEM((2, 2), jnp.int32)]
    tile_slot, tile_cols, rows = pl.pallas_call(
        table_kernel, name="tables", in_specs=[SMEM] * 3, out_specs=[SMEM] * 3, out_shape=tables)(
        tile_slot, tile_cols, rows)
    quarters = along_y(quarters)
    got = gather(wide)
    slabs = call(split_kernel, near(*quarters, start, line), [arr((PIECE, TILE), BF16)] * 4, 0,
                 (arr((SIDE, PIECE, TILE), BF16),))
    slabs = along_x(slabs)
    own, up, down = choose(pick_home_kernel, got)
    halos = halo(up, down)
    ordered = call(order_kernel, [tile_slot] + near(*slabs), [arr((8, SLAB, TILE), BF16)] * 4, 1,
                   (arr((TILES, SLAB, TILE), BF16),))
    product, = call(near_kernel, near(*slabs, own), [NEAR])
    wide, *state = call(first_kernel, [tile_slot, tile_cols] + near(*slabs, product, *halos),
                        [WIDE] + [SLABS] * 3, 2, WORK)
    first, up, down = choose(pick_slab_kernel, gather(wide))
    halos = halo(up, down)
    parts = along_x(ordered)
    product, = call(near_kernel, near(*slabs, first), [NEAR])
    wide, = call(second_kernel, [tile_slot, tile_cols] + near(*slabs, product, *halos, *state),
                 [arr((GROUP, 120, NRHS), BF16)], 2, WORK)
    got = gather(wide)
    own, up, down = choose(pick_slab_kernel, got)
    halos = halo(up, down)
    result, = call(last_kernel, [tile_cols] + near(*parts, own, *halos, got, first, scale),
                   [jax.ShapeDtypeStruct((SHARE, NRHS), F32)], 1, (EXT, ROWS))
    return result


def solution(mesh):
    in_specs = (
        P(("lead", "grp"), None, None),
        P("lead", None),
        P("lead", None),
        P(),
        P(("lead", "grp"), None),
        P(("lead", "grp")),
    )
    out_specs = P(("lead", "grp"), None)
    return jax.shard_map(body, mesh=mesh, in_specs=in_specs, out_specs=out_specs, check_vma=False)
```

```python
import jax
import jax.numpy as jnp
from jax import lax
from jax.experimental import pallas as pl
from jax.experimental.pallas import tpu as pltpu
from jax.sharding import PartitionSpec as P


TILE = 384
NRHS = 128
SIDE = 4
GROUP = 16
SHARE = 96
SLAB = 24
TILES = 32
PIECE = 216
F32 = jnp.float32
BF16 = jnp.bfloat16
GRANT = 20 << 20
GAIN = 8.0 / 7.0

VMEM = pl.BlockSpec(memory_space=pltpu.VMEM)
SMEM = pl.BlockSpec(memory_space=pltpu.SMEM)


def place():
    member = lax.axis_index("grp")
    return lax.shift_right_logical(member, 2), lax.bitwise_and(member, 3)


def wrap(index):
    return lax.bitwise_and(index, 3)


def column_of(row, first, count):
    line = lax.broadcasted_iota(jnp.int32, (count, 128), 0) + first
    lane = lax.broadcasted_iota(jnp.int32, (count, 128), 1)
    return jnp.sum(jnp.where(line == lane, jnp.broadcast_to(row, (count, 128)), 0.0), axis=1, keepdims=True)


def padded(diag_ref):
    return jnp.concatenate([diag_ref[...], jnp.zeros((1, 128 - SHARE), F32)], axis=1)


def start_kernel(tiles_hbm, residual_hbm, diag_hbm, part0, part1, part2, part3, wide_ref, start_ref, scale_ref,
                 line_ref, residual_ref, diag_ref, high_ref, sems):
    _, q = place()
    copies = [pltpu.make_async_copy(residual_hbm, residual_ref, sems.at[0]),
              pltpu.make_async_copy(diag_hbm, diag_ref, sems.at[1])]
    for k, part in enumerate((part0, part1, part2, part3)):
        at = pl.multiple_of(wrap(q + k) * SHARE, SHARE)
        copies.append(pltpu.make_async_copy(tiles_hbm.at[:, pl.ds(at, SHARE)], part, sems.at[2 + k]))
    for copy in copies:
        copy.start()
    for copy in copies[:2]:
        copy.wait()
    row = padded(diag_ref)
    d_high = row.astype(BF16).astype(F32)
    d_mid = (row - d_high).astype(BF16).astype(F32)
    line_ref[...] = jnp.broadcast_to(jnp.concatenate([d_high, d_mid, row - d_high - d_mid], axis=1), (8, TILE))
    scale = jnp.broadcast_to(column_of(row, 0, SHARE), (SHARE, NRHS))
    scaled = residual_ref[...] * scale
    scale_ref[...] = scale
    start_ref[...] = scaled
    high_ref[...] = scaled.astype(BF16)
    pieces = [pltpu.make_async_copy(high_ref, wide_ref.at[m], sems.at[6 + m]) for m in range(GROUP)]
    for piece in pieces:
        piece.start()
    for copy in copies[2:] + pieces:
        copy.wait()


def spread(value, wide_ref):
    value = value.astype(BF16)
    for m in range(GROUP):
        wide_ref[m] = value


def thirds(rows):
    return jnp.concatenate([rows[8 * k:8 * k + 8] for k in range(3)], axis=1)


def unthirds(rows):
    return jnp.concatenate([rows[:, NRHS * k:NRHS * (k + 1)] for k in range(3)], axis=0)


def split_kernel(*refs):
    parts, (start_ref, line_ref), outs, held_ref = refs[:4], refs[4:6], refs[6:10], refs[10]
    x, q = place()
    high = start_ref[...].astype(BF16).astype(F32)
    low = start_ref[...] - high
    for s in range(SIDE):
        at = slice(SLAB * s, SLAB * (s + 1))
        tail = jnp.concatenate([thirds(high[at]), thirds(low[at]), line_ref[...]], axis=0)
        held_ref[wrap(s - x), 192:PIECE] = tail.astype(BF16)
    for k in range(SIDE):
        tiles = [parts[k][j].astype(F32) for j in range(2)]
        to = pl.multiple_of(48 * wrap(q - k), 48)
        for s in range(SIDE):
            pair = jnp.concatenate([tile[SLAB * s:SLAB * (s + 1)] for tile in tiles], axis=0)
            held_ref[wrap(s - x), pl.ds(to, 48)] = pair.astype(BF16)
    for k in range(SIDE):
        outs[k][...] = held_ref[k]


def table_kernel(slot_ref, cols_ref, rows_ref, slot_out, cols_out, rows_out):
    for t in range(TILES):
        slot_out[0, t] = slot_ref[0, t]
    for r in range(SIDE):
        for k in range(8):
            cols_out[r, k] = cols_ref[r, k]
    lead = lax.axis_index("lead")
    for side in range(2):
        for h in range(2):
            rows_out[side, h] = rows_ref[side, h, lead]


def send_halves(rows_ref, own_ref, up_ref, down_ref):
    for side, ref in ((0, up_ref), (1, down_ref)):
        for h in range(2):
            ref[h] = own_ref[rows_ref[side, h]]


def pick_slab_kernel(rows_ref, got_ref, own_ref, up_ref, down_ref):
    for q in range(SIDE):
        parts = [got_ref[SIDE * x + q, 0:SHARE].astype(F32) for x in range(SIDE)]
        for r in range(SIDE):
            block = jnp.concatenate([p[SLAB * r:SLAB * (r + 1)] for p in parts], axis=0)
            own_ref[r, SHARE * q:SHARE * (q + 1)] = block.astype(BF16)
    send_halves(rows_ref, own_ref, up_ref, down_ref)


def pick_home_kernel(rows_ref, got_ref, own_ref, up_ref, down_ref):
    for r in range(SIDE):
        for q in range(SIDE):
            own_ref[r, SHARE * q:SHARE * (q + 1)] = got_ref[SIDE * r + q]
    send_halves(rows_ref, own_ref, up_ref, down_ref)


def slot_of(slot_ref, x, k, i):
    return slot_ref[0, 8 * wrap(x - k) + i]


def order_kernel(slot_ref, *refs):
    parts, outs, held_ref = refs[:4], refs[4:8], refs[8]
    x, _ = place()
    for k in range(SIDE):
        for y in range(SIDE):
            pair = parts[k][48 * y:48 * (y + 1)].astype(F32)
            for j in range(2):
                to = lax.bitwise_and(slot_of(slot_ref, x, k, 2 * y + j) - 8 * x, TILES - 1)
                held_ref[to] = pair[SLAB * j:SLAB * (j + 1)].astype(BF16)
    for k in range(SIDE):
        outs[k][...] = held_ref[8 * k:8 * k + 8]


def slab_products(slabs, blocks, product_ref, first):
    for pair in range(len(blocks) // 2):
        wide = jnp.concatenate(blocks[2 * pair:2 * pair + 2], axis=1)
        product = jnp.dot(slabs, wide, preferred_element_type=F32)
        product_ref[first + 2 * pair] = product[:, :NRHS]
        product_ref[first + 2 * pair + 1] = product[:, NRHS:]


def all_slabs(parts):
    return jnp.concatenate([part[0:192] for part in parts], axis=0)


def add_up(slot_ref, cols_ref, block_of, product_ref, total_ref):
    x, _ = place()
    product_ref[0] = jnp.zeros((TILES * SLAB, NRHS), F32)
    for t in range(TILES):
        slot = slot_of(slot_ref, x, t // 8, t % 8)
        row = lax.shift_right_logical(slot, 3)
        block = block_of(cols_ref[row, lax.bitwise_and(slot, 7)])
        total_ref[row] += product_ref[block, SLAB * t:SLAB * (t + 1)]


def own_block(col):
    return jnp.where(col < 4, col + 1, 0)


def halo_block(col):
    return jnp.maximum(col - 3, 0)


def near_kernel(slot_ref, cols_ref, *refs):
    own_ref, total_ref, product_ref = refs[4:]
    slab_products(all_slabs(refs[:4]), [own_ref[r] for r in range(SIDE)], product_ref, 1)
    total_ref[...] = jnp.zeros_like(total_ref)
    add_up(slot_ref, cols_ref, own_block, product_ref, total_ref)


def slab_total(slot_ref, cols_ref, parts, near_ref, low_ref, high_ref, product_ref, total_ref):
    slab_products(all_slabs(parts), [low_ref[0], low_ref[1], high_ref[0], high_ref[1]], product_ref, 1)
    total_ref[...] = near_ref[...]
    add_up(slot_ref, cols_ref, halo_block, product_ref, total_ref)


def first_kernel(slot_ref, cols_ref, *refs):
    parts, halo, (wide_ref, first_ref, start_ref, scale_ref), work = refs[:4], refs[4:7], refs[7:11], refs[11:]
    slab_total(slot_ref, cols_ref, parts, *halo, *work)
    total_ref = work[1]
    x, _ = place()
    for k in range(SIDE):
        tail = parts[k][192:PIECE].astype(F32)
        row = tail[16:17, 0:128] + (tail[16:17, 128:256] + tail[16:17, 256:384])
        start = unthirds(tail[0:8]) + unthirds(tail[8:16])
        scale = jnp.broadcast_to(column_of(row, x * SLAB, SLAB), (SLAB, NRHS))
        r = wrap(x - k)
        start_ref[r] = start
        scale_ref[r] = scale
        first_ref[r] = GAIN * (start - scale * total_ref[r])
    spread(jnp.concatenate([first_ref[r] for r in range(SIDE)], axis=0), wide_ref)


def second_kernel(slot_ref, cols_ref, *refs):
    parts, halo, (first_ref, start_ref, scale_ref) = refs[:4], refs[4:7], refs[7:10]
    wide_ref, work = refs[10], refs[11:]
    slab_total(slot_ref, cols_ref, parts, *halo, *work)
    total_ref = work[1]
    seconds, rests = [], []
    for r in range(SIDE):
        first = first_ref[r]
        second = start_ref[r] - first - scale_ref[r] * total_ref[r]
        seconds.append(second)
        rest = first - first.astype(BF16).astype(F32) + GAIN * (second - second.astype(BF16).astype(F32))
        rests.append(rest.astype(BF16))
    high = jnp.concatenate(seconds, axis=0).astype(BF16)
    for r in range(SIDE):
        for s in range(SIDE):
            wide_ref[SIDE * r + s, 0:SHARE] = high
            wide_ref[SIDE * r + s, SHARE:120] = rests[r]


def home_total(cols_ref, block_of, parts, ext_ref, line_ref):
    x, _ = place()
    ext_ref[0] = jnp.zeros((TILE, NRHS), BF16)
    total = jnp.zeros((SHARE, NRHS), F32)
    for k in range(8):
        left = jnp.concatenate([part[k] for part in parts], axis=0)
        total += jnp.dot(left, ext_ref[block_of(cols_ref[x, k])], preferred_element_type=F32)
    for k in range(SIDE):
        line_ref[pl.ds(pl.multiple_of(wrap(x - k) * SLAB, 8), SLAB), :] = total[SLAB * k:SLAB * (k + 1)]
    return line_ref[...]


def third_kernel(cols_ref, *refs):
    parts, (own_ref, got_ref, first_ref, scale_ref, sum_ref, ext_ref, line_ref) = refs[:4], refs[4:]
    x, q = place()
    ext_ref[1:5] = own_ref[...]
    total = home_total(cols_ref, own_block, parts, ext_ref, line_ref)
    mine = pl.ds(pl.multiple_of(q * SHARE, SHARE), SHARE)
    rest = jnp.concatenate([got_ref[SIDE * s + q, SHARE:120].astype(F32) for s in range(SIDE)], axis=0)
    second = own_ref[x, mine].astype(F32) - scale_ref[...] * total
    sum_ref[...] = first_ref[x, mine].astype(F32) + rest + GAIN * second


def last_kernel(cols_ref, *refs):
    parts, (low_ref, high_ref, sum_ref, scale_ref, out_ref, ext_ref, line_ref) = refs[:4], refs[4:]
    ext_ref[1:3] = low_ref[...]
    ext_ref[3:5] = high_ref[...]
    total = home_total(cols_ref, halo_block, parts, ext_ref, line_ref)
    out_ref[...] = sum_ref[...] - GAIN * (scale_ref[...] * total)


def arr(shape, dtype):
    return pltpu.VMEM(shape, dtype)


def call(kernel, args, outs, scalars=0, scratch=(), far=0, away=()):
    vectors = args[scalars:]
    space = pltpu.HBM if far else pltpu.VMEM
    vectors = [pltpu.with_memory_space_constraint(a, space) for a in vectors]
    specs = [SMEM] * scalars + [pl.BlockSpec(memory_space=space)] * len(vectors)
    tables = [pltpu.with_memory_space_constraint(a, pltpu.SMEM) for a in args[:scalars]]
    return pl.pallas_call(kernel, in_specs=specs,
                          out_specs=[pl.BlockSpec(memory_space=pltpu.HBM) if n in away else VMEM for n in range(len(outs))],
                          out_shape=outs, scratch_shapes=list(scratch),
                          compiler_params=pltpu.CompilerParams(vmem_limit_bytes=GRANT))(*tables, *vectors)


def near(*arrays):
    return list(arrays)


HALVES = [arr((2, TILE, NRHS), BF16), arr((2, TILE, NRHS), BF16)]
OWN = arr((SIDE, TILE, NRHS), BF16)
ROWS = arr((SHARE, NRHS), F32)
EXT = arr((5, TILE, NRHS), BF16)
SLABS = arr((SIDE, SLAB, NRHS), F32)
WIDE = arr((GROUP, SHARE, NRHS), BF16)
WORK = (arr((5, TILES * SLAB, NRHS), F32), SLABS)


def body(matrix_tiles, tile_slot, tile_cols, send_rows, residual, diag_inv):
    leads = lax.axis_size("lead")
    rows = send_rows.transpose(1, 2, 0)
    diag = diag_inv.reshape(1, SHARE)

    def halo(up, down):
        lower = lax.ppermute(up, "lead", [(i, (i + 1) % leads) for i in range(leads)])
        upper = lax.ppermute(down, "lead", [(i, (i - 1) % leads) for i in range(leads)])
        return lower, upper

    def gather(wide):
        return lax.all_to_all(wide, "grp", 0, 0)

    def choose(kernel, got):
        return call(kernel, [rows] + near(got), [OWN] + HALVES, 1)

    def along_x(values):
        pairs = [[(m, (m + SIDE * k) % GROUP) for m in range(GROUP)] for k in range(SIDE)]
        return exchange(values, pairs)

    def along_y(values):
        pairs = [[(m, m - m % SIDE + (m + k) % SIDE) for m in range(GROUP)] for k in range(SIDE)]
        return exchange(values, pairs)

    def exchange(values, pairs):
        out = [values[0]]
        for k in range(1, SIDE):
            out.append(lax.ppermute(values[k], "grp", pairs[k]))
        return out

    *quarters, wide, start, scale, line = call(
        start_kernel, [matrix_tiles, residual, diag],
        [arr((2, SHARE, TILE), BF16)] * 4 + [pltpu.HBM((GROUP, SHARE, NRHS), BF16), ROWS, ROWS, arr((8, TILE), F32)],
        scratch=(ROWS, arr((1, SHARE), F32), arr((SHARE, NRHS), BF16), pltpu.SemaphoreType.DMA((6 + GROUP,))), far=1,
        away=(4,))
    tables = [pltpu.SMEM((1, TILES), jnp.int32), pltpu.SMEM((SIDE, 8), jnp.int32), pltpu.SMEM((2, 2), jnp.int32)]
    tile_slot, tile_cols, rows = pl.pallas_call(
        table_kernel, name="tables", in_specs=[SMEM] * 3, out_specs=[SMEM] * 3, out_shape=tables)(
        tile_slot, tile_cols, rows)
    quarters = along_y(quarters)
    got = gather(wide)
    slabs = call(split_kernel, near(*quarters, start, line), [arr((PIECE, TILE), BF16)] * 4, 0,
                 (arr((SIDE, PIECE, TILE), BF16),))
    slabs = along_x(slabs)
    own, up, down = choose(pick_home_kernel, got)
    halos = halo(up, down)
    ordered = call(order_kernel, [tile_slot] + near(*slabs), [arr((8, SLAB, TILE), BF16)] * 4, 1,
                   (arr((TILES, SLAB, TILE), BF16),))
    product, = call(near_kernel, [tile_slot, tile_cols] + near(*slabs, own), [SLABS], 2, WORK[:1])
    wide, *state = call(first_kernel, [tile_slot, tile_cols] + near(*slabs, product, *halos),
                        [WIDE] + [SLABS] * 3, 2, WORK)
    first, up, down = choose(pick_slab_kernel, gather(wide))
    halos = halo(up, down)
    parts = along_x(ordered)
    product, = call(near_kernel, [tile_slot, tile_cols] + near(*slabs, first), [SLABS], 2, WORK[:1])
    wide, = call(second_kernel, [tile_slot, tile_cols] + near(*slabs, product, *halos, *state),
                 [arr((GROUP, 120, NRHS), BF16)], 2, WORK)
    got = gather(wide)
    own, up, down = choose(pick_slab_kernel, got)
    halos = halo(up, down)
    partial, = call(third_kernel, [tile_cols] + near(*parts, own, got, first, scale), [ROWS], 1, (EXT, ROWS))
    result, = call(last_kernel, [tile_cols] + near(*parts, *halos, partial, scale),
                   [jax.ShapeDtypeStruct((SHARE, NRHS), F32)], 1, (EXT, ROWS))
    return result


def solution(mesh):
    in_specs = (
        P(("lead", "grp"), None, None),
        P("lead", None),
        P("lead", None),
        P(),
        P(("lead", "grp"), None),
        P(("lead", "grp")),
    )
    out_specs = P(("lead", "grp"), None)
    return jax.shard_map(body, mesh=mesh, in_specs=in_specs, out_specs=out_specs, check_vma=False)
```

```python
import jax
import jax.numpy as jnp
from jax import lax
from jax.experimental import pallas as pl
from jax.experimental.pallas import tpu as pltpu
from jax.sharding import PartitionSpec as P


TILE = 384
NRHS = 128
SIDE = 4
GROUP = 16
SHARE = 96
SLAB = 24
TILES = 32
PIECE = 216
F32 = jnp.float32
BF16 = jnp.bfloat16
GRANT = 20 << 20
GAIN = 8.0 / 7.0

VMEM = pl.BlockSpec(memory_space=pltpu.VMEM)
SMEM = pl.BlockSpec(memory_space=pltpu.SMEM)


def place():
    member = lax.axis_index("grp")
    return lax.shift_right_logical(member, 2), lax.bitwise_and(member, 3)


def wrap(index):
    return lax.bitwise_and(index, 3)


def column_of(row, first, count):
    line = lax.broadcasted_iota(jnp.int32, (count, 128), 0) + first
    lane = lax.broadcasted_iota(jnp.int32, (count, 128), 1)
    return jnp.sum(jnp.where(line == lane, jnp.broadcast_to(row, (count, 128)), 0.0), axis=1, keepdims=True)


def padded(diag_ref):
    return jnp.concatenate([diag_ref[...], jnp.zeros((1, 128 - SHARE), F32)], axis=1)


def start_kernel(tiles_hbm, residual_hbm, diag_hbm, part0, part1, part2, part3, high_ref, start_ref, scale_ref,
                 line_ref, residual_ref, diag_ref, sems):
    _, q = place()
    copies = [pltpu.make_async_copy(residual_hbm, residual_ref, sems.at[0]),
              pltpu.make_async_copy(diag_hbm, diag_ref, sems.at[1])]
    for k, part in enumerate((part0, part1, part2, part3)):
        at = pl.multiple_of(wrap(q + k) * SHARE, SHARE)
        copies.append(pltpu.make_async_copy(tiles_hbm.at[:, pl.ds(at, SHARE)], part, sems.at[2 + k]))
    for copy in copies:
        copy.start()
    for copy in copies[:2]:
        copy.wait()
    row = padded(diag_ref)
    d_high = row.astype(BF16).astype(F32)
    d_mid = (row - d_high).astype(BF16).astype(F32)
    line_ref[...] = jnp.broadcast_to(jnp.concatenate([d_high, d_mid, row - d_high - d_mid], axis=1), (8, TILE))
    scale = jnp.broadcast_to(column_of(row, 0, SHARE), (SHARE, NRHS))
    scaled = residual_ref[...] * scale
    scale_ref[...] = scale
    start_ref[...] = scaled
    high_ref[...] = scaled.astype(BF16)
    for copy in copies[2:]:
        copy.wait()


def spread(value, wide_ref):
    value = value.astype(BF16)
    for m in range(GROUP):
        wide_ref[m] = value


def thirds(rows):
    return jnp.concatenate([rows[8 * k:8 * k + 8] for k in range(3)], axis=1)


def unthirds(rows):
    return jnp.concatenate([rows[:, NRHS * k:NRHS * (k + 1)] for k in range(3)], axis=0)


def split_kernel(*refs):
    parts, (start_ref, line_ref), outs, held_ref = refs[:4], refs[4:6], refs[6:10], refs[10]
    x, q = place()
    high = start_ref[...].astype(BF16).astype(F32)
    low = start_ref[...] - high
    for s in range(SIDE):
        at = slice(SLAB * s, SLAB * (s + 1))
        tail = jnp.concatenate([thirds(high[at]), thirds(low[at]), line_ref[...]], axis=0)
        held_ref[wrap(s - x), 192:PIECE] = tail.astype(BF16)
    for k in range(SIDE):
        tiles = [parts[k][j].astype(F32) for j in range(2)]
        to = pl.multiple_of(48 * wrap(q - k), 48)
        for s in range(SIDE):
            pair = jnp.concatenate([tile[SLAB * s:SLAB * (s + 1)] for tile in tiles], axis=0)
            held_ref[wrap(s - x), pl.ds(to, 48)] = pair.astype(BF16)
    for k in range(SIDE):
        outs[k][...] = held_ref[k]


def table_kernel(slot_ref, cols_ref, rows_ref, slot_out, cols_out, rows_out):
    for t in range(TILES):
        slot_out[0, t] = slot_ref[0, t]
    for r in range(SIDE):
        for k in range(8):
            cols_out[r, k] = cols_ref[r, k]
    lead = lax.axis_index("lead")
    for side in range(2):
        for h in range(2):
            rows_out[side, h] = rows_ref[side, h, lead]


def send_halves(rows_ref, own_ref, up_ref, down_ref):
    for side, ref in ((0, up_ref), (1, down_ref)):
        for h in range(2):
            ref[h] = own_ref[rows_ref[side, h]]


def pick_slab_kernel(rows_ref, got_ref, own_ref, up_ref, down_ref):
    for q in range(SIDE):
        parts = [got_ref[SIDE * x + q, 0:SHARE].astype(F32) for x in range(SIDE)]
        for r in range(SIDE):
            block = jnp.concatenate([p[SLAB * r:SLAB * (r + 1)] for p in parts], axis=0)
            own_ref[r, SHARE * q:SHARE * (q + 1)] = block.astype(BF16)
    send_halves(rows_ref, own_ref, up_ref, down_ref)


def stack_kernel(*refs):
    out_ref = refs[-1]
    x, _ = place()
    for k in range(SIDE):
        out_ref[wrap(x - k)] = refs[k][...]


def pick_stack_kernel(rows_ref, *refs):
    own_ref, up_ref, down_ref = refs[4:]
    _, q = place()
    for k in range(SIDE):
        at = pl.multiple_of(wrap(q - k) * SHARE, SHARE)
        for r in range(SIDE):
            own_ref[r, pl.ds(at, SHARE)] = refs[k][r]
    send_halves(rows_ref, own_ref, up_ref, down_ref)


def slot_of(slot_ref, x, k, i):
    return slot_ref[0, 8 * wrap(x - k) + i]


def order_kernel(slot_ref, *refs):
    parts, outs, held_ref = refs[:4], refs[4:8], refs[8]
    x, _ = place()
    for k in range(SIDE):
        for y in range(SIDE):
            pair = parts[k][48 * y:48 * (y + 1)].astype(F32)
            for j in range(2):
                to = lax.bitwise_and(slot_of(slot_ref, x, k, 2 * y + j) - 8 * x, TILES - 1)
                held_ref[to] = pair[SLAB * j:SLAB * (j + 1)].astype(BF16)
    for k in range(SIDE):
        outs[k][...] = held_ref[8 * k:8 * k + 8]


def slab_products(slabs, blocks, product_ref, first):
    for pair in range(len(blocks) // 2):
        wide = jnp.concatenate(blocks[2 * pair:2 * pair + 2], axis=1)
        product = jnp.dot(slabs, wide, preferred_element_type=F32)
        product_ref[first + 2 * pair] = product[:, :NRHS]
        product_ref[first + 2 * pair + 1] = product[:, NRHS:]


def all_slabs(parts):
    return jnp.concatenate([part[0:192] for part in parts], axis=0)


def near_kernel(*refs):
    own_ref, product_ref = refs[4:]
    slab_products(all_slabs(refs[:4]), [own_ref[r] for r in range(SIDE)], product_ref, 0)


def slab_total(slot_ref, cols_ref, parts, near_ref, low_ref, high_ref, product_ref, total_ref):
    x, _ = place()
    slab_products(all_slabs(parts), [low_ref[0], low_ref[1], high_ref[0], high_ref[1]], product_ref, 4)
    product_ref[0:4] = near_ref[...]
    total_ref[...] = jnp.zeros_like(total_ref)
    for t in range(TILES):
        slot = slot_of(slot_ref, x, t // 8, t % 8)
        row = lax.shift_right_logical(slot, 3)
        col = cols_ref[row, lax.bitwise_and(slot, 7)]
        total_ref[row] += product_ref[col, SLAB * t:SLAB * (t + 1)]


def first_kernel(slot_ref, cols_ref, *refs):
    parts, halo, (wide_ref, first_ref, start_ref, scale_ref), work = refs[:4], refs[4:7], refs[7:11], refs[11:]
    slab_total(slot_ref, cols_ref, parts, *halo, *work)
    total_ref = work[1]
    x, _ = place()
    for k in range(SIDE):
        tail = parts[k][192:PIECE].astype(F32)
        row = tail[16:17, 0:128] + (tail[16:17, 128:256] + tail[16:17, 256:384])
        start = unthirds(tail[0:8]) + unthirds(tail[8:16])
        scale = jnp.broadcast_to(column_of(row, x * SLAB, SLAB), (SLAB, NRHS))
        r = wrap(x - k)
        start_ref[r] = start
        scale_ref[r] = scale
        first_ref[r] = GAIN * (start - scale * total_ref[r])
    spread(jnp.concatenate([first_ref[r] for r in range(SIDE)], axis=0), wide_ref)


def second_kernel(slot_ref, cols_ref, *refs):
    parts, halo, (first_ref, start_ref, scale_ref) = refs[:4], refs[4:7], refs[7:10]
    wide_ref, work = refs[10], refs[11:]
    slab_total(slot_ref, cols_ref, parts, *halo, *work)
    total_ref = work[1]
    seconds, rests = [], []
    for r in range(SIDE):
        first = first_ref[r]
        second = start_ref[r] - first - scale_ref[r] * total_ref[r]
        seconds.append(second)
        rest = first - first.astype(BF16).astype(F32) + GAIN * (second - second.astype(BF16).astype(F32))
        rests.append(rest.astype(BF16))
    high = jnp.concatenate(seconds, axis=0).astype(BF16)
    for r in range(SIDE):
        for s in range(SIDE):
            wide_ref[SIDE * r + s, 0:SHARE] = high
            wide_ref[SIDE * r + s, SHARE:120] = rests[r]


def last_kernel(cols_ref, *refs):
    parts, halo, (got_ref, first_ref, scale_ref, out_ref, ext_ref, line_ref) = refs[:4], refs[4:7], refs[7:]
    own_ref, low_ref, high_ref = halo
    x, q = place()
    ext_ref[0:4] = own_ref[...]
    ext_ref[4:6] = low_ref[...]
    ext_ref[6:8] = high_ref[...]
    total = jnp.zeros((SHARE, NRHS), F32)
    for k in range(8):
        left = jnp.concatenate([part[k] for part in parts], axis=0)
        total += jnp.dot(left, ext_ref[cols_ref[x, k]], preferred_element_type=F32)
    for k in range(SIDE):
        line_ref[pl.ds(pl.multiple_of(wrap(x - k) * SLAB, 8), SLAB), :] = total[SLAB * k:SLAB * (k + 1)]
    mine = pl.ds(pl.multiple_of(q * SHARE, SHARE), SHARE)
    rest = jnp.concatenate([got_ref[SIDE * s + q, SHARE:120].astype(F32) for s in range(SIDE)], axis=0)
    second = own_ref[x, mine].astype(F32) - scale_ref[...] * line_ref[...]
    out_ref[...] = first_ref[x, mine].astype(F32) + rest + GAIN * second


def arr(shape, dtype):
    return pltpu.VMEM(shape, dtype)


def call(kernel, args, outs, scalars=0, scratch=(), far=0):
    vectors = args[scalars:]
    space = pltpu.HBM if far else pltpu.VMEM
    vectors = [pltpu.with_memory_space_constraint(a, space) for a in vectors]
    specs = [SMEM] * scalars + [pl.BlockSpec(memory_space=space)] * len(vectors)
    tables = [pltpu.with_memory_space_constraint(a, pltpu.SMEM) for a in args[:scalars]]
    return pl.pallas_call(kernel, in_specs=specs, out_specs=[VMEM] * len(outs),
                          out_shape=outs, scratch_shapes=list(scratch),
                          compiler_params=pltpu.CompilerParams(vmem_limit_bytes=GRANT))(*tables, *vectors)


def near(*arrays):
    return list(arrays)


HALVES = [arr((2, TILE, NRHS), BF16), arr((2, TILE, NRHS), BF16)]
OWN = arr((SIDE, TILE, NRHS), BF16)
ROWS = arr((SHARE, NRHS), F32)
EXT = arr((8, TILE, NRHS), BF16)
SLABS = arr((SIDE, SLAB, NRHS), F32)
WIDE = arr((GROUP, SHARE, NRHS), BF16)
NEAR = arr((4, TILES * SLAB, NRHS), F32)
WORK = (arr((8, TILES * SLAB, NRHS), F32), SLABS)


def body(matrix_tiles, tile_slot, tile_cols, send_rows, residual, diag_inv):
    leads = lax.axis_size("lead")
    rows = send_rows.transpose(1, 2, 0)
    diag = diag_inv.reshape(1, SHARE)

    def halo(up, down):
        lower = lax.ppermute(up, "lead", [(i, (i + 1) % leads) for i in range(leads)])
        upper = lax.ppermute(down, "lead", [(i, (i - 1) % leads) for i in range(leads)])
        return lower, upper

    def gather(wide):
        return lax.all_to_all(wide, "grp", 0, 0)

    def choose(kernel, *got):
        return call(kernel, [rows] + near(*got), [OWN] + HALVES, 1)

    def along_x(values):
        pairs = [[(m, (m + SIDE * k) % GROUP) for m in range(GROUP)] for k in range(SIDE)]
        return exchange(values, pairs)

    def along_y(values):
        pairs = [[(m, m - m % SIDE + (m + k) % SIDE) for m in range(GROUP)] for k in range(SIDE)]
        return exchange(values, pairs)

    def exchange(values, pairs):
        out = [values[0]]
        for k in range(1, SIDE):
            out.append(lax.ppermute(values[k], "grp", pairs[k]))
        return out

    *quarters, high, start, scale, line = call(
        start_kernel, [matrix_tiles, residual, diag],
        [arr((2, SHARE, TILE), BF16)] * 4 + [arr((SHARE, NRHS), BF16), ROWS, ROWS, arr((8, TILE), F32)],
        scratch=(ROWS, arr((1, SHARE), F32), pltpu.SemaphoreType.DMA((6,))), far=1)
    tables = [pltpu.SMEM((1, TILES), jnp.int32), pltpu.SMEM((SIDE, 8), jnp.int32), pltpu.SMEM((2, 2), jnp.int32)]
    tile_slot, tile_cols, rows = pl.pallas_call(
        table_kernel, name="tables", in_specs=[SMEM] * 3, out_specs=[SMEM] * 3, out_shape=tables)(
        tile_slot, tile_cols, rows)
    shares = along_x([high] * SIDE)
    quarters = along_y(quarters)
    column, = call(stack_kernel, near(*shares), [arr((SIDE, SHARE, NRHS), BF16)])
    columns = along_y([column] * SIDE)
    slabs = call(split_kernel, near(*quarters, start, line), [arr((PIECE, TILE), BF16)] * 4, 0,
                 (arr((SIDE, PIECE, TILE), BF16),))
    slabs = along_x(slabs)
    own, up, down = choose(pick_stack_kernel, *columns)
    halos = halo(up, down)
    ordered = call(order_kernel, [tile_slot] + near(*slabs), [arr((8, SLAB, TILE), BF16)] * 4, 1,
                   (arr((TILES, SLAB, TILE), BF16),))
    product, = call(near_kernel, near(*slabs, own), [NEAR])
    wide, *state = call(first_kernel, [tile_slot, tile_cols] + near(*slabs, product, *halos),
                        [WIDE] + [SLABS] * 3, 2, WORK)
    first, up, down = choose(pick_slab_kernel, gather(wide))
    halos = halo(up, down)
    parts = along_x(ordered)
    product, = call(near_kernel, near(*slabs, first), [NEAR])
    wide, = call(second_kernel, [tile_slot, tile_cols] + near(*slabs, product, *halos, *state),
                 [arr((GROUP, 120, NRHS), BF16)], 2, WORK)
    got = gather(wide)
    own, up, down = choose(pick_slab_kernel, got)
    halos = halo(up, down)
    result, = call(last_kernel, [tile_cols] + near(*parts, own, *halos, got, first, scale),
                   [jax.ShapeDtypeStruct((SHARE, NRHS), F32)], 1, (EXT, ROWS))
    return result


def solution(mesh):
    in_specs = (
        P(("lead", "grp"), None, None),
        P("lead", None),
        P("lead", None),
        P(),
        P(("lead", "grp"), None),
        P(("lead", "grp")),
    )
    out_specs = P(("lead", "grp"), None)
    return jax.shard_map(body, mesh=mesh, in_specs=in_specs, out_specs=out_specs, check_vma=False)
```

```python
import jax
import jax.numpy as jnp
from jax import lax
from jax.experimental import pallas as pl
from jax.experimental.pallas import tpu as pltpu
from jax.sharding import PartitionSpec as P


TILE = 384
NRHS = 128
SIDE = 4
GROUP = 16
SHARE = 96
SLAB = 24
TILES = 32
PIECE = 216
F32 = jnp.float32
BF16 = jnp.bfloat16
GRANT = 20 << 20
GAIN = 8.0 / 7.0

VMEM = pl.BlockSpec(memory_space=pltpu.VMEM)
SMEM = pl.BlockSpec(memory_space=pltpu.SMEM)


def place():
    member = lax.axis_index("grp")
    return lax.shift_right_logical(member, 2), lax.bitwise_and(member, 3)


def wrap(index):
    return lax.bitwise_and(index, 3)


def column_of(row, first, count):
    line = lax.broadcasted_iota(jnp.int32, (count, 128), 0) + first
    lane = lax.broadcasted_iota(jnp.int32, (count, 128), 1)
    return jnp.sum(jnp.where(line == lane, jnp.broadcast_to(row, (count, 128)), 0.0), axis=1, keepdims=True)


def padded(diag_ref):
    return jnp.concatenate([diag_ref[...], jnp.zeros((1, 128 - SHARE), F32)], axis=1)


def start_kernel(tiles_hbm, residual_hbm, diag_hbm, part0, part1, part2, part3, wide_ref, start_ref, scale_ref,
                 line_ref, residual_ref, diag_ref, high_ref, sems):
    _, q = place()
    copies = [pltpu.make_async_copy(residual_hbm, residual_ref, sems.at[0]),
              pltpu.make_async_copy(diag_hbm, diag_ref, sems.at[1])]
    for k, part in enumerate((part0, part1, part2, part3)):
        at = pl.multiple_of(wrap(q + k) * SHARE, SHARE)
        copies.append(pltpu.make_async_copy(tiles_hbm.at[:, pl.ds(at, SHARE)], part, sems.at[2 + k]))
    for copy in copies:
        copy.start()
    for copy in copies[:2]:
        copy.wait()
    row = padded(diag_ref)
    d_high = row.astype(BF16).astype(F32)
    d_mid = (row - d_high).astype(BF16).astype(F32)
    line_ref[...] = jnp.broadcast_to(jnp.concatenate([d_high, d_mid, row - d_high - d_mid], axis=1), (8, TILE))
    scale = jnp.broadcast_to(column_of(row, 0, SHARE), (SHARE, NRHS))
    scaled = residual_ref[...] * scale
    scale_ref[...] = scale
    start_ref[...] = scaled
    high_ref[...] = scaled.astype(BF16)
    pieces = [pltpu.make_async_copy(high_ref, wide_ref.at[m], sems.at[6 + m]) for m in range(GROUP)]
    for piece in pieces:
        piece.start()
    for copy in copies[2:] + pieces:
        copy.wait()


def spread(value, wide_ref):
    value = value.astype(BF16)
    for m in range(GROUP):
        wide_ref[m] = value


def thirds(rows):
    return jnp.concatenate([rows[8 * k:8 * k + 8] for k in range(3)], axis=1)


def unthirds(rows):
    return jnp.concatenate([rows[:, NRHS * k:NRHS * (k + 1)] for k in range(3)], axis=0)


def split_kernel(*refs):
    parts, (start_ref, line_ref), outs, held_ref = refs[:4], refs[4:6], refs[6:10], refs[10]
    x, q = place()
    high = start_ref[...].astype(BF16).astype(F32)
    low = start_ref[...] - high
    for s in range(SIDE):
        at = slice(SLAB * s, SLAB * (s + 1))
        tail = jnp.concatenate([thirds(high[at]), thirds(low[at]), line_ref[...]], axis=0)
        held_ref[wrap(s - x), 192:PIECE] = tail.astype(BF16)
    for k in range(SIDE):
        tiles = [parts[k][j].astype(F32) for j in range(2)]
        to = pl.multiple_of(48 * wrap(q - k), 48)
        for s in range(SIDE):
            pair = jnp.concatenate([tile[SLAB * s:SLAB * (s + 1)] for tile in tiles], axis=0)
            held_ref[wrap(s - x), pl.ds(to, 48)] = pair.astype(BF16)
    for k in range(SIDE):
        outs[k][...] = held_ref[k]


def table_kernel(slot_ref, cols_ref, rows_ref, slot_out, cols_out, rows_out):
    for t in range(TILES):
        slot_out[0, t] = slot_ref[0, t]
    for r in range(SIDE):
        for k in range(8):
            cols_out[r, k] = cols_ref[r, k]
    lead = lax.axis_index("lead")
    for side in range(2):
        for h in range(2):
            rows_out[side, h] = rows_ref[side, h, lead]


def send_halves(rows_ref, own_ref, up_ref, down_ref):
    for side, ref in ((0, up_ref), (1, down_ref)):
        for h in range(2):
            ref[h] = own_ref[rows_ref[side, h]]


def pick_slab_kernel(rows_ref, got_ref, own_ref, up_ref, down_ref):
    for q in range(SIDE):
        parts = [got_ref[SIDE * x + q, 0:SHARE].astype(F32) for x in range(SIDE)]
        for r in range(SIDE):
            block = jnp.concatenate([p[SLAB * r:SLAB * (r + 1)] for p in parts], axis=0)
            own_ref[r, SHARE * q:SHARE * (q + 1)] = block.astype(BF16)
    send_halves(rows_ref, own_ref, up_ref, down_ref)


def pick_home_kernel(rows_ref, got_ref, own_ref, up_ref, down_ref):
    for r in range(SIDE):
        for q in range(SIDE):
            own_ref[r, SHARE * q:SHARE * (q + 1)] = got_ref[SIDE * r + q]
    send_halves(rows_ref, own_ref, up_ref, down_ref)


def slot_of(slot_ref, x, k, i):
    return slot_ref[0, 8 * wrap(x - k) + i]


def order_kernel(slot_ref, *refs):
    parts, outs, held_ref = refs[:4], refs[4:8], refs[8]
    x, _ = place()
    for k in range(SIDE):
        for y in range(SIDE):
            pair = parts[k][48 * y:48 * (y + 1)].astype(F32)
            for j in range(2):
                to = lax.bitwise_and(slot_of(slot_ref, x, k, 2 * y + j) - 8 * x, TILES - 1)
                held_ref[to] = pair[SLAB * j:SLAB * (j + 1)].astype(BF16)
    for k in range(SIDE):
        outs[k][...] = held_ref[8 * k:8 * k + 8]


def slab_products(slabs, blocks, product_ref, first):
    for pair in range(len(blocks) // 2):
        wide = jnp.concatenate(blocks[2 * pair:2 * pair + 2], axis=1)
        product = jnp.dot(slabs, wide, preferred_element_type=F32)
        product_ref[first + 2 * pair] = product[:, :NRHS]
        product_ref[first + 2 * pair + 1] = product[:, NRHS:]


def all_slabs(parts):
    return jnp.concatenate([part[0:192] for part in parts], axis=0)


def add_up(slot_ref, cols_ref, base, blocks, parts, product_ref, total_ref):
    x, _ = place()
    product_ref[0] = jnp.zeros((TILES * SLAB, NRHS), F32)
    slab_products(all_slabs(parts), blocks, product_ref, 1)
    for t in range(TILES):
        slot = slot_of(slot_ref, x, t // 8, t % 8)
        row = lax.shift_right_logical(slot, 3)
        block = cols_ref[row, lax.bitwise_and(slot, 7)] - base + 1
        block = jnp.where(block > len(blocks), 0, jnp.maximum(block, 0))
        total_ref[row] += product_ref[block, SLAB * t:SLAB * (t + 1)]


def near_kernel(slot_ref, cols_ref, *refs):
    own_ref, total_ref, product_ref = refs[4:]
    total_ref[...] = jnp.zeros_like(total_ref)
    add_up(slot_ref, cols_ref, 0, [own_ref[r] for r in range(SIDE)], refs[:4], product_ref, total_ref)


def half_kernel(slot_ref, cols_ref, *refs):
    near_ref, high_ref, total_ref, product_ref = refs[4:]
    total_ref[...] = near_ref[...]
    add_up(slot_ref, cols_ref, 6, [high_ref[0], high_ref[1]], refs[:4], product_ref, total_ref)


def slab_total(slot_ref, cols_ref, parts, near_ref, low_ref, product_ref, total_ref):
    total_ref[...] = near_ref[...]
    add_up(slot_ref, cols_ref, 4, [low_ref[0], low_ref[1]], parts, product_ref, total_ref)


def first_kernel(slot_ref, cols_ref, *refs):
    parts, halo, (wide_ref, first_ref, start_ref, scale_ref), work = refs[:4], refs[4:6], refs[6:10], refs[10:]
    slab_total(slot_ref, cols_ref, parts, *halo, *work)
    total_ref = work[1]
    x, _ = place()
    for k in range(SIDE):
        tail = parts[k][192:PIECE].astype(F32)
        row = tail[16:17, 0:128] + (tail[16:17, 128:256] + tail[16:17, 256:384])
        start = unthirds(tail[0:8]) + unthirds(tail[8:16])
        scale = jnp.broadcast_to(column_of(row, x * SLAB, SLAB), (SLAB, NRHS))
        r = wrap(x - k)
        start_ref[r] = start
        scale_ref[r] = scale
        first_ref[r] = GAIN * (start - scale * total_ref[r])
    spread(jnp.concatenate([first_ref[r] for r in range(SIDE)], axis=0), wide_ref)


def second_kernel(slot_ref, cols_ref, *refs):
    parts, halo, (first_ref, start_ref, scale_ref) = refs[:4], refs[4:6], refs[6:9]
    wide_ref, work = refs[9], refs[10:]
    slab_total(slot_ref, cols_ref, parts, *halo, *work)
    total_ref = work[1]
    seconds, rests = [], []
    for r in range(SIDE):
        first = first_ref[r]
        second = start_ref[r] - first - scale_ref[r] * total_ref[r]
        seconds.append(second)
        rest = first - first.astype(BF16).astype(F32) + GAIN * (second - second.astype(BF16).astype(F32))
        rests.append(rest.astype(BF16))
    high = jnp.concatenate(seconds, axis=0).astype(BF16)
    for r in range(SIDE):
        for s in range(SIDE):
            wide_ref[SIDE * r + s, 0:SHARE] = high
            wide_ref[SIDE * r + s, SHARE:120] = rests[r]


def last_kernel(cols_ref, *refs):
    parts, halo, (got_ref, first_ref, scale_ref, out_ref, ext_ref, line_ref) = refs[:4], refs[4:7], refs[7:]
    own_ref, low_ref, high_ref = halo
    x, q = place()
    ext_ref[0:4] = own_ref[...]
    ext_ref[4:6] = low_ref[...]
    ext_ref[6:8] = high_ref[...]
    total = jnp.zeros((SHARE, NRHS), F32)
    for k in range(8):
        left = jnp.concatenate([part[k] for part in parts], axis=0)
        total += jnp.dot(left, ext_ref[cols_ref[x, k]], preferred_element_type=F32)
    for k in range(SIDE):
        line_ref[pl.ds(pl.multiple_of(wrap(x - k) * SLAB, 8), SLAB), :] = total[SLAB * k:SLAB * (k + 1)]
    mine = pl.ds(pl.multiple_of(q * SHARE, SHARE), SHARE)
    rest = jnp.concatenate([got_ref[SIDE * s + q, SHARE:120].astype(F32) for s in range(SIDE)], axis=0)
    second = own_ref[x, mine].astype(F32) - scale_ref[...] * line_ref[...]
    out_ref[...] = first_ref[x, mine].astype(F32) + rest + GAIN * second


def arr(shape, dtype):
    return pltpu.VMEM(shape, dtype)


def call(kernel, args, outs, scalars=0, scratch=(), far=0, away=()):
    vectors = args[scalars:]
    space = pltpu.HBM if far else pltpu.VMEM
    vectors = [pltpu.with_memory_space_constraint(a, space) for a in vectors]
    specs = [SMEM] * scalars + [pl.BlockSpec(memory_space=space)] * len(vectors)
    tables = [pltpu.with_memory_space_constraint(a, pltpu.SMEM) for a in args[:scalars]]
    return pl.pallas_call(kernel, in_specs=specs,
                          out_specs=[pl.BlockSpec(memory_space=pltpu.HBM) if n in away else VMEM for n in range(len(outs))],
                          out_shape=outs, scratch_shapes=list(scratch),
                          compiler_params=pltpu.CompilerParams(vmem_limit_bytes=GRANT))(*tables, *vectors)


def near(*arrays):
    return list(arrays)


HALVES = [arr((2, TILE, NRHS), BF16), arr((2, TILE, NRHS), BF16)]
OWN = arr((SIDE, TILE, NRHS), BF16)
ROWS = arr((SHARE, NRHS), F32)
EXT = arr((8, TILE, NRHS), BF16)
SLABS = arr((SIDE, SLAB, NRHS), F32)
WIDE = arr((GROUP, SHARE, NRHS), BF16)
WORK = (arr((5, TILES * SLAB, NRHS), F32), SLABS)


def body(matrix_tiles, tile_slot, tile_cols, send_rows, residual, diag_inv):
    leads = lax.axis_size("lead")
    rows = send_rows.transpose(1, 2, 0)
    diag = diag_inv.reshape(1, SHARE)

    def halo(up, down):
        lower = lax.ppermute(up, "lead", [(i, (i + 1) % leads) for i in range(leads)])
        upper = lax.ppermute(down, "lead", [(i, (i - 1) % leads) for i in range(leads)])
        return lower, upper

    def gather(wide):
        return lax.all_to_all(wide, "grp", 0, 0)

    def choose(kernel, got):
        return call(kernel, [rows] + near(got), [OWN] + HALVES, 1)

    def along_x(values):
        pairs = [[(m, (m + SIDE * k) % GROUP) for m in range(GROUP)] for k in range(SIDE)]
        return exchange(values, pairs)

    def along_y(values):
        pairs = [[(m, m - m % SIDE + (m + k) % SIDE) for m in range(GROUP)] for k in range(SIDE)]
        return exchange(values, pairs)

    def exchange(values, pairs):
        out = [values[0]]
        for k in range(1, SIDE):
            out.append(lax.ppermute(values[k], "grp", pairs[k]))
        return out

    *quarters, wide, start, scale, line = call(
        start_kernel, [matrix_tiles, residual, diag],
        [arr((2, SHARE, TILE), BF16)] * 4 + [pltpu.HBM((GROUP, SHARE, NRHS), BF16), ROWS, ROWS, arr((8, TILE), F32)],
        scratch=(ROWS, arr((1, SHARE), F32), arr((SHARE, NRHS), BF16), pltpu.SemaphoreType.DMA((6 + GROUP,))), far=1,
        away=(4,))
    tables = [pltpu.SMEM((1, TILES), jnp.int32), pltpu.SMEM((SIDE, 8), jnp.int32), pltpu.SMEM((2, 2), jnp.int32)]
    tile_slot, tile_cols, rows = pl.pallas_call(
        table_kernel, name="tables", in_specs=[SMEM] * 3, out_specs=[SMEM] * 3, out_shape=tables)(
        tile_slot, tile_cols, rows)
    quarters = along_y(quarters)
    got = gather(wide)
    slabs = call(split_kernel, near(*quarters, start, line), [arr((PIECE, TILE), BF16)] * 4, 0,
                 (arr((SIDE, PIECE, TILE), BF16),))
    slabs = along_x(slabs)
    own, up, down = choose(pick_home_kernel, got)
    halos = halo(up, down)
    ordered = call(order_kernel, [tile_slot] + near(*slabs), [arr((8, SLAB, TILE), BF16)] * 4, 1,
                   (arr((TILES, SLAB, TILE), BF16),))
    total, = call(near_kernel, [tile_slot, tile_cols] + near(*slabs, own), [SLABS], 2, WORK[:1])
    total, = call(half_kernel, [tile_slot, tile_cols] + near(*slabs, total, halos[1]), [SLABS], 2, WORK[:1])
    wide, *state = call(first_kernel, [tile_slot, tile_cols] + near(*slabs, total, halos[0]),
                        [WIDE] + [SLABS] * 3, 2, WORK)
    first, up, down = choose(pick_slab_kernel, gather(wide))
    halos = halo(up, down)
    parts = along_x(ordered)
    total, = call(near_kernel, [tile_slot, tile_cols] + near(*slabs, first), [SLABS], 2, WORK[:1])
    total, = call(half_kernel, [tile_slot, tile_cols] + near(*slabs, total, halos[1]), [SLABS], 2, WORK[:1])
    wide, = call(second_kernel, [tile_slot, tile_cols] + near(*slabs, total, halos[0], *state),
                 [arr((GROUP, 120, NRHS), BF16)], 2, WORK)
    got = gather(wide)
    own, up, down = choose(pick_slab_kernel, got)
    halos = halo(up, down)
    result, = call(last_kernel, [tile_cols] + near(*parts, own, *halos, got, first, scale),
                   [jax.ShapeDtypeStruct((SHARE, NRHS), F32)], 1, (EXT, ROWS))
    return result


def solution(mesh):
    in_specs = (
        P(("lead", "grp"), None, None),
        P("lead", None),
        P("lead", None),
        P(),
        P(("lead", "grp"), None),
        P(("lead", "grp")),
    )
    out_specs = P(("lead", "grp"), None)
    return jax.shard_map(body, mesh=mesh, in_specs=in_specs, out_specs=out_specs, check_vma=False)
```

```python
import jax
import jax.numpy as jnp
from jax import lax
from jax.experimental import pallas as pl
from jax.experimental.pallas import tpu as pltpu
from jax.sharding import PartitionSpec as P


TILE = 384
NRHS = 128
SIDE = 4
GROUP = 16
SHARE = 96
SLAB = 24
TILES = 32
PIECE = 216
F32 = jnp.float32
BF16 = jnp.bfloat16
GRANT = 20 << 20
GAIN = 8.0 / 7.0

VMEM = pl.BlockSpec(memory_space=pltpu.VMEM)
SMEM = pl.BlockSpec(memory_space=pltpu.SMEM)


def place():
    member = lax.axis_index("grp")
    return lax.shift_right_logical(member, 2), lax.bitwise_and(member, 3)


def swap(index, k):
    return lax.bitwise_xor(index, k)


def column_of(row, first, count):
    line = lax.broadcasted_iota(jnp.int32, (count, 128), 0) + first
    lane = lax.broadcasted_iota(jnp.int32, (count, 128), 1)
    return jnp.sum(jnp.where(line == lane, jnp.broadcast_to(row, (count, 128)), 0.0), axis=1, keepdims=True)


def padded(diag_ref):
    return jnp.concatenate([diag_ref[...], jnp.zeros((1, 128 - SHARE), F32)], axis=1)


def start_kernel(tiles_hbm, residual_hbm, diag_hbm, part0, part1, part2, part3, wide_ref, start_ref, scale_ref,
                 line_ref, residual_ref, diag_ref, sems):
    _, q = place()
    copies = [pltpu.make_async_copy(residual_hbm, residual_ref, sems.at[0]),
              pltpu.make_async_copy(diag_hbm, diag_ref, sems.at[1])]
    for k, part in enumerate((part0, part1, part2, part3)):
        at = pl.multiple_of(swap(q, k) * SHARE, SHARE)
        copies.append(pltpu.make_async_copy(tiles_hbm.at[:, pl.ds(at, SHARE)], part, sems.at[2 + k]))
    for copy in copies:
        copy.start()
    for copy in copies[:2]:
        copy.wait()
    row = padded(diag_ref)
    d_high = row.astype(BF16).astype(F32)
    d_mid = (row - d_high).astype(BF16).astype(F32)
    line_ref[...] = jnp.broadcast_to(jnp.concatenate([d_high, d_mid, row - d_high - d_mid], axis=1), (8, TILE))
    scale = jnp.broadcast_to(column_of(row, 0, SHARE), (SHARE, NRHS))
    scaled = residual_ref[...] * scale
    scale_ref[...] = scale
    start_ref[...] = scaled
    spread(scaled, wide_ref)
    for copy in copies[2:]:
        copy.wait()


def spread(value, wide_ref):
    value = value.astype(BF16)
    for m in range(GROUP):
        wide_ref[m] = value


def thirds(rows):
    return jnp.concatenate([rows[8 * k:8 * k + 8] for k in range(3)], axis=1)


def unthirds(rows):
    return jnp.concatenate([rows[:, NRHS * k:NRHS * (k + 1)] for k in range(3)], axis=0)


def split_kernel(*refs):
    parts, (start_ref, line_ref), outs, held_ref = refs[:4], refs[4:6], refs[6:10], refs[10]
    x, q = place()
    high = start_ref[...].astype(BF16).astype(F32)
    low = start_ref[...] - high
    for s in range(SIDE):
        at = slice(SLAB * s, SLAB * (s + 1))
        tail = jnp.concatenate([thirds(high[at]), thirds(low[at]), line_ref[...]], axis=0)
        held_ref[swap(x, s), 192:PIECE] = tail.astype(BF16)
    for k in range(SIDE):
        tiles = [parts[k][j].astype(F32) for j in range(2)]
        to = pl.multiple_of(48 * swap(q, k), 48)
        for s in range(SIDE):
            pair = jnp.concatenate([tile[SLAB * s:SLAB * (s + 1)] for tile in tiles], axis=0)
            held_ref[swap(x, s), pl.ds(to, 48)] = pair.astype(BF16)
    for k in range(SIDE):
        outs[k][...] = held_ref[k]


def table_kernel(slot_ref, cols_ref, rows_ref, slot_out, cols_out, rows_out):
    for t in range(TILES):
        slot_out[0, t] = slot_ref[0, t]
    for r in range(SIDE):
        for k in range(8):
            cols_out[r, k] = cols_ref[r, k]
    lead = lax.axis_index("lead")
    for side in range(2):
        for h in range(2):
            rows_out[side, h] = rows_ref[side, h, lead]


def send_halves(rows_ref, own_ref, up_ref, down_ref):
    for side, ref in ((0, up_ref), (1, down_ref)):
        for h in range(2):
            ref[h] = own_ref[rows_ref[side, h]]


def pick_slab_kernel(rows_ref, got_ref, own_ref, up_ref, down_ref):
    for q in range(SIDE):
        parts = [got_ref[SIDE * x + q, 0:SHARE].astype(F32) for x in range(SIDE)]
        for r in range(SIDE):
            block = jnp.concatenate([p[SLAB * r:SLAB * (r + 1)] for p in parts], axis=0)
            own_ref[r, SHARE * q:SHARE * (q + 1)] = block.astype(BF16)
    send_halves(rows_ref, own_ref, up_ref, down_ref)


def pick_home_kernel(rows_ref, got_ref, own_ref, up_ref, down_ref):
    for r in range(SIDE):
        for q in range(SIDE):
            own_ref[r, SHARE * q:SHARE * (q + 1)] = got_ref[SIDE * r + q]
    send_halves(rows_ref, own_ref, up_ref, down_ref)


def slot_of(slot_ref, x, k, i):
    return slot_ref[0, 8 * swap(x, k) + i]


def order_kernel(slot_ref, *refs):
    parts, outs, held_ref = refs[:4], refs[4:8], refs[8]
    x, _ = place()
    for k in range(SIDE):
        for y in range(SIDE):
            pair = parts[k][48 * y:48 * (y + 1)].astype(F32)
            for j in range(2):
                to = lax.bitwise_xor(slot_of(slot_ref, x, k, 2 * y + j), 8 * x)
                held_ref[to] = pair[SLAB * j:SLAB * (j + 1)].astype(BF16)
    for k in range(SIDE):
        outs[k][...] = held_ref[8 * k:8 * k + 8]


def slab_products(slabs, blocks, product_ref, first):
    for pair in range(len(blocks) // 2):
        wide = jnp.concatenate(blocks[2 * pair:2 * pair + 2], axis=1)
        product = jnp.dot(slabs, wide, preferred_element_type=F32)
        product_ref[first + 2 * pair] = product[:, :NRHS]
        product_ref[first + 2 * pair + 1] = product[:, NRHS:]


def all_slabs(parts):
    return jnp.concatenate([part[0:192] for part in parts], axis=0)


def near_kernel(*refs):
    own_ref, product_ref = refs[4:]
    slab_products(all_slabs(refs[:4]), [own_ref[r] for r in range(SIDE)], product_ref, 0)


def slab_total(slot_ref, cols_ref, parts, near_ref, low_ref, high_ref, product_ref, total_ref):
    x, _ = place()
    slab_products(all_slabs(parts), [low_ref[0], low_ref[1], high_ref[0], high_ref[1]], product_ref, 4)
    product_ref[0:4] = near_ref[...]
    total_ref[...] = jnp.zeros_like(total_ref)
    for t in range(TILES):
        slot = slot_of(slot_ref, x, t // 8, t % 8)
        row = lax.shift_right_logical(slot, 3)
        col = cols_ref[row, lax.bitwise_and(slot, 7)]
        total_ref[row] += product_ref[col, SLAB * t:SLAB * (t + 1)]


def first_kernel(slot_ref, cols_ref, *refs):
    parts, halo, (wide_ref, first_ref, start_ref, scale_ref), work = refs[:4], refs[4:7], refs[7:11], refs[11:]
    slab_total(slot_ref, cols_ref, parts, *halo, *work)
    total_ref = work[1]
    x, _ = place()
    for k in range(SIDE):
        tail = parts[k][192:PIECE].astype(F32)
        row = tail[16:17, 0:128] + (tail[16:17, 128:256] + tail[16:17, 256:384])
        start = unthirds(tail[0:8]) + unthirds(tail[8:16])
        scale = jnp.broadcast_to(column_of(row, x * SLAB, SLAB), (SLAB, NRHS))
        r = swap(x, k)
        start_ref[r] = start
        scale_ref[r] = scale
        first_ref[r] = GAIN * (start - scale * total_ref[r])
    spread(jnp.concatenate([first_ref[r] for r in range(SIDE)], axis=0), wide_ref)


def second_kernel(slot_ref, cols_ref, *refs):
    parts, halo, (first_ref, start_ref, scale_ref) = refs[:4], refs[4:7], refs[7:10]
    wide_ref, work = refs[10], refs[11:]
    slab_total(slot_ref, cols_ref, parts, *halo, *work)
    total_ref = work[1]
    seconds, rests = [], []
    for r in range(SIDE):
        first = first_ref[r]
        second = start_ref[r] - first - scale_ref[r] * total_ref[r]
        seconds.append(second)
        rest = first - first.astype(BF16).astype(F32) + GAIN * (second - second.astype(BF16).astype(F32))
        rests.append(rest.astype(BF16))
    high = jnp.concatenate(seconds, axis=0).astype(BF16)
    for r in range(SIDE):
        for s in range(SIDE):
            wide_ref[SIDE * r + s, 0:SHARE] = high
            wide_ref[SIDE * r + s, SHARE:120] = rests[r]


def last_kernel(cols_ref, *refs):
    parts, halo, (got_ref, first_ref, scale_ref, out_ref, ext_ref, line_ref) = refs[:4], refs[4:7], refs[7:]
    own_ref, low_ref, high_ref = halo
    x, q = place()
    ext_ref[0:4] = own_ref[...]
    ext_ref[4:6] = low_ref[...]
    ext_ref[6:8] = high_ref[...]
    total = jnp.zeros((SHARE, NRHS), F32)
    for k in range(8):
        left = jnp.concatenate([part[k] for part in parts], axis=0)
        total += jnp.dot(left, ext_ref[cols_ref[x, k]], preferred_element_type=F32)
    for k in range(SIDE):
        line_ref[pl.ds(pl.multiple_of(swap(x, k) * SLAB, 8), SLAB), :] = total[SLAB * k:SLAB * (k + 1)]
    mine = pl.ds(pl.multiple_of(q * SHARE, SHARE), SHARE)
    rest = jnp.concatenate([got_ref[SIDE * s + q, SHARE:120].astype(F32) for s in range(SIDE)], axis=0)
    second = own_ref[x, mine].astype(F32) - scale_ref[...] * line_ref[...]
    out_ref[...] = first_ref[x, mine].astype(F32) + rest + GAIN * second


def arr(shape, dtype):
    return pltpu.VMEM(shape, dtype)


def call(kernel, args, outs, scalars=0, scratch=(), far=0):
    vectors = args[scalars:]
    space = pltpu.HBM if far else pltpu.VMEM
    vectors = [pltpu.with_memory_space_constraint(a, space) for a in vectors]
    specs = [SMEM] * scalars + [pl.BlockSpec(memory_space=space)] * len(vectors)
    tables = [pltpu.with_memory_space_constraint(a, pltpu.SMEM) for a in args[:scalars]]
    return pl.pallas_call(kernel, in_specs=specs, out_specs=[VMEM] * len(outs),
                          out_shape=outs, scratch_shapes=list(scratch),
                          compiler_params=pltpu.CompilerParams(vmem_limit_bytes=GRANT))(*tables, *vectors)


def near(*arrays):
    return list(arrays)


HALVES = [arr((2, TILE, NRHS), BF16), arr((2, TILE, NRHS), BF16)]
OWN = arr((SIDE, TILE, NRHS), BF16)
ROWS = arr((SHARE, NRHS), F32)
EXT = arr((8, TILE, NRHS), BF16)
SLABS = arr((SIDE, SLAB, NRHS), F32)
WIDE = arr((GROUP, SHARE, NRHS), BF16)
NEAR = arr((4, TILES * SLAB, NRHS), F32)
WORK = (arr((8, TILES * SLAB, NRHS), F32), SLABS)


def body(matrix_tiles, tile_slot, tile_cols, send_rows, residual, diag_inv):
    leads = lax.axis_size("lead")
    rows = send_rows.transpose(1, 2, 0)
    diag = diag_inv.reshape(1, SHARE)

    def halo(up, down):
        lower = lax.ppermute(up, "lead", [(i, (i + 1) % leads) for i in range(leads)])
        upper = lax.ppermute(down, "lead", [(i, (i - 1) % leads) for i in range(leads)])
        return lower, upper

    def gather(wide):
        return lax.all_to_all(wide, "grp", 0, 0)

    def choose(kernel, got):
        return call(kernel, [rows] + near(got), [OWN] + HALVES, 1)

    def along_x(values):
        pairs = [[(m, m ^ (SIDE * k)) for m in range(GROUP)] for k in range(SIDE)]
        return exchange(values, pairs)

    def along_y(values):
        pairs = [[(m, m ^ k) for m in range(GROUP)] for k in range(SIDE)]
        return exchange(values, pairs)

    def exchange(values, pairs):
        out = [values[0]]
        for k in range(1, SIDE):
            out.append(lax.ppermute(values[k], "grp", pairs[k]))
        return out

    *quarters, wide, start, scale, line = call(
        start_kernel, [matrix_tiles, residual, diag],
        [arr((2, SHARE, TILE), BF16)] * 4 + [WIDE, ROWS, ROWS, arr((8, TILE), F32)],
        scratch=(ROWS, arr((1, SHARE), F32), pltpu.SemaphoreType.DMA((6,))), far=1)
    tables = [pltpu.SMEM((1, TILES), jnp.int32), pltpu.SMEM((SIDE, 8), jnp.int32), pltpu.SMEM((2, 2), jnp.int32)]
    tile_slot, tile_cols, rows = pl.pallas_call(
        table_kernel, name="tables", in_specs=[SMEM] * 3, out_specs=[SMEM] * 3, out_shape=tables)(
        tile_slot, tile_cols, rows)
    quarters = along_y(quarters)
    got = gather(wide)
    slabs = call(split_kernel, near(*quarters, start, line), [arr((PIECE, TILE), BF16)] * 4, 0,
                 (arr((SIDE, PIECE, TILE), BF16),))
    slabs = along_x(slabs)
    own, up, down = choose(pick_home_kernel, got)
    halos = halo(up, down)
    ordered = call(order_kernel, [tile_slot] + near(*slabs), [arr((8, SLAB, TILE), BF16)] * 4, 1,
                   (arr((TILES, SLAB, TILE), BF16),))
    product, = call(near_kernel, near(*slabs, own), [NEAR])
    wide, *state = call(first_kernel, [tile_slot, tile_cols] + near(*slabs, product, *halos),
                        [WIDE] + [SLABS] * 3, 2, WORK)
    first, up, down = choose(pick_slab_kernel, gather(wide))
    halos = halo(up, down)
    parts = along_x(ordered)
    product, = call(near_kernel, near(*slabs, first), [NEAR])
    wide, = call(second_kernel, [tile_slot, tile_cols] + near(*slabs, product, *halos, *state),
                 [arr((GROUP, 120, NRHS), BF16)], 2, WORK)
    got = gather(wide)
    own, up, down = choose(pick_slab_kernel, got)
    halos = halo(up, down)
    result, = call(last_kernel, [tile_cols] + near(*parts, own, *halos, got, first, scale),
                   [jax.ShapeDtypeStruct((SHARE, NRHS), F32)], 1, (EXT, ROWS))
    return result


def solution(mesh):
    in_specs = (
        P(("lead", "grp"), None, None),
        P("lead", None),
        P("lead", None),
        P(),
        P(("lead", "grp"), None),
        P(("lead", "grp")),
    )
    out_specs = P(("lead", "grp"), None)
    return jax.shard_map(body, mesh=mesh, in_specs=in_specs, out_specs=out_specs, check_vma=False)
```

```python
import jax
import jax.numpy as jnp
from jax import lax
from jax.experimental import pallas as pl
from jax.experimental.pallas import tpu as pltpu
from jax.sharding import PartitionSpec as P


TILE = 384
NRHS = 128
SIDE = 4
GROUP = 16
SHARE = 96
SLAB = 24
TILES = 32
PIECE = 216
F32 = jnp.float32
BF16 = jnp.bfloat16
GRANT = 20 << 20
GAIN = 8.0 / 7.0

VMEM = pl.BlockSpec(memory_space=pltpu.VMEM)
SMEM = pl.BlockSpec(memory_space=pltpu.SMEM)


def place():
    member = lax.axis_index("grp")
    return lax.shift_right_logical(member, 2), lax.bitwise_and(member, 3)


def wrap(index):
    return lax.bitwise_and(index, 3)


def column_of(row, first, count):
    line = lax.broadcasted_iota(jnp.int32, (count, 128), 0) + first
    lane = lax.broadcasted_iota(jnp.int32, (count, 128), 1)
    return jnp.sum(jnp.where(line == lane, jnp.broadcast_to(row, (count, 128)), 0.0), axis=1, keepdims=True)


def padded(diag_ref):
    return jnp.concatenate([diag_ref[...], jnp.zeros((1, 128 - SHARE), F32)], axis=1)


def start_kernel(tiles_hbm, residual_hbm, diag_hbm, part0, part1, part2, part3, wide_ref, start_ref, scale_ref,
                 line_ref, residual_ref, diag_ref, high_ref, sems):
    _, q = place()
    copies = [pltpu.make_async_copy(residual_hbm, residual_ref, sems.at[0]),
              pltpu.make_async_copy(diag_hbm, diag_ref, sems.at[1])]
    for k, part in enumerate((part0, part1, part2, part3)):
        at = pl.multiple_of(wrap(q + k) * SHARE, SHARE)
        copies.append(pltpu.make_async_copy(tiles_hbm.at[:, pl.ds(at, SHARE)], part, sems.at[2 + k]))
    for copy in copies:
        copy.start()
    for copy in copies[:2]:
        copy.wait()
    row = padded(diag_ref)
    d_high = row.astype(BF16).astype(F32)
    d_mid = (row - d_high).astype(BF16).astype(F32)
    line_ref[...] = jnp.broadcast_to(jnp.concatenate([d_high, d_mid, row - d_high - d_mid], axis=1), (8, TILE))
    scale = jnp.broadcast_to(column_of(row, 0, SHARE), (SHARE, NRHS))
    scaled = residual_ref[...] * scale
    scale_ref[...] = scale
    start_ref[...] = scaled
    high_ref[...] = scaled.astype(BF16)
    pieces = [pltpu.make_async_copy(high_ref, wide_ref.at[m], sems.at[6 + m]) for m in range(GROUP)]
    for piece in pieces:
        piece.start()
    for copy in copies[2:] + pieces:
        copy.wait()


def spread(value, wide_ref):
    value = value.astype(BF16)
    for m in range(GROUP):
        wide_ref[m] = value


def thirds(rows):
    return jnp.concatenate([rows[8 * k:8 * k + 8] for k in range(3)], axis=1)


def unthirds(rows):
    return jnp.concatenate([rows[:, NRHS * k:NRHS * (k + 1)] for k in range(3)], axis=0)


def split_kernel(*refs):
    parts, (start_ref, line_ref), outs, held_ref = refs[:4], refs[4:6], refs[6:10], refs[10]
    x, q = place()
    high = start_ref[...].astype(BF16).astype(F32)
    low = start_ref[...] - high
    for s in range(SIDE):
        at = slice(SLAB * s, SLAB * (s + 1))
        tail = jnp.concatenate([thirds(high[at]), thirds(low[at]), line_ref[...]], axis=0)
        held_ref[wrap(s - x), 192:PIECE] = tail.astype(BF16)
    for k in range(SIDE):
        tiles = [parts[k][j].astype(F32) for j in range(2)]
        to = pl.multiple_of(48 * wrap(q - k), 48)
        for s in range(SIDE):
            pair = jnp.concatenate([tile[SLAB * s:SLAB * (s + 1)] for tile in tiles], axis=0)
            held_ref[wrap(s - x), pl.ds(to, 48)] = pair.astype(BF16)
    for k in range(SIDE):
        outs[k][...] = held_ref[k]


def table_kernel(slot_ref, cols_ref, rows_ref, slot_out, cols_out, rows_out):
    for t in range(TILES):
        slot_out[0, t] = slot_ref[0, t]
    for r in range(SIDE):
        for k in range(8):
            cols_out[r, k] = cols_ref[r, k]
    lead = lax.axis_index("lead")
    for side in range(2):
        for h in range(2):
            rows_out[side, h] = rows_ref[side, h, lead]


def send_halves(rows_ref, own_ref, up_ref, down_ref):
    for side, ref in ((0, up_ref), (1, down_ref)):
        for h in range(2):
            ref[h] = own_ref[rows_ref[side, h]]


def pick_slab_kernel(rows_ref, got_ref, own_ref, up_ref, down_ref):
    for q in range(SIDE):
        parts = [got_ref[SIDE * x + q, 0:SHARE].astype(F32) for x in range(SIDE)]
        for r in range(SIDE):
            block = jnp.concatenate([p[SLAB * r:SLAB * (r + 1)] for p in parts], axis=0)
            own_ref[r, SHARE * q:SHARE * (q + 1)] = block.astype(BF16)
    send_halves(rows_ref, own_ref, up_ref, down_ref)


def pick_home_kernel(rows_ref, got_ref, own_ref, up_ref, down_ref):
    for r in range(SIDE):
        for q in range(SIDE):
            own_ref[r, SHARE * q:SHARE * (q + 1)] = got_ref[SIDE * r + q]
    send_halves(rows_ref, own_ref, up_ref, down_ref)


def slot_of(slot_ref, x, k, i):
    return slot_ref[0, 8 * wrap(x - k) + i]


def order_kernel(slot_ref, *refs):
    parts, outs, held_ref = refs[:4], refs[4:8], refs[8]
    x, _ = place()
    for k in range(SIDE):
        for y in range(SIDE):
            pair = parts[k][48 * y:48 * (y + 1)].astype(F32)
            for j in range(2):
                to = lax.bitwise_and(slot_of(slot_ref, x, k, 2 * y + j) - 8 * x, TILES - 1)
                held_ref[to] = pair[SLAB * j:SLAB * (j + 1)].astype(BF16)
    for k in range(SIDE):
        outs[k][...] = held_ref[8 * k:8 * k + 8]


def slab_products(slabs, blocks, product_ref, first):
    for pair in range(len(blocks) // 2):
        wide = jnp.concatenate(blocks[2 * pair:2 * pair + 2], axis=1)
        product = jnp.dot(slabs, wide, preferred_element_type=F32)
        product_ref[first + 2 * pair] = product[:, :NRHS]
        product_ref[first + 2 * pair + 1] = product[:, NRHS:]


def all_slabs(parts):
    return jnp.concatenate([part[0:192] for part in parts], axis=0)


def near_kernel(*refs):
    own_ref, product_ref = refs[4:]
    slab_products(all_slabs(refs[:4]), [own_ref[r] for r in range(SIDE)], product_ref, 0)


def slab_total(slot_ref, cols_ref, parts, near_ref, low_ref, high_ref, product_ref, total_ref):
    x, _ = place()
    slab_products(all_slabs(parts), [low_ref[0], low_ref[1], high_ref[0], high_ref[1]], product_ref, 4)
    product_ref[0:4] = near_ref[...]
    total_ref[...] = jnp.zeros_like(total_ref)
    for t in range(TILES):
        slot = slot_of(slot_ref, x, t // 8, t % 8)
        row = lax.shift_right_logical(slot, 3)
        col = cols_ref[row, lax.bitwise_and(slot, 7)]
        total_ref[row] += product_ref[col, SLAB * t:SLAB * (t + 1)]


def first_kernel(slot_ref, cols_ref, *refs):
    parts, halo, (wide_ref, first_ref, start_ref, scale_ref), work = refs[:4], refs[4:7], refs[7:11], refs[11:]
    slab_total(slot_ref, cols_ref, parts, *halo, *work)
    total_ref = work[1]
    x, _ = place()
    for k in range(SIDE):
        tail = parts[k][192:PIECE].astype(F32)
        row = tail[16:17, 0:128] + (tail[16:17, 128:256] + tail[16:17, 256:384])
        start = unthirds(tail[0:8]) + unthirds(tail[8:16])
        scale = jnp.broadcast_to(column_of(row, x * SLAB, SLAB), (SLAB, NRHS))
        r = wrap(x - k)
        start_ref[r] = start
        scale_ref[r] = scale
        first_ref[r] = GAIN * (start - scale * total_ref[r])
    spread(jnp.concatenate([first_ref[r] for r in range(SIDE)], axis=0), wide_ref)


def second_kernel(slot_ref, cols_ref, *refs):
    parts, halo, (first_ref, start_ref, scale_ref) = refs[:4], refs[4:7], refs[7:10]
    wide_ref, work = refs[10], refs[11:]
    slab_total(slot_ref, cols_ref, parts, *halo, *work)
    total_ref = work[1]
    seconds, rests = [], []
    for r in range(SIDE):
        first = first_ref[r]
        second = start_ref[r] - first - scale_ref[r] * total_ref[r]
        seconds.append(second)
        rest = first - first.astype(BF16).astype(F32) + GAIN * (second - second.astype(BF16).astype(F32))
        rests.append(rest.astype(BF16))
    high = jnp.concatenate(seconds, axis=0).astype(BF16)
    for r in range(SIDE):
        for s in range(SIDE):
            wide_ref[SIDE * r + s, 0:SHARE] = high
            wide_ref[SIDE * r + s, SHARE:120] = rests[r]


def last_kernel(cols_ref, *refs):
    parts, halo, (got_ref, first_ref, scale_ref, out_ref, ext_ref, line_ref) = refs[:4], refs[4:7], refs[7:]
    own_ref, low_ref, high_ref = halo
    x, q = place()
    ext_ref[0:4] = own_ref[...]
    ext_ref[4:6] = low_ref[...]
    ext_ref[6:8] = high_ref[...]
    total = jnp.zeros((SHARE, NRHS), F32)
    for k in range(8):
        left = jnp.concatenate([part[k] for part in parts], axis=0)
        total += jnp.dot(left, ext_ref[cols_ref[x, k]], preferred_element_type=F32)
    for k in range(SIDE):
        line_ref[pl.ds(pl.multiple_of(wrap(x - k) * SLAB, 8), SLAB), :] = total[SLAB * k:SLAB * (k + 1)]
    mine = pl.ds(pl.multiple_of(q * SHARE, SHARE), SHARE)
    rest = jnp.concatenate([got_ref[SIDE * s + q, SHARE:120].astype(F32) for s in range(SIDE)], axis=0)
    second = own_ref[x, mine].astype(F32) - scale_ref[...] * line_ref[...]
    out_ref[...] = first_ref[x, mine].astype(F32) + rest + GAIN * second


def arr(shape, dtype):
    return pltpu.VMEM(shape, dtype)


def call(kernel, args, outs, scalars=0, scratch=(), far=0, away=()):
    vectors = args[scalars:]
    space = pltpu.HBM if far else pltpu.VMEM
    vectors = [pltpu.with_memory_space_constraint(a, space) for a in vectors]
    specs = [SMEM] * scalars + [pl.BlockSpec(memory_space=space)] * len(vectors)
    tables = [pltpu.with_memory_space_constraint(a, pltpu.SMEM) for a in args[:scalars]]
    return pl.pallas_call(kernel, in_specs=specs,
                          out_specs=[pl.BlockSpec(memory_space=pltpu.HBM) if n in away else VMEM for n in range(len(outs))],
                          out_shape=outs, scratch_shapes=list(scratch),
                          compiler_params=pltpu.CompilerParams(vmem_limit_bytes=GRANT))(*tables, *vectors)


def near(*arrays):
    return list(arrays)


HALVES = [arr((2, TILE, NRHS), BF16), arr((2, TILE, NRHS), BF16)]
OWN = arr((SIDE, TILE, NRHS), BF16)
ROWS = arr((SHARE, NRHS), F32)
EXT = arr((8, TILE, NRHS), BF16)
SLABS = arr((SIDE, SLAB, NRHS), F32)
WIDE = arr((GROUP, SHARE, NRHS), BF16)
NEAR = arr((4, TILES * SLAB, NRHS), F32)
WORK = (arr((8, TILES * SLAB, NRHS), F32), SLABS)


def body(matrix_tiles, tile_slot, tile_cols, send_rows, residual, diag_inv):
    leads = lax.axis_size("lead")
    rows = send_rows.transpose(1, 2, 0)
    diag = diag_inv.reshape(1, SHARE)

    def halo(up, down):
        lower = lax.ppermute(up, "lead", [(i, (i + 1) % leads) for i in range(leads)])
        upper = lax.ppermute(down, "lead", [(i, (i - 1) % leads) for i in range(leads)])
        return lower, upper

    def gather(wide):
        return lax.all_to_all(wide, "grp", 0, 0)

    def choose(kernel, got):
        return call(kernel, [rows] + near(got), [OWN] + HALVES, 1)

    def along_x(values):
        pairs = [[(m, (m + SIDE * k) % GROUP) for m in range(GROUP)] for k in range(SIDE)]
        return exchange(values, pairs)

    def along_y(values):
        pairs = [[(m, m - m % SIDE + (m + k) % SIDE) for m in range(GROUP)] for k in range(SIDE)]
        return exchange(values, pairs)

    def exchange(values, pairs):
        out = [values[0]]
        for k in range(1, SIDE):
            out.append(lax.ppermute(values[k], "grp", pairs[k]))
        return out

    *quarters, wide, start, scale, line = call(
        start_kernel, [matrix_tiles, residual, diag],
        [arr((2, SHARE, TILE), BF16)] * 4 + [pltpu.HBM((GROUP, SHARE, NRHS), BF16), ROWS, ROWS, arr((8, TILE), F32)],
        scratch=(ROWS, arr((1, SHARE), F32), arr((SHARE, NRHS), BF16), pltpu.SemaphoreType.DMA((6 + GROUP,))), far=1,
        away=(4,))
    tables = [pltpu.SMEM((1, TILES), jnp.int32), pltpu.SMEM((SIDE, 8), jnp.int32), pltpu.SMEM((2, 2), jnp.int32)]
    tile_slot, tile_cols, rows = pl.pallas_call(
        table_kernel, name="tables", in_specs=[SMEM] * 3, out_specs=[SMEM] * 3, out_shape=tables)(
        tile_slot, tile_cols, rows)
    quarters = along_y(quarters)
    got = gather(wide)
    slabs = call(split_kernel, near(*quarters, start, line), [arr((PIECE, TILE), BF16)] * 4, 0,
                 (arr((SIDE, PIECE, TILE), BF16),))
    slabs = along_x(slabs)
    own, up, down = choose(pick_home_kernel, got)
    halos = halo(up, down)
    ordered = call(order_kernel, [tile_slot] + near(*slabs), [arr((8, SLAB, TILE), BF16)] * 4, 1,
                   (arr((TILES, SLAB, TILE), BF16),))
    product, = call(near_kernel, near(*slabs, own), [NEAR])
    wide, *state = call(first_kernel, [tile_slot, tile_cols] + near(*slabs, product, *halos),
                        [WIDE] + [SLABS] * 3, 2, WORK)
    first, up, down = choose(pick_slab_kernel, gather(wide))
    halos = halo(up, down)
    parts = along_x(ordered)
    product, = call(near_kernel, near(*slabs, first), [NEAR])
    wide, = call(second_kernel, [tile_slot, tile_cols] + near(*slabs, product, *halos, *state),
                 [arr((GROUP, 120, NRHS), BF16)], 2, WORK)
    got = gather(wide)
    own, up, down = choose(pick_slab_kernel, got)
    halos = halo(up, down)
    result, = call(last_kernel, [tile_cols] + near(*parts, own, *halos, got, first, scale),
                   [jax.ShapeDtypeStruct((SHARE, NRHS), F32)], 1, (EXT, ROWS))
    return result


def solution(mesh):
    in_specs = (
        P(("lead", "grp"), None, None),
        P("lead", None),
        P("lead", None),
        P(),
        P(("lead", "grp"), None),
        P(("lead", "grp")),
    )
    out_specs = P(("lead", "grp"), None)
    return jax.shard_map(body, mesh=mesh, in_specs=in_specs, out_specs=out_specs, check_vma=False)
```

```python
import jax
import jax.numpy as jnp
from jax import lax
from jax.experimental import pallas as pl
from jax.experimental.pallas import tpu as pltpu
from jax.sharding import PartitionSpec as P


TILE = 384
NRHS = 128
SIDE = 4
GROUP = 16
SHARE = 96
SLAB = 24
TILES = 32
PIECE = 216
F32 = jnp.float32
BF16 = jnp.bfloat16
GRANT = 20 << 20
GAIN = 8.0 / 7.0

VMEM = pl.BlockSpec(memory_space=pltpu.VMEM)
SMEM = pl.BlockSpec(memory_space=pltpu.SMEM)


def place():
    member = lax.axis_index("grp")
    return lax.shift_right_logical(member, 2), lax.bitwise_and(member, 3)


def wrap(index):
    return lax.bitwise_and(index, 3)


def column_of(row, first, count):
    line = lax.broadcasted_iota(jnp.int32, (count, 128), 0) + first
    lane = lax.broadcasted_iota(jnp.int32, (count, 128), 1)
    return jnp.sum(jnp.where(line == lane, jnp.broadcast_to(row, (count, 128)), 0.0), axis=1, keepdims=True)


def padded(diag_ref):
    return jnp.concatenate([diag_ref[...], jnp.zeros((1, 128 - SHARE), F32)], axis=1)


def start_kernel(tiles_hbm, residual_hbm, diag_hbm, part0, part1, part2, part3, wide_ref, start_ref, scale_ref,
                 line_ref, residual_ref, diag_ref, sems):
    _, q = place()
    copies = [pltpu.make_async_copy(residual_hbm, residual_ref, sems.at[0]),
              pltpu.make_async_copy(diag_hbm, diag_ref, sems.at[1])]
    for k, part in enumerate((part0, part1, part2, part3)):
        at = pl.multiple_of(wrap(q + k) * SHARE, SHARE)
        copies.append(pltpu.make_async_copy(tiles_hbm.at[:, pl.ds(at, SHARE)], part, sems.at[2 + k]))
    for copy in copies:
        copy.start()
    for copy in copies[:2]:
        copy.wait()
    row = padded(diag_ref)
    d_high = row.astype(BF16).astype(F32)
    d_mid = (row - d_high).astype(BF16).astype(F32)
    line_ref[...] = jnp.broadcast_to(jnp.concatenate([d_high, d_mid, row - d_high - d_mid], axis=1), (8, TILE))
    scale = jnp.broadcast_to(column_of(row, 0, SHARE), (SHARE, NRHS))
    scaled = residual_ref[...] * scale
    scale_ref[...] = scale
    start_ref[...] = scaled
    spread(scaled, wide_ref)
    for copy in copies[2:]:
        copy.wait()


def spread(value, wide_ref):
    value = value.astype(BF16)
    for m in range(GROUP):
        wide_ref[m] = value


def thirds(rows):
    return jnp.concatenate([rows[8 * k:8 * k + 8] for k in range(3)], axis=1)


def unthirds(rows):
    return jnp.concatenate([rows[:, NRHS * k:NRHS * (k + 1)] for k in range(3)], axis=0)


def split_kernel(*refs):
    parts, (start_ref, line_ref), outs, held_ref = refs[:4], refs[4:6], refs[6:10], refs[10]
    x, q = place()
    high = start_ref[...].astype(BF16).astype(F32)
    low = start_ref[...] - high
    for s in range(SIDE):
        at = slice(SLAB * s, SLAB * (s + 1))
        tail = jnp.concatenate([thirds(high[at]), thirds(low[at]), line_ref[...]], axis=0)
        held_ref[wrap(s - x), 192:PIECE] = tail.astype(BF16)
    for k in range(SIDE):
        tiles = [parts[k][j].astype(F32) for j in range(2)]
        to = pl.multiple_of(48 * wrap(q - k), 48)
        for s in range(SIDE):
            pair = jnp.concatenate([tile[SLAB * s:SLAB * (s + 1)] for tile in tiles], axis=0)
            held_ref[wrap(s - x), pl.ds(to, 48)] = pair.astype(BF16)
    for k in range(SIDE):
        outs[k][...] = held_ref[k]


def table_kernel(slot_ref, cols_ref, rows_ref, slot_out, cols_out, rows_out):
    for t in range(TILES):
        slot_out[0, t] = slot_ref[0, t]
    lead = lax.axis_index("lead")
    odd = lax.bitwise_and(lead, 1)
    for r in range(SIDE):
        for k in range(8):
            col = cols_ref[r, k]
            cols_out[r, k] = jnp.where(col >= 4, lax.bitwise_xor(col, 2 * odd), col)
    for h in range(2):
        rows_out[0, h] = rows_ref[1 - odd, h, lead]
        rows_out[1, h] = rows_ref[odd, h, lead]


def send_halves(rows_ref, own_ref, up_ref, down_ref):
    for side, ref in ((0, up_ref), (1, down_ref)):
        for h in range(2):
            ref[h] = own_ref[rows_ref[side, h]]


def pick_slab_kernel(rows_ref, got_ref, own_ref, up_ref, down_ref):
    for q in range(SIDE):
        parts = [got_ref[SIDE * x + q, 0:SHARE].astype(F32) for x in range(SIDE)]
        for r in range(SIDE):
            block = jnp.concatenate([p[SLAB * r:SLAB * (r + 1)] for p in parts], axis=0)
            own_ref[r, SHARE * q:SHARE * (q + 1)] = block.astype(BF16)
    send_halves(rows_ref, own_ref, up_ref, down_ref)


def pick_home_kernel(rows_ref, got_ref, own_ref, up_ref, down_ref):
    for r in range(SIDE):
        for q in range(SIDE):
            own_ref[r, SHARE * q:SHARE * (q + 1)] = got_ref[SIDE * r + q]
    send_halves(rows_ref, own_ref, up_ref, down_ref)


def slot_of(slot_ref, x, k, i):
    return slot_ref[0, 8 * wrap(x - k) + i]


def order_kernel(slot_ref, *refs):
    parts, outs, held_ref = refs[:4], refs[4:8], refs[8]
    x, _ = place()
    for k in range(SIDE):
        for y in range(SIDE):
            pair = parts[k][48 * y:48 * (y + 1)].astype(F32)
            for j in range(2):
                to = lax.bitwise_and(slot_of(slot_ref, x, k, 2 * y + j) - 8 * x, TILES - 1)
                held_ref[to] = pair[SLAB * j:SLAB * (j + 1)].astype(BF16)
    for k in range(SIDE):
        outs[k][...] = held_ref[8 * k:8 * k + 8]


def slab_products(slabs, blocks, product_ref, first):
    for pair in range(len(blocks) // 2):
        wide = jnp.concatenate(blocks[2 * pair:2 * pair + 2], axis=1)
        product = jnp.dot(slabs, wide, preferred_element_type=F32)
        product_ref[first + 2 * pair] = product[:, :NRHS]
        product_ref[first + 2 * pair + 1] = product[:, NRHS:]


def all_slabs(parts):
    return jnp.concatenate([part[0:192] for part in parts], axis=0)


def near_kernel(*refs):
    own_ref, product_ref = refs[4:]
    slab_products(all_slabs(refs[:4]), [own_ref[r] for r in range(SIDE)], product_ref, 0)


def slab_total(slot_ref, cols_ref, parts, near_ref, low_ref, high_ref, product_ref, total_ref):
    x, _ = place()
    slab_products(all_slabs(parts), [low_ref[0], low_ref[1], high_ref[0], high_ref[1]], product_ref, 4)
    product_ref[0:4] = near_ref[...]
    total_ref[...] = jnp.zeros_like(total_ref)
    for t in range(TILES):
        slot = slot_of(slot_ref, x, t // 8, t % 8)
        row = lax.shift_right_logical(slot, 3)
        col = cols_ref[row, lax.bitwise_and(slot, 7)]
        total_ref[row] += product_ref[col, SLAB * t:SLAB * (t + 1)]


def first_kernel(slot_ref, cols_ref, *refs):
    parts, halo, (wide_ref, first_ref, start_ref, scale_ref), work = refs[:4], refs[4:7], refs[7:11], refs[11:]
    slab_total(slot_ref, cols_ref, parts, *halo, *work)
    total_ref = work[1]
    x, _ = place()
    for k in range(SIDE):
        tail = parts[k][192:PIECE].astype(F32)
        row = tail[16:17, 0:128] + (tail[16:17, 128:256] + tail[16:17, 256:384])
        start = unthirds(tail[0:8]) + unthirds(tail[8:16])
        scale = jnp.broadcast_to(column_of(row, x * SLAB, SLAB), (SLAB, NRHS))
        r = wrap(x - k)
        start_ref[r] = start
        scale_ref[r] = scale
        first_ref[r] = GAIN * (start - scale * total_ref[r])
    spread(jnp.concatenate([first_ref[r] for r in range(SIDE)], axis=0), wide_ref)


def second_kernel(slot_ref, cols_ref, *refs):
    parts, halo, (first_ref, start_ref, scale_ref) = refs[:4], refs[4:7], refs[7:10]
    wide_ref, work = refs[10], refs[11:]
    slab_total(slot_ref, cols_ref, parts, *halo, *work)
    total_ref = work[1]
    seconds, rests = [], []
    for r in range(SIDE):
        first = first_ref[r]
        second = start_ref[r] - first - scale_ref[r] * total_ref[r]
        seconds.append(second)
        rest = first - first.astype(BF16).astype(F32) + GAIN * (second - second.astype(BF16).astype(F32))
        rests.append(rest.astype(BF16))
    high = jnp.concatenate(seconds, axis=0).astype(BF16)
    for r in range(SIDE):
        for s in range(SIDE):
            wide_ref[SIDE * r + s, 0:SHARE] = high
            wide_ref[SIDE * r + s, SHARE:120] = rests[r]


def last_kernel(cols_ref, *refs):
    parts, halo, (got_ref, first_ref, scale_ref, out_ref, ext_ref, line_ref) = refs[:4], refs[4:7], refs[7:]
    own_ref, low_ref, high_ref = halo
    x, q = place()
    ext_ref[0:4] = own_ref[...]
    ext_ref[4:6] = low_ref[...]
    ext_ref[6:8] = high_ref[...]
    total = jnp.zeros((SHARE, NRHS), F32)
    for k in range(8):
        left = jnp.concatenate([part[k] for part in parts], axis=0)
        total += jnp.dot(left, ext_ref[cols_ref[x, k]], preferred_element_type=F32)
    for k in range(SIDE):
        line_ref[pl.ds(pl.multiple_of(wrap(x - k) * SLAB, 8), SLAB), :] = total[SLAB * k:SLAB * (k + 1)]
    mine = pl.ds(pl.multiple_of(q * SHARE, SHARE), SHARE)
    rest = jnp.concatenate([got_ref[SIDE * s + q, SHARE:120].astype(F32) for s in range(SIDE)], axis=0)
    second = own_ref[x, mine].astype(F32) - scale_ref[...] * line_ref[...]
    out_ref[...] = first_ref[x, mine].astype(F32) + rest + GAIN * second


def arr(shape, dtype):
    return pltpu.VMEM(shape, dtype)


def call(kernel, args, outs, scalars=0, scratch=(), far=0):
    vectors = args[scalars:]
    space = pltpu.HBM if far else pltpu.VMEM
    vectors = [pltpu.with_memory_space_constraint(a, space) for a in vectors]
    specs = [SMEM] * scalars + [pl.BlockSpec(memory_space=space)] * len(vectors)
    tables = [pltpu.with_memory_space_constraint(a, pltpu.SMEM) for a in args[:scalars]]
    return pl.pallas_call(kernel, in_specs=specs, out_specs=[VMEM] * len(outs),
                          out_shape=outs, scratch_shapes=list(scratch),
                          compiler_params=pltpu.CompilerParams(vmem_limit_bytes=GRANT))(*tables, *vectors)


def near(*arrays):
    return list(arrays)


HALVES = [arr((2, TILE, NRHS), BF16), arr((2, TILE, NRHS), BF16)]
OWN = arr((SIDE, TILE, NRHS), BF16)
ROWS = arr((SHARE, NRHS), F32)
EXT = arr((8, TILE, NRHS), BF16)
SLABS = arr((SIDE, SLAB, NRHS), F32)
WIDE = arr((GROUP, SHARE, NRHS), BF16)
NEAR = arr((4, TILES * SLAB, NRHS), F32)
WORK = (arr((8, TILES * SLAB, NRHS), F32), SLABS)


def body(matrix_tiles, tile_slot, tile_cols, send_rows, residual, diag_inv):
    leads = lax.axis_size("lead")
    rows = send_rows.transpose(1, 2, 0)
    diag = diag_inv.reshape(1, SHARE)

    def halo(up, down):
        lower = lax.ppermute(up, "lead", [(i, (i + 2 * (i % 2) - 1) % leads) for i in range(leads)])
        upper = lax.ppermute(down, "lead", [(i, i ^ 1) for i in range(leads)])
        return lower, upper

    def gather(wide):
        return lax.all_to_all(wide, "grp", 0, 0)

    def choose(kernel, got):
        return call(kernel, [rows] + near(got), [OWN] + HALVES, 1)

    def along_x(values):
        pairs = [[(m, (m + SIDE * k) % GROUP) for m in range(GROUP)] for k in range(SIDE)]
        return exchange(values, pairs)

    def along_y(values):
        pairs = [[(m, m - m % SIDE + (m + k) % SIDE) for m in range(GROUP)] for k in range(SIDE)]
        return exchange(values, pairs)

    def exchange(values, pairs):
        out = [values[0]]
        for k in range(1, SIDE):
            out.append(lax.ppermute(values[k], "grp", pairs[k]))
        return out

    *quarters, wide, start, scale, line = call(
        start_kernel, [matrix_tiles, residual, diag],
        [arr((2, SHARE, TILE), BF16)] * 4 + [WIDE, ROWS, ROWS, arr((8, TILE), F32)],
        scratch=(ROWS, arr((1, SHARE), F32), pltpu.SemaphoreType.DMA((6,))), far=1)
    tables = [pltpu.SMEM((1, TILES), jnp.int32), pltpu.SMEM((SIDE, 8), jnp.int32), pltpu.SMEM((2, 2), jnp.int32)]
    tile_slot, tile_cols, rows = pl.pallas_call(
        table_kernel, name="tables", in_specs=[SMEM] * 3, out_specs=[SMEM] * 3, out_shape=tables)(
        tile_slot, tile_cols, rows)
    quarters = along_y(quarters)
    got = gather(wide)
    slabs = call(split_kernel, near(*quarters, start, line), [arr((PIECE, TILE), BF16)] * 4, 0,
                 (arr((SIDE, PIECE, TILE), BF16),))
    slabs = along_x(slabs)
    own, up, down = choose(pick_home_kernel, got)
    halos = halo(up, down)
    ordered = call(order_kernel, [tile_slot] + near(*slabs), [arr((8, SLAB, TILE), BF16)] * 4, 1,
                   (arr((TILES, SLAB, TILE), BF16),))
    product, = call(near_kernel, near(*slabs, own), [NEAR])
    wide, *state = call(first_kernel, [tile_slot, tile_cols] + near(*slabs, product, *halos),
                        [WIDE] + [SLABS] * 3, 2, WORK)
    first, up, down = choose(pick_slab_kernel, gather(wide))
    halos = halo(up, down)
    parts = along_x(ordered)
    product, = call(near_kernel, near(*slabs, first), [NEAR])
    wide, = call(second_kernel, [tile_slot, tile_cols] + near(*slabs, product, *halos, *state),
                 [arr((GROUP, 120, NRHS), BF16)], 2, WORK)
    got = gather(wide)
    own, up, down = choose(pick_slab_kernel, got)
    halos = halo(up, down)
    result, = call(last_kernel, [tile_cols] + near(*parts, own, *halos, got, first, scale),
                   [jax.ShapeDtypeStruct((SHARE, NRHS), F32)], 1, (EXT, ROWS))
    return result


def solution(mesh):
    in_specs = (
        P(("lead", "grp"), None, None),
        P("lead", None),
        P("lead", None),
        P(),
        P(("lead", "grp"), None),
        P(("lead", "grp")),
    )
    out_specs = P(("lead", "grp"), None)
    return jax.shard_map(body, mesh=mesh, in_specs=in_specs, out_specs=out_specs, check_vma=False)
```

```python
import jax
import jax.numpy as jnp
from jax import lax
from jax.experimental import pallas as pl
from jax.experimental.pallas import tpu as pltpu
from jax.sharding import PartitionSpec as P


TILE = 384
NRHS = 128
SIDE = 4
GROUP = 16
SHARE = 96
SLAB = 24
TILES = 32
PIECE = 216
F32 = jnp.float32
BF16 = jnp.bfloat16
GRANT = 20 << 20
GAIN = 8.0 / 7.0

VMEM = pl.BlockSpec(memory_space=pltpu.VMEM)
SMEM = pl.BlockSpec(memory_space=pltpu.SMEM)


def place():
    member = lax.axis_index("grp")
    return lax.shift_right_logical(member, 2), lax.bitwise_and(member, 3)


def wrap(index):
    return lax.bitwise_and(index, 3)


def column_of(row, first, count):
    line = lax.broadcasted_iota(jnp.int32, (count, 128), 0) + first
    lane = lax.broadcasted_iota(jnp.int32, (count, 128), 1)
    return jnp.sum(jnp.where(line == lane, jnp.broadcast_to(row, (count, 128)), 0.0), axis=1, keepdims=True)


def padded(diag_ref):
    return jnp.concatenate([diag_ref[...], jnp.zeros((1, 128 - SHARE), F32)], axis=1)


def start_kernel(tiles_hbm, residual_hbm, diag_hbm, part0, part1, part2, part3, wide_ref, start_ref, scale_ref,
                 line_ref, residual_ref, diag_ref, high_ref, sems):
    _, q = place()
    copies = [pltpu.make_async_copy(residual_hbm, residual_ref, sems.at[0]),
              pltpu.make_async_copy(diag_hbm, diag_ref, sems.at[1])]
    for k, part in enumerate((part0, part1, part2, part3)):
        at = pl.multiple_of(wrap(q + k) * SHARE, SHARE)
        copies.append(pltpu.make_async_copy(tiles_hbm.at[:, pl.ds(at, SHARE)], part, sems.at[2 + k]))
    for copy in copies:
        copy.start()
    for copy in copies[:2]:
        copy.wait()
    row = padded(diag_ref)
    d_high = row.astype(BF16).astype(F32)
    d_mid = (row - d_high).astype(BF16).astype(F32)
    line_ref[...] = jnp.broadcast_to(jnp.concatenate([d_high, d_mid, row - d_high - d_mid], axis=1), (8, TILE))
    scale = jnp.broadcast_to(column_of(row, 0, SHARE), (SHARE, NRHS))
    scaled = residual_ref[...] * scale
    scale_ref[...] = scale
    start_ref[...] = scaled
    high_ref[...] = scaled.astype(BF16)
    pieces = [pltpu.make_async_copy(high_ref, wide_ref.at[m], sems.at[6 + m]) for m in range(GROUP)]
    for piece in pieces:
        piece.start()
    for copy in copies[2:] + pieces:
        copy.wait()


def spread(value, wide_ref):
    value = value.astype(BF16)
    for m in range(GROUP):
        wide_ref[m] = value


def thirds(rows):
    return jnp.concatenate([rows[8 * k:8 * k + 8] for k in range(3)], axis=1)


def unthirds(rows):
    return jnp.concatenate([rows[:, NRHS * k:NRHS * (k + 1)] for k in range(3)], axis=0)


def split_kernel(*refs):
    parts, (start_ref, line_ref), outs, held_ref = refs[:4], refs[4:6], refs[6:10], refs[10]
    x, q = place()
    high = start_ref[...].astype(BF16).astype(F32)
    low = start_ref[...] - high
    for s in range(SIDE):
        at = slice(SLAB * s, SLAB * (s + 1))
        tail = jnp.concatenate([thirds(high[at]), thirds(low[at]), line_ref[...]], axis=0)
        held_ref[wrap(s - x), 192:PIECE] = tail.astype(BF16)
    for k in range(SIDE):
        tiles = [parts[k][j].astype(F32) for j in range(2)]
        to = pl.multiple_of(48 * wrap(q - k), 48)
        for s in range(SIDE):
            pair = jnp.concatenate([tile[SLAB * s:SLAB * (s + 1)] for tile in tiles], axis=0)
            held_ref[wrap(s - x), pl.ds(to, 48)] = pair.astype(BF16)
    for k in range(SIDE):
        outs[k][...] = held_ref[k]


def table_kernel(slot_ref, cols_ref, rows_ref, slot_out, cols_out, rows_out):
    for t in range(TILES):
        slot_out[0, t] = slot_ref[0, t]
    lead = lax.axis_index("lead")
    odd = lax.bitwise_and(lead, 1)
    for r in range(SIDE):
        for k in range(8):
            col = cols_ref[r, k]
            cols_out[r, k] = jnp.where(col >= 4, lax.bitwise_xor(col, 2 * odd), col)
    for h in range(2):
        rows_out[0, h] = rows_ref[1 - odd, h, lead]
        rows_out[1, h] = rows_ref[odd, h, lead]


def send_halves(rows_ref, own_ref, up_ref, down_ref):
    for side, ref in ((0, up_ref), (1, down_ref)):
        for h in range(2):
            ref[h] = own_ref[rows_ref[side, h]]


def pick_slab_kernel(rows_ref, got_ref, own_ref, up_ref, down_ref):
    for q in range(SIDE):
        parts = [got_ref[SIDE * x + q, 0:SHARE].astype(F32) for x in range(SIDE)]
        for r in range(SIDE):
            block = jnp.concatenate([p[SLAB * r:SLAB * (r + 1)] for p in parts], axis=0)
            own_ref[r, SHARE * q:SHARE * (q + 1)] = block.astype(BF16)
    send_halves(rows_ref, own_ref, up_ref, down_ref)


def pick_home_kernel(rows_ref, got_ref, own_ref, up_ref, down_ref):
    for r in range(SIDE):
        for q in range(SIDE):
            own_ref[r, SHARE * q:SHARE * (q + 1)] = got_ref[SIDE * r + q]
    send_halves(rows_ref, own_ref, up_ref, down_ref)


def slot_of(slot_ref, x, k, i):
    return slot_ref[0, 8 * wrap(x - k) + i]


def order_kernel(slot_ref, *refs):
    parts, outs, held_ref = refs[:4], refs[4:8], refs[8]
    x, _ = place()
    for k in range(SIDE):
        for y in range(SIDE):
            pair = parts[k][48 * y:48 * (y + 1)].astype(F32)
            for j in range(2):
                to = lax.bitwise_and(slot_of(slot_ref, x, k, 2 * y + j) - 8 * x, TILES - 1)
                held_ref[to] = pair[SLAB * j:SLAB * (j + 1)].astype(BF16)
    for k in range(SIDE):
        outs[k][...] = held_ref[8 * k:8 * k + 8]


def slab_products(slabs, blocks, product_ref, first):
    for pair in range(len(blocks) // 2):
        wide = jnp.concatenate(blocks[2 * pair:2 * pair + 2], axis=1)
        product = jnp.dot(slabs, wide, preferred_element_type=F32)
        product_ref[first + 2 * pair] = product[:, :NRHS]
        product_ref[first + 2 * pair + 1] = product[:, NRHS:]


def all_slabs(parts):
    return jnp.concatenate([part[0:192] for part in parts], axis=0)


def near_kernel(*refs):
    own_ref, product_ref = refs[4:]
    slab_products(all_slabs(refs[:4]), [own_ref[r] for r in range(SIDE)], product_ref, 0)


def slab_total(slot_ref, cols_ref, parts, near_ref, low_ref, high_ref, product_ref, total_ref):
    x, _ = place()
    slab_products(all_slabs(parts), [low_ref[0], low_ref[1], high_ref[0], high_ref[1]], product_ref, 4)
    product_ref[0:4] = near_ref[...]
    total_ref[...] = jnp.zeros_like(total_ref)
    for t in range(TILES):
        slot = slot_of(slot_ref, x, t // 8, t % 8)
        row = lax.shift_right_logical(slot, 3)
        col = cols_ref[row, lax.bitwise_and(slot, 7)]
        total_ref[row] += product_ref[col, SLAB * t:SLAB * (t + 1)]


def first_kernel(slot_ref, cols_ref, *refs):
    parts, halo, (wide_ref, first_ref, start_ref, scale_ref), work = refs[:4], refs[4:7], refs[7:11], refs[11:]
    slab_total(slot_ref, cols_ref, parts, *halo, *work)
    total_ref = work[1]
    x, _ = place()
    for k in range(SIDE):
        tail = parts[k][192:PIECE].astype(F32)
        row = tail[16:17, 0:128] + (tail[16:17, 128:256] + tail[16:17, 256:384])
        start = unthirds(tail[0:8]) + unthirds(tail[8:16])
        scale = jnp.broadcast_to(column_of(row, x * SLAB, SLAB), (SLAB, NRHS))
        r = wrap(x - k)
        start_ref[r] = start
        scale_ref[r] = scale
        first_ref[r] = GAIN * (start - scale * total_ref[r])
    spread(jnp.concatenate([first_ref[r] for r in range(SIDE)], axis=0), wide_ref)


def second_kernel(slot_ref, cols_ref, *refs):
    parts, halo, (first_ref, start_ref, scale_ref) = refs[:4], refs[4:7], refs[7:10]
    wide_ref, work = refs[10], refs[11:]
    slab_total(slot_ref, cols_ref, parts, *halo, *work)
    total_ref = work[1]
    seconds, rests = [], []
    for r in range(SIDE):
        first = first_ref[r]
        second = start_ref[r] - first - scale_ref[r] * total_ref[r]
        seconds.append(second)
        rest = first - first.astype(BF16).astype(F32) + GAIN * (second - second.astype(BF16).astype(F32))
        rests.append(rest.astype(BF16))
    high = jnp.concatenate(seconds, axis=0).astype(BF16)
    for r in range(SIDE):
        for s in range(SIDE):
            wide_ref[SIDE * r + s, 0:SHARE] = high
            wide_ref[SIDE * r + s, SHARE:120] = rests[r]


def last_kernel(cols_ref, *refs):
    parts, halo, (got_ref, first_ref, scale_ref, out_ref, ext_ref, line_ref) = refs[:4], refs[4:7], refs[7:]
    own_ref, low_ref, high_ref = halo
    x, q = place()
    ext_ref[0:4] = own_ref[...]
    ext_ref[4:6] = low_ref[...]
    ext_ref[6:8] = high_ref[...]
    total = jnp.zeros((SHARE, NRHS), F32)
    for k in range(8):
        left = jnp.concatenate([part[k] for part in parts], axis=0)
        total += jnp.dot(left, ext_ref[cols_ref[x, k]], preferred_element_type=F32)
    for k in range(SIDE):
        line_ref[pl.ds(pl.multiple_of(wrap(x - k) * SLAB, 8), SLAB), :] = total[SLAB * k:SLAB * (k + 1)]
    mine = pl.ds(pl.multiple_of(q * SHARE, SHARE), SHARE)
    rest = jnp.concatenate([got_ref[SIDE * s + q, SHARE:120].astype(F32) for s in range(SIDE)], axis=0)
    second = own_ref[x, mine].astype(F32) - scale_ref[...] * line_ref[...]
    out_ref[...] = first_ref[x, mine].astype(F32) + rest + GAIN * second


def arr(shape, dtype):
    return pltpu.VMEM(shape, dtype)


def call(kernel, args, outs, scalars=0, scratch=(), far=0, away=()):
    vectors = args[scalars:]
    space = pltpu.HBM if far else pltpu.VMEM
    vectors = [pltpu.with_memory_space_constraint(a, space) for a in vectors]
    specs = [SMEM] * scalars + [pl.BlockSpec(memory_space=space)] * len(vectors)
    tables = [pltpu.with_memory_space_constraint(a, pltpu.SMEM) for a in args[:scalars]]
    return pl.pallas_call(kernel, in_specs=specs,
                          out_specs=[pl.BlockSpec(memory_space=pltpu.HBM) if n in away else VMEM for n in range(len(outs))],
                          out_shape=outs, scratch_shapes=list(scratch),
                          compiler_params=pltpu.CompilerParams(vmem_limit_bytes=GRANT))(*tables, *vectors)


def near(*arrays):
    return list(arrays)


HALVES = [arr((2, TILE, NRHS), BF16), arr((2, TILE, NRHS), BF16)]
OWN = arr((SIDE, TILE, NRHS), BF16)
ROWS = arr((SHARE, NRHS), F32)
EXT = arr((8, TILE, NRHS), BF16)
SLABS = arr((SIDE, SLAB, NRHS), F32)
WIDE = arr((GROUP, SHARE, NRHS), BF16)
NEAR = arr((4, TILES * SLAB, NRHS), F32)
WORK = (arr((8, TILES * SLAB, NRHS), F32), SLABS)


def body(matrix_tiles, tile_slot, tile_cols, send_rows, residual, diag_inv):
    leads = lax.axis_size("lead")
    rows = send_rows.transpose(1, 2, 0)
    diag = diag_inv.reshape(1, SHARE)

    def halo(up, down):
        lower = lax.ppermute(up, "lead", [(i, (i + 2 * (i % 2) - 1) % leads) for i in range(leads)])
        upper = lax.ppermute(down, "lead", [(i, i ^ 1) for i in range(leads)])
        return lower, upper

    def gather(wide):
        return lax.all_to_all(wide, "grp", 0, 0)

    def choose(kernel, got):
        return call(kernel, [rows] + near(got), [OWN] + HALVES, 1)

    def along_x(values):
        pairs = [[(m, (m + SIDE * k) % GROUP) for m in range(GROUP)] for k in range(SIDE)]
        return exchange(values, pairs)

    def along_y(values):
        pairs = [[(m, m - m % SIDE + (m + k) % SIDE) for m in range(GROUP)] for k in range(SIDE)]
        return exchange(values, pairs)

    def exchange(values, pairs):
        out = [values[0]]
        for k in range(1, SIDE):
            out.append(lax.ppermute(values[k], "grp", pairs[k]))
        return out

    *quarters, wide, start, scale, line = call(
        start_kernel, [matrix_tiles, residual, diag],
        [arr((2, SHARE, TILE), BF16)] * 4 + [pltpu.HBM((GROUP, SHARE, NRHS), BF16), ROWS, ROWS, arr((8, TILE), F32)],
        scratch=(ROWS, arr((1, SHARE), F32), arr((SHARE, NRHS), BF16), pltpu.SemaphoreType.DMA((6 + GROUP,))), far=1,
        away=(4,))
    tables = [pltpu.SMEM((1, TILES), jnp.int32), pltpu.SMEM((SIDE, 8), jnp.int32), pltpu.SMEM((2, 2), jnp.int32)]
    tile_slot, tile_cols, rows = pl.pallas_call(
        table_kernel, name="tables", in_specs=[SMEM] * 3, out_specs=[SMEM] * 3, out_shape=tables)(
        tile_slot, tile_cols, rows)
    quarters = along_y(quarters)
    got = gather(wide)
    slabs = call(split_kernel, near(*quarters, start, line), [arr((PIECE, TILE), BF16)] * 4, 0,
                 (arr((SIDE, PIECE, TILE), BF16),))
    slabs = along_x(slabs)
    own, up, down = choose(pick_home_kernel, got)
    halos = halo(up, down)
    ordered = call(order_kernel, [tile_slot] + near(*slabs), [arr((8, SLAB, TILE), BF16)] * 4, 1,
                   (arr((TILES, SLAB, TILE), BF16),))
    product, = call(near_kernel, near(*slabs, own), [NEAR])
    wide, *state = call(first_kernel, [tile_slot, tile_cols] + near(*slabs, product, *halos),
                        [WIDE] + [SLABS] * 3, 2, WORK)
    first, up, down = choose(pick_slab_kernel, gather(wide))
    halos = halo(up, down)
    parts = along_x(ordered)
    product, = call(near_kernel, near(*slabs, first), [NEAR])
    wide, = call(second_kernel, [tile_slot, tile_cols] + near(*slabs, product, *halos, *state),
                 [arr((GROUP, 120, NRHS), BF16)], 2, WORK)
    got = gather(wide)
    own, up, down = choose(pick_slab_kernel, got)
    halos = halo(up, down)
    result, = call(last_kernel, [tile_cols] + near(*parts, own, *halos, got, first, scale),
                   [jax.ShapeDtypeStruct((SHARE, NRHS), F32)], 1, (EXT, ROWS))
    return result


def solution(mesh):
    in_specs = (
        P(("lead", "grp"), None, None),
        P("lead", None),
        P("lead", None),
        P(),
        P(("lead", "grp"), None),
        P(("lead", "grp")),
    )
    out_specs = P(("lead", "grp"), None)
    return jax.shard_map(body, mesh=mesh, in_specs=in_specs, out_specs=out_specs, check_vma=False)
```

```python
import jax
import jax.numpy as jnp
from jax import lax
from jax.experimental import pallas as pl
from jax.experimental.pallas import tpu as pltpu
from jax.sharding import PartitionSpec as P


TILE = 384
NRHS = 128
SIDE = 4
GROUP = 16
SHARE = 96
SLAB = 24
TILES = 32
PIECE = 216
F32 = jnp.float32
BF16 = jnp.bfloat16
GRANT = 20 << 20
GAIN = 8.0 / 7.0

VMEM = pl.BlockSpec(memory_space=pltpu.VMEM)
SMEM = pl.BlockSpec(memory_space=pltpu.SMEM)


def place():
    member = lax.axis_index("grp")
    return lax.shift_right_logical(member, 2), lax.bitwise_and(member, 3)


def wrap(index):
    return lax.bitwise_and(index, 3)


def column_of(row, first, count):
    line = lax.broadcasted_iota(jnp.int32, (count, 128), 0) + first
    lane = lax.broadcasted_iota(jnp.int32, (count, 128), 1)
    return jnp.sum(jnp.where(line == lane, jnp.broadcast_to(row, (count, 128)), 0.0), axis=1, keepdims=True)


def padded(diag_ref):
    return jnp.concatenate([diag_ref[...], jnp.zeros((1, 128 - SHARE), F32)], axis=1)


def start_kernel(tiles_hbm, residual_hbm, diag_hbm, part0, part1, part2, part3, wide_ref, start_ref, scale_ref,
                 line_ref, residual_ref, diag_ref, high_ref, sems):
    _, q = place()
    copies = [pltpu.make_async_copy(residual_hbm, residual_ref, sems.at[0]),
              pltpu.make_async_copy(diag_hbm, diag_ref, sems.at[1])]
    for k, part in enumerate((part0, part1, part2, part3)):
        at = pl.multiple_of(wrap(q + k) * SHARE, SHARE)
        copies.append(pltpu.make_async_copy(tiles_hbm.at[:, pl.ds(at, SHARE)], part, sems.at[2 + k]))
    for copy in copies:
        copy.start()
    for copy in copies[:2]:
        copy.wait()
    row = padded(diag_ref)
    d_high = row.astype(BF16).astype(F32)
    d_mid = (row - d_high).astype(BF16).astype(F32)
    line_ref[...] = jnp.broadcast_to(jnp.concatenate([d_high, d_mid, row - d_high - d_mid], axis=1), (8, TILE))
    scale = jnp.broadcast_to(column_of(row, 0, SHARE), (SHARE, NRHS))
    scaled = residual_ref[...] * scale
    scale_ref[...] = scale
    start_ref[...] = scaled
    high_ref[...] = scaled.astype(BF16)
    pieces = [pltpu.make_async_copy(high_ref, wide_ref.at[m], sems.at[6 + m]) for m in range(GROUP)]
    for piece in pieces:
        piece.start()
    for copy in copies[2:] + pieces:
        copy.wait()


def spread(value, wide_ref):
    value = value.astype(BF16)
    for m in range(GROUP):
        wide_ref[m] = value


def thirds(rows):
    return jnp.concatenate([rows[8 * k:8 * k + 8] for k in range(3)], axis=1)


def unthirds(rows):
    return jnp.concatenate([rows[:, NRHS * k:NRHS * (k + 1)] for k in range(3)], axis=0)


def split_kernel(*refs):
    parts, (start_ref, line_ref), outs, held_ref = refs[:4], refs[4:6], refs[6:10], refs[10]
    x, q = place()
    high = start_ref[...].astype(BF16).astype(F32)
    low = start_ref[...] - high
    for s in range(SIDE):
        at = slice(SLAB * s, SLAB * (s + 1))
        tail = jnp.concatenate([thirds(high[at]), thirds(low[at]), line_ref[...]], axis=0)
        held_ref[wrap(s - x), 192:PIECE] = tail.astype(BF16)
    for k in range(SIDE):
        tiles = [parts[k][j].astype(F32) for j in range(2)]
        to = pl.multiple_of(48 * wrap(q - k), 48)
        for s in range(SIDE):
            pair = jnp.concatenate([tile[SLAB * s:SLAB * (s + 1)] for tile in tiles], axis=0)
            held_ref[wrap(s - x), pl.ds(to, 48)] = pair.astype(BF16)
    for k in range(SIDE):
        outs[k][...] = held_ref[k]


def table_kernel(slot_ref, cols_ref, rows_ref, slot_out, cols_out, rows_out):
    for t in range(TILES):
        slot_out[0, t] = slot_ref[0, t]
    lead = lax.axis_index("lead")
    odd = lax.bitwise_and(lead, 1)
    for r in range(SIDE):
        for k in range(8):
            col = cols_ref[r, k]
            cols_out[r, k] = jnp.where(col >= 4, lax.bitwise_xor(col, 2 * odd), col)
    for h in range(2):
        rows_out[0, h] = rows_ref[1 - odd, h, lead]
        rows_out[1, h] = rows_ref[odd, h, lead]


def send_halves(rows_ref, own_ref, up_ref, down_ref):
    for side, ref in ((0, up_ref), (1, down_ref)):
        for h in range(2):
            ref[h] = own_ref[rows_ref[side, h]]


def pick_slab_kernel(rows_ref, got_ref, own_ref, up_ref, down_ref):
    for q in range(SIDE):
        parts = [got_ref[SIDE * x + q, 0:SHARE].astype(F32) for x in range(SIDE)]
        for r in range(SIDE):
            block = jnp.concatenate([p[SLAB * r:SLAB * (r + 1)] for p in parts], axis=0)
            own_ref[r, SHARE * q:SHARE * (q + 1)] = block.astype(BF16)
    send_halves(rows_ref, own_ref, up_ref, down_ref)


def pick_home_kernel(rows_ref, got_ref, own_ref, up_ref, down_ref):
    for r in range(SIDE):
        for q in range(SIDE):
            own_ref[r, SHARE * q:SHARE * (q + 1)] = got_ref[SIDE * r + q]
    send_halves(rows_ref, own_ref, up_ref, down_ref)


def slot_of(slot_ref, x, k, i):
    return slot_ref[0, 8 * wrap(x - k) + i]


def order_kernel(slot_ref, *refs):
    parts, outs, held_ref = refs[:4], refs[4:8], refs[8]
    x, _ = place()
    for k in range(SIDE):
        for y in range(SIDE):
            pair = parts[k][48 * y:48 * (y + 1)].astype(F32)
            for j in range(2):
                to = lax.bitwise_and(slot_of(slot_ref, x, k, 2 * y + j) - 8 * x, TILES - 1)
                held_ref[to] = pair[SLAB * j:SLAB * (j + 1)].astype(BF16)
    for k in range(SIDE):
        outs[k][...] = held_ref[8 * k:8 * k + 8]


def slab_products(slabs, blocks, product_ref, first):
    for pair in range(len(blocks) // 2):
        wide = jnp.concatenate(blocks[2 * pair:2 * pair + 2], axis=1)
        product = jnp.dot(slabs, wide, preferred_element_type=F32)
        product_ref[first + 2 * pair] = product[:, :NRHS]
        product_ref[first + 2 * pair + 1] = product[:, NRHS:]


def all_slabs(parts):
    return jnp.concatenate([part[0:192] for part in parts], axis=0)


def add_up(slot_ref, cols_ref, base, blocks, parts, product_ref, total_ref):
    x, _ = place()
    product_ref[0] = jnp.zeros((TILES * SLAB, NRHS), F32)
    slab_products(all_slabs(parts), blocks, product_ref, 1)
    for t in range(TILES):
        slot = slot_of(slot_ref, x, t // 8, t % 8)
        row = lax.shift_right_logical(slot, 3)
        block = cols_ref[row, lax.bitwise_and(slot, 7)] - base + 1
        block = jnp.where(block > len(blocks), 0, jnp.maximum(block, 0))
        total_ref[row] += product_ref[block, SLAB * t:SLAB * (t + 1)]


def near_kernel(slot_ref, cols_ref, *refs):
    own_ref, total_ref, product_ref = refs[4:]
    total_ref[...] = jnp.zeros_like(total_ref)
    add_up(slot_ref, cols_ref, 0, [own_ref[r] for r in range(SIDE)], refs[:4], product_ref, total_ref)


def half_kernel(slot_ref, cols_ref, *refs):
    near_ref, high_ref, total_ref, product_ref = refs[4:]
    total_ref[...] = near_ref[...]
    add_up(slot_ref, cols_ref, 6, [high_ref[0], high_ref[1]], refs[:4], product_ref, total_ref)


def slab_total(slot_ref, cols_ref, parts, near_ref, low_ref, product_ref, total_ref):
    total_ref[...] = near_ref[...]
    add_up(slot_ref, cols_ref, 4, [low_ref[0], low_ref[1]], parts, product_ref, total_ref)


def first_kernel(slot_ref, cols_ref, *refs):
    parts, halo, (wide_ref, first_ref, start_ref, scale_ref), work = refs[:4], refs[4:6], refs[6:10], refs[10:]
    slab_total(slot_ref, cols_ref, parts, *halo, *work)
    total_ref = work[1]
    x, _ = place()
    for k in range(SIDE):
        tail = parts[k][192:PIECE].astype(F32)
        row = tail[16:17, 0:128] + (tail[16:17, 128:256] + tail[16:17, 256:384])
        start = unthirds(tail[0:8]) + unthirds(tail[8:16])
        scale = jnp.broadcast_to(column_of(row, x * SLAB, SLAB), (SLAB, NRHS))
        r = wrap(x - k)
        start_ref[r] = start
        scale_ref[r] = scale
        first_ref[r] = GAIN * (start - scale * total_ref[r])
    spread(jnp.concatenate([first_ref[r] for r in range(SIDE)], axis=0), wide_ref)


def second_kernel(slot_ref, cols_ref, *refs):
    parts, halo, (first_ref, start_ref, scale_ref) = refs[:4], refs[4:6], refs[6:9]
    wide_ref, work = refs[9], refs[10:]
    slab_total(slot_ref, cols_ref, parts, *halo, *work)
    total_ref = work[1]
    seconds, rests = [], []
    for r in range(SIDE):
        first = first_ref[r]
        second = start_ref[r] - first - scale_ref[r] * total_ref[r]
        seconds.append(second)
        rest = first - first.astype(BF16).astype(F32) + GAIN * (second - second.astype(BF16).astype(F32))
        rests.append(rest.astype(BF16))
    high = jnp.concatenate(seconds, axis=0).astype(BF16)
    for r in range(SIDE):
        for s in range(SIDE):
            wide_ref[SIDE * r + s, 0:SHARE] = high
            wide_ref[SIDE * r + s, SHARE:120] = rests[r]


def last_kernel(cols_ref, *refs):
    parts, halo, (got_ref, first_ref, scale_ref, out_ref, ext_ref, line_ref) = refs[:4], refs[4:7], refs[7:]
    own_ref, low_ref, high_ref = halo
    x, q = place()
    ext_ref[0:4] = own_ref[...]
    ext_ref[4:6] = low_ref[...]
    ext_ref[6:8] = high_ref[...]
    total = jnp.zeros((SHARE, NRHS), F32)
    for k in range(8):
        left = jnp.concatenate([part[k] for part in parts], axis=0)
        total += jnp.dot(left, ext_ref[cols_ref[x, k]], preferred_element_type=F32)
    for k in range(SIDE):
        line_ref[pl.ds(pl.multiple_of(wrap(x - k) * SLAB, 8), SLAB), :] = total[SLAB * k:SLAB * (k + 1)]
    mine = pl.ds(pl.multiple_of(q * SHARE, SHARE), SHARE)
    rest = jnp.concatenate([got_ref[SIDE * s + q, SHARE:120].astype(F32) for s in range(SIDE)], axis=0)
    second = own_ref[x, mine].astype(F32) - scale_ref[...] * line_ref[...]
    out_ref[...] = first_ref[x, mine].astype(F32) + rest + GAIN * second


def arr(shape, dtype):
    return pltpu.VMEM(shape, dtype)


def call(kernel, args, outs, scalars=0, scratch=(), far=0, away=()):
    vectors = args[scalars:]
    space = pltpu.HBM if far else pltpu.VMEM
    vectors = [pltpu.with_memory_space_constraint(a, space) for a in vectors]
    specs = [SMEM] * scalars + [pl.BlockSpec(memory_space=space)] * len(vectors)
    tables = [pltpu.with_memory_space_constraint(a, pltpu.SMEM) for a in args[:scalars]]
    return pl.pallas_call(kernel, in_specs=specs,
                          out_specs=[pl.BlockSpec(memory_space=pltpu.HBM) if n in away else VMEM for n in range(len(outs))],
                          out_shape=outs, scratch_shapes=list(scratch),
                          compiler_params=pltpu.CompilerParams(vmem_limit_bytes=GRANT))(*tables, *vectors)


def near(*arrays):
    return list(arrays)


HALVES = [arr((2, TILE, NRHS), BF16), arr((2, TILE, NRHS), BF16)]
OWN = arr((SIDE, TILE, NRHS), BF16)
ROWS = arr((SHARE, NRHS), F32)
EXT = arr((8, TILE, NRHS), BF16)
SLABS = arr((SIDE, SLAB, NRHS), F32)
WIDE = arr((GROUP, SHARE, NRHS), BF16)
WORK = (arr((5, TILES * SLAB, NRHS), F32), SLABS)


def body(matrix_tiles, tile_slot, tile_cols, send_rows, residual, diag_inv):
    leads = lax.axis_size("lead")
    rows = send_rows.transpose(1, 2, 0)
    diag = diag_inv.reshape(1, SHARE)

    def halo(up, down):
        lower = lax.ppermute(up, "lead", [(i, (i + 2 * (i % 2) - 1) % leads) for i in range(leads)])
        upper = lax.ppermute(down, "lead", [(i, i ^ 1) for i in range(leads)])
        return lower, upper

    def gather(wide):
        return lax.all_to_all(wide, "grp", 0, 0)

    def choose(kernel, got):
        return call(kernel, [rows] + near(got), [OWN] + HALVES, 1)

    def along_x(values):
        pairs = [[(m, (m + SIDE * k) % GROUP) for m in range(GROUP)] for k in range(SIDE)]
        return exchange(values, pairs)

    def along_y(values):
        pairs = [[(m, m - m % SIDE + (m + k) % SIDE) for m in range(GROUP)] for k in range(SIDE)]
        return exchange(values, pairs)

    def exchange(values, pairs):
        out = [values[0]]
        for k in range(1, SIDE):
            out.append(lax.ppermute(values[k], "grp", pairs[k]))
        return out

    *quarters, wide, start, scale, line = call(
        start_kernel, [matrix_tiles, residual, diag],
        [arr((2, SHARE, TILE), BF16)] * 4 + [pltpu.HBM((GROUP, SHARE, NRHS), BF16), ROWS, ROWS, arr((8, TILE), F32)],
        scratch=(ROWS, arr((1, SHARE), F32), arr((SHARE, NRHS), BF16), pltpu.SemaphoreType.DMA((6 + GROUP,))), far=1,
        away=(4,))
    tables = [pltpu.SMEM((1, TILES), jnp.int32), pltpu.SMEM((SIDE, 8), jnp.int32), pltpu.SMEM((2, 2), jnp.int32)]
    tile_slot, tile_cols, rows = pl.pallas_call(
        table_kernel, name="tables", in_specs=[SMEM] * 3, out_specs=[SMEM] * 3, out_shape=tables)(
        tile_slot, tile_cols, rows)
    quarters = along_y(quarters)
    got = gather(wide)
    slabs = call(split_kernel, near(*quarters, start, line), [arr((PIECE, TILE), BF16)] * 4, 0,
                 (arr((SIDE, PIECE, TILE), BF16),))
    slabs = along_x(slabs)
    own, up, down = choose(pick_home_kernel, got)
    halos = halo(up, down)
    ordered = call(order_kernel, [tile_slot] + near(*slabs), [arr((8, SLAB, TILE), BF16)] * 4, 1,
                   (arr((TILES, SLAB, TILE), BF16),))
    total, = call(near_kernel, [tile_slot, tile_cols] + near(*slabs, own), [SLABS], 2, WORK[:1])
    total, = call(half_kernel, [tile_slot, tile_cols] + near(*slabs, total, halos[1]), [SLABS], 2, WORK[:1])
    wide, *state = call(first_kernel, [tile_slot, tile_cols] + near(*slabs, total, halos[0]),
                        [WIDE] + [SLABS] * 3, 2, WORK)
    first, up, down = choose(pick_slab_kernel, gather(wide))
    halos = halo(up, down)
    parts = along_x(ordered)
    total, = call(near_kernel, [tile_slot, tile_cols] + near(*slabs, first), [SLABS], 2, WORK[:1])
    total, = call(half_kernel, [tile_slot, tile_cols] + near(*slabs, total, halos[1]), [SLABS], 2, WORK[:1])
    wide, = call(second_kernel, [tile_slot, tile_cols] + near(*slabs, total, halos[0], *state),
                 [arr((GROUP, 120, NRHS), BF16)], 2, WORK)
    got = gather(wide)
    own, up, down = choose(pick_slab_kernel, got)
    halos = halo(up, down)
    result, = call(last_kernel, [tile_cols] + near(*parts, own, *halos, got, first, scale),
                   [jax.ShapeDtypeStruct((SHARE, NRHS), F32)], 1, (EXT, ROWS))
    return result


def solution(mesh):
    in_specs = (
        P(("lead", "grp"), None, None),
        P("lead", None),
        P("lead", None),
        P(),
        P(("lead", "grp"), None),
        P(("lead", "grp")),
    )
    out_specs = P(("lead", "grp"), None)
    return jax.shard_map(body, mesh=mesh, in_specs=in_specs, out_specs=out_specs, check_vma=False)
```
